32 devices in a mesh: gx: 4 (over z), gy: 8 (over y, x, core).
Axes of the slice: x: 2, y: 2, z: 4, core: 2. Of those that a mesh axis runs over, the one named last changes fastest.
Arguments:
- conductivity: bfloat16 [2, 1024, 4096], P(None, 'gy', 'gx'), may hold values from 0.099609375 to 1.59375
Outputs:
- coarse_stencil: float32 [9, 8, 64, 2048], P(None, 'gy', 'gx')
The draws below stay inside these ranges and needn't reach their ends.
All inputs are finite; a program needn't handle non-finite values.
Results may differ from the reference program's by a relative error of at most 0.0003.
Values may be sent and summed in bfloat16 or wider, within the bound.
A program may use at most 64 MiB of HBM per device.

```python
import math
import jax
import jax.numpy as jnp
from jax import lax

CY = 128
PLANES = 2
NX = 4096
NY = 1024


def block_levels(own_key, dims, shards, low, largest):
    def one(axis_at, parts):
        heights = jax.random.uniform(jax.random.fold_in(jax.random.fold_in(own_key, 6), axis_at), (parts,), jnp.float32, low / len(shards), largest / len(shards))
        return jnp.repeat(jnp.exp(heights), dims[axis_at] // parts).reshape((-1,) + (1,) * (len(dims) - axis_at - 1))

    gain = one(*shards[0])
    for cut in shards[1:]:
        gain = gain * one(*cut)
    return gain


def setup_inputs(seed: int = 0) -> dict:
    arg_keys = jax.random.split(jax.random.key(seed), 2)
    return {
        "conductivity": jnp.clip(jnp.exp(math.log(1.59375) - 2.7725887 * jax.random.uniform(arg_keys[0], (PLANES, NY, NX), jnp.float32) ** block_levels(arg_keys[0], (PLANES, NY, NX), ((1, 8), (2, 4)), -0.2, 0.2)), 0.099609375, 1.59375).astype(jnp.bfloat16),
    }


def harmonic(first, second):
    return 2.0 * first * second / (first + second)


def prepare_window(extended, row_start, col_start, rows_all, cols_all):
    conduct = extended.astype(jnp.float32)
    ext_rows = conduct.shape[1]
    ext_cols = conduct.shape[2]
    row_ids = row_start - 2 + jnp.arange(ext_rows, dtype=jnp.int32)
    col_ids = col_start - 2 + jnp.arange(ext_cols, dtype=jnp.int32)
    row_inside = (row_ids >= 0) & (row_ids < rows_all)
    col_inside = (col_ids >= 0) & (col_ids < cols_all)
    inside = row_inside[:, None] & col_inside[None, :]
    safe_values = jnp.where(inside[None], conduct, 1.0)
    east_face = jnp.where(jnp.roll(inside, -1, 1)[None], harmonic(safe_values, jnp.roll(safe_values, -1, 2)), safe_values)
    west_face = jnp.where(jnp.roll(inside, 1, 1)[None], harmonic(safe_values, jnp.roll(safe_values, 1, 2)), safe_values)
    north_face = jnp.where(jnp.roll(inside, -1, 0)[None], harmonic(safe_values, jnp.roll(safe_values, -1, 1)), safe_values)
    south_face = jnp.where(jnp.roll(inside, 1, 0)[None], harmonic(safe_values, jnp.roll(safe_values, 1, 1)), safe_values)
    vertical = harmonic(safe_values[0], safe_values[1])
    centre = east_face + west_face + north_face + south_face + vertical[None] + safe_values
    col_east = east_face[0] + east_face[1]
    col_west = west_face[0] + west_face[1]
    row_north = north_face[0] + north_face[1]
    row_south = south_face[0] + south_face[1]
    left_weight = col_west / (col_west + col_east)
    right_weight = col_east / (col_west + col_east)
    south_weight = row_south / (row_south + row_north)
    north_weight = row_north / (row_south + row_north)
    odd_rows = (row_ids % 2 == 1)[:, None]
    odd_cols = (col_ids % 2 == 1)[None, :]
    even_point = inside & (row_ids % 2 == 0)[:, None] & (col_ids % 2 == 0)[None, :]
    row_class = ((row_ids // 2) % 3)[:, None]
    col_class = ((col_ids // 2) % 3)[None, :]
    return (inside, odd_rows, odd_cols, even_point, row_class, col_class, east_face, west_face, north_face, south_face, vertical, centre, left_weight, right_weight, south_weight, north_weight)


def probe_sum(prepared, colour):
    (inside, odd_rows, odd_cols, even_point, row_class, col_class, east_face, west_face, north_face, south_face, vertical, centre, left_weight, right_weight, south_weight, north_weight) = prepared
    chosen = even_point & (row_class == colour // 3) & (col_class == colour % 3)
    probe_field = chosen.astype(jnp.float32)
    along_x = jnp.where(odd_cols, left_weight * jnp.roll(probe_field, 1, 1) + right_weight * jnp.roll(probe_field, -1, 1), probe_field)
    fine_field = jnp.where(odd_rows, south_weight * jnp.roll(along_x, 1, 0) + north_weight * jnp.roll(along_x, -1, 0), along_x)
    fine_field = jnp.where(inside, fine_field, 0.0)
    applied = (centre * fine_field - east_face * jnp.roll(fine_field, -1, 1) - west_face * jnp.roll(fine_field, 1, 1)
               - north_face * jnp.roll(fine_field, -1, 0) - south_face * jnp.roll(fine_field, 1, 0) - vertical * fine_field)
    folded = jnp.where(inside, applied[0] + applied[1], 0.0)
    rows_done = folded + jnp.roll(south_weight * folded, -1, 0) + jnp.roll(north_weight * folded, 1, 0)
    cols_done = rows_done + jnp.roll(left_weight * rows_done, -1, 1) + jnp.roll(right_weight * rows_done, 1, 1)
    return cols_done[2:-2:2, 2:-2:2]


def by_offset(colours, row_first, col_first):
    count_rows = colours.shape[1]
    count_cols = colours.shape[2]
    coarse_rows = row_first + jnp.arange(count_rows, dtype=jnp.int32)
    coarse_cols = col_first + jnp.arange(count_cols, dtype=jnp.int32)
    fields = []
    for step_row in (-1, 0, 1):
        for step_col in (-1, 0, 1):
            row_group = (coarse_rows + step_row) % 3
            col_group = (coarse_cols + step_col) % 3
            selected = jnp.zeros((count_rows, count_cols), jnp.float32)
            for colour in range(9):
                chosen = (row_group == colour // 3)[:, None] & (col_group == colour % 3)[None, :]
                selected = jnp.where(chosen, colours[colour], selected)
            fields.append(selected)
    return jnp.stack(fields)


def reference(conductivity):
    rows_all = conductivity.shape[1]
    cols_all = conductivity.shape[2]
    padded = jnp.pad(conductivity, ((0, 0), (2, 2), (2, 2)))
    prepared = prepare_window(padded, 0, 0, rows_all, cols_all)

    def one_colour(colour):
        return probe_sum(prepared, colour)

    colours = lax.map(one_colour, jnp.arange(9, dtype=jnp.int32))
    stencil = by_offset(colours, 0, 0)
    band_rows = CY // 2
    return stencil.reshape(9, stencil.shape[1] // band_rows, band_rows, stencil.shape[2])
```

```python
import functools

import jax
import jax.numpy as jnp
from jax import lax
from jax.experimental import pallas as pl
from jax.experimental.pallas import tpu as pltpu
from jax.sharding import PartitionSpec as P

MESH = pl.DeviceIdType.MESH
LANES = 128
UNROLL = 4
STEPS = 4
VMEM_LIMIT = 16 * 1024 * 1024


def arrivals(n, i):
    half = n // 2
    own_half = range(half) if i < half else range(half, n)
    if i < half:
        return [k for k in own_half if k != i] + list(range(n - 1, half - 1, -1))
    return [k for k in own_half if k < i] + list(range(half)) + [k for k in own_half if k > i]


def chosen(i, values):
    picked = values[-1]
    for at in range(len(values) - 2, -1, -1):
        picked = jnp.where(i == at, values[at], picked)
    return picked


def coarse_kernel(
    n, m, cells, fields, main, mid, tails, heads, south_in, north_in, pack,
    main_send, main_recv, mid_send, mid_recv, edge_send, edge_recv, known, own,
):
    i = lax.axis_index("gx")
    j = lax.axis_index("gy")
    band = main.shape[2]
    has_left, has_right = i > 0, i < n - 1
    has_south, has_north = j > 0, j < m - 1

    barrier = pltpu.get_barrier_semaphore()

    def greet(there, x, y):
        @pl.when(there)
        def _():
            pl.semaphore_signal(barrier, inc=1, device_id=(x, y), device_id_type=MESH)

    greet(has_left, i - 1, j)
    greet(has_right, i + 1, j)
    greet(has_south, i, j - 1)
    greet(has_north, i, j + 1)

    def rows_of(t):
        return cells.at[:, pl.ds(pl.multiple_of(t * band, band), band), :]

    loads = []
    for t in range(n):
        loads.append(pltpu.make_async_copy(cells.at[:, pl.ds(t * band + band - 8, 8), :], tails.at[t], own.at[2 * t]))
        loads.append(pltpu.make_async_copy(cells.at[:, pl.ds(t * band, 8), :], heads.at[t], own.at[2 * t + 1]))
    for load in loads:
        load.start()
    own_main = pltpu.make_async_copy(rows_of(i), main.at[i], own.at[2 * n])
    own_main.start()

    @pl.when(jnp.logical_not(has_south))
    def _():
        south_in[...] = jnp.ones(south_in.shape, south_in.dtype)

    @pl.when(jnp.logical_not(has_north))
    def _():
        north_in[...] = jnp.ones(north_in.shape, north_in.dtype)

    def one(there):
        return jnp.where(there, 1, 0)

    pl.semaphore_wait(barrier, one(has_left) + one(has_right) + one(has_south) + one(has_north))

    def tell(d):
        @pl.when(has_left & (i + d - 1 < n))
        def _():
            pl.semaphore_signal(known.at[0, d], inc=1, device_id=(i - 1, j), device_id_type=MESH)

        @pl.when(has_right & (i - d + 1 >= 0))
        def _():
            pl.semaphore_signal(known.at[1, d], inc=1, device_id=(i + 1, j), device_id_type=MESH)

    def hear(d):
        @pl.when(i + d < n)
        def _():
            pl.semaphore_wait(known.at[0, d], 1)

        @pl.when(i - d >= 0)
        def _():
            pl.semaphore_wait(known.at[1, d], 1)

    def remote(src, dst, send, recv, x, y):
        return pltpu.make_async_remote_copy(
            src_ref=src, dst_ref=dst, send_sem=send, recv_sem=recv, device_id=(x, y), device_id_type=MESH
        )

    def main_copy(t):
        return remote(rows_of(t), main.at[i], main_send.at[t], main_recv.at[i], t, j)

    def mid_copy(t):
        return remote(pack.at[t], mid.at[i], mid_send.at[t], mid_recv.at[i], t, j)

    def to_north():
        return remote(cells.at[:, pl.ds(n * band - 8, 8), :], south_in, edge_send.at[0], edge_recv.at[0], i, jnp.minimum(j + 1, m - 1))

    def to_south():
        return remote(cells.at[:, pl.ds(0, 8), :], north_in, edge_send.at[1], edge_recv.at[1], i, jnp.maximum(j - 1, 0))

    sub = lax.broadcasted_iota(jnp.int32, (8, cells.shape[2]), 0)

    def make_pack(t, under, over):
        low = [pltpu.roll(under[p].astype(jnp.float32), 2 + 2 * p, 0) for p in range(2)]
        high = [pltpu.roll(over[p].astype(jnp.float32), 4 + p, 0) for p in range(2)]
        rows = jnp.where(sub < 2, low[0], jnp.where(sub < 4, low[1], jnp.where(sub == 4, high[0], high[1])))
        pack[t] = rows.astype(jnp.bfloat16)

    def edges():
        @pl.when(has_south)
        def _():
            to_north().wait_recv()

        @pl.when(has_north)
        def _():
            to_south().wait_recv()

        make_pack(0, south_in, heads.at[1])
        make_pack(n - 1, tails.at[n - 2], north_in)

    tell(2)

    @pl.when(has_north)
    def _():
        to_north().start()

    @pl.when(has_south)
    def _():
        to_south().start()

    edge_phase = min(2, n - 1)
    for d in range(1, n):
        if d > 1:
            hear(d)
            if d < n - 1:
                tell(d + 1)

        @pl.when(i + d < n)
        def _():
            main_copy(i + d).start()

        @pl.when(i == d)
        def _():
            main_copy(0).start()

        if d == 1:
            for load in loads:
                load.wait()
            for t in range(1, n - 1):
                make_pack(t, tails.at[t - 1], heads.at[t + 1])

        @pl.when(i + d < n - 1)
        def _():
            mid_copy(i + d).start()

        if d == edge_phase:
            edges()

            @pl.when((i >= n - 1 - d) & has_right)
            def _():
                mid_copy(n - 1).start()

            @pl.when((i <= d) & has_left)
            def _():
                mid_copy(0).start()

        if d > edge_phase:
            @pl.when(i + d == n - 1)
            def _():
                mid_copy(n - 1).start()

        @pl.when(i == d)
        def _():
            if d > edge_phase:
                mid_copy(0).start()
            for t in range(1, d):
                main_copy(t).start()
                mid_copy(t).start()

    own_mid = pltpu.make_async_copy(pack.at[i], mid.at[i], own.at[2 * n + 1])
    own_mid.start()

    first = arrival_stage(n, m, main, mid, fields)
    own_main.wait()
    own_mid.wait()
    first(i)
    orders = [arrivals(n, at) for at in range(n)]
    for step in range(n - 1):
        k = chosen(i, [order[step] for order in orders])
        remote(pack.at[0], mid.at[k], mid_send.at[k], mid_recv.at[k], k, j).wait_recv()
        remote(rows_of(0), main.at[k], main_send.at[k], main_recv.at[k], k, j).wait_recv()
        first(k)

    for t in range(n):
        @pl.when(i != t)
        def _():
            main_copy(t).wait_send()
            mid_copy(t).wait_send()

    @pl.when(has_north)
    def _():
        to_north().wait_send()

    @pl.when(has_south)
    def _():
        to_south().wait_send()


def parts(x0, y0, x1, y1):
    s0, s1 = x0 + y0, x1 + y1
    return x0 * y0 * s1 + x1 * y1 * s0, s0 * s1


def two_faces(one, two):
    scale = 2.0 / (one[1] * two[1])
    return one[0] * two[1] * scale, two[0] * one[1] * scale


def middle(one, two):
    x, y = one[0] * two[1], two[0] * one[1]
    total = 1.0 / (x + y)
    return x * total, y * total, 2.0 * (one[0] * two[0]) * total


def verticals(pairs):
    sums = [x + y for x, y in pairs]
    low, high = sums[0] * sums[1], sums[2] * sums[3]
    scale = 4.0 / (low * high)
    low, high = high * scale, low * scale
    shares = (sums[1] * low, sums[0] * low, sums[3] * high, sums[2] * high)
    return [x * y * share for (x, y), share in zip(pairs, shares)]


def arrival_stage(n, m, main, mid, fields):
    band = main.shape[2]
    block = main.shape[3]
    half = band // 2
    rows = fields.shape[2]
    tiles = fields.shape[0] - 1
    per_block = block // (2 * LANES)
    i = lax.axis_index("gx")
    j = lax.axis_index("gy")
    last_rows = (i == n - 1) & (j == m - 1)

    taken = 2 * band + 8
    want = lax.broadcasted_iota(jnp.int32, (4 * rows, taken), 0)
    have = lax.broadcasted_iota(jnp.int32, (4 * rows, taken), 1)
    group = jnp.where(want >= 3 * rows, 3, jnp.where(want >= 2 * rows, 2, jnp.where(want >= rows, 1, 0)))
    place = want - group * rows
    plane = jnp.where(group >= 2, 1, 0)
    odd = group - 2 * plane
    inside = plane * band + 2 * jnp.where(place < half, place, 0) + odd
    above = jnp.where(odd == 0, 2 * band + 4 + plane, plane * band + 1)
    below = 2 * band + 2 * plane + odd
    source = jnp.where(place == half, above, jnp.where(place == rows - 1, below, inside))
    pick_rows = jnp.where(have == source, 1.0, 0.0).astype(jnp.bfloat16)
    fine = lax.broadcasted_iota(jnp.int32, (2 * LANES, 2 * LANES), 0)
    to = lax.broadcasted_iota(jnp.int32, (2 * LANES, 2 * LANES), 1)
    pick_cols = jnp.where(fine == jnp.where(to < LANES, 2 * to, 2 * (to - LANES) + 1), 1.0, 0.0).astype(jnp.bfloat16)

    top = (lax.broadcasted_iota(jnp.int32, (rows, LANES), 0) == half - 1) & last_rows

    def up(x):
        return pltpu.roll(x, rows - 1, 0)

    def tile_terms(k, part):
        t = k * per_block + part
        cols = pl.ds(pl.multiple_of(part * 2 * LANES, 2 * LANES), 2 * LANES)
        stored = jnp.concatenate(
            [
                main[k, 0, :, cols].astype(jnp.float32),
                main[k, 1, :, cols].astype(jnp.float32),
                mid[k, :, cols].astype(jnp.float32),
            ],
            axis=0,
        ).astype(jnp.bfloat16)
        picked = jnp.dot(pick_rows, stored, preferred_element_type=jnp.float32).astype(jnp.bfloat16)
        split = jnp.dot(picked, pick_cols, preferred_element_type=jnp.float32)
        a0, c0, a1, c1 = (split[g * rows : (g + 1) * rows, :LANES] for g in range(4))
        b0, d0, b1, d1 = (split[g * rows : (g + 1) * rows, LANES:] for g in range(4))
        def wall(x0, x1, inner):
            return jnp.where(top, 0.5 * (x0 + x1), inner[0]), jnp.where(top, 1.0, inner[1])

        s0, n0, t0 = middle(parts(a0, c0, a1, c1), wall(c0, c1, parts(c0, up(a0), c1, up(a1))))
        s1, n1, t1 = middle(parts(b0, d0, b1, d1), wall(d0, d1, parts(d0, up(b0), d1, up(b1))))
        h1, g1 = two_faces(parts(a0, b0, a1, b1), parts(c0, d0, c1, d1))
        pairs = ((a0, a1), (b0, b1), (c0, c1), (d0, d1))
        side_a, side_b, side_c, side_d = (
            (x + ((k0 + k1) + v)) - v for x, (k0, k1), v in zip((h1, h1, g1, g1), pairs, verticals(pairs))
        )
        for at, value in enumerate(
            (a0, a1, c0, c1, s0, n0, b0, b1, d0, d1, t0, s1, n1, t1, h1, g1, side_a, side_b, side_c, side_d)
        ):
            fields[t, at] = value

    def first(k):
        lax.fori_loop(0, per_block, lambda part, carry: (tile_terms(k, part), carry)[1], 0, unroll=UNROLL)

    ones = jnp.ones((rows, LANES), jnp.float32)
    for at in range(6):
        fields[tiles, at] = ones

    return first


def stencil_kernel(n, m, half, chunk, fields, out, held, sent):
    rows = fields.shape[2]
    tiles = fields.shape[0] - 1
    i = lax.axis_index("gx")
    j = lax.axis_index("gy")
    lane = lax.broadcasted_iota(jnp.int32, (rows, LANES), 1)
    sub = lax.broadcasted_iota(jnp.int32, (rows, LANES), 0)
    bottom = (sub == 0) & (i == 0) & (j == 0)
    top = (sub == half - 1) & (i == n - 1) & (j == m - 1)

    def up(x):
        return pltpu.roll(x, rows - 1, 0)

    def down(x):
        return pltpu.roll(x, 1, 0)

    def step(t, carry):
        last = (lane == LANES - 1) & (t == tiles - 1)
        first_lane = (lane == 0) & (t == 0)

        def ahead(at):
            return pltpu.roll(jnp.where(lane == 0, fields[t + 1, at], fields[t, at]), LANES - 1, 1)

        rolled = []

        def behind(x):
            turned = pltpu.roll(x, 1, 1)
            before = carry[len(rolled)]
            rolled.append(turned)
            return jnp.where(lane == 0, before, turned)

        a0, a1, c0, c1, s0, n0, b0, b1, d0, d1 = (fields[t, at] for at in range(10))
        t0, s1, n1, t1, h1, g1, side_a, side_b, side_c, side_d = (fields[t, at] for at in range(10, 20))
        wall_a, wall_b = a0 + a1, b0 + b1
        h2, g2 = two_faces(parts(b0, ahead(0), b1, ahead(1)), parts(d0, ahead(2), d1, ahead(3)))
        h2 = jnp.where(last, wall_b, h2)
        g2 = jnp.where(last, d0 + d1, g2)
        total = 1.0 / (h1 + h2)
        left, right = h1 * total, h2 * total
        left_up = up(left)
        right_up = up(right)
        s0_next = ahead(4)
        n0_next = ahead(5)
        side_a = side_a + jnp.where(first_lane, wall_a, behind(h2))
        side_c = side_c + jnp.where(first_lane, c0 + c1, behind(g2))
        side_b = side_b + h2
        side_d = side_d + g2

        nc = n0 * side_c
        sc = s0 * side_c
        nd = n1 * side_d
        sd = s1 * side_d
        even = side_a + t0 + s0 * sc + jnp.where(bottom, wall_a, down(t0 + n0 * nc))
        odd_ = side_b + t1 + s1 * sd + jnp.where(bottom, wall_b, down(t1 + n1 * nd))
        even_up = s0 * nc - t0
        odd_up = s1 * nd - t1
        sg = s0 * g1
        ng = n0 * g1
        sq = s0_next * g2
        nq = n0_next * g2
        p = h1 + s1 * sg + jnp.where(bottom, 0.0, down(n1 * ng))
        q = h2 + s1 * sq + jnp.where(bottom, 0.0, down(n1 * nq))
        p_up = n1 * sg
        p_down = s1 * ng
        q_up = s1 * nq
        q_down = n1 * sq

        mid = left * odd_ - p
        east = jnp.where(last, 0.0, right * mid - left * q)
        centre = even + left * (mid - p) + behind(right * (right * odd_ - 2.0 * q))
        lo = left * odd_up - p_up
        ro = right * odd_up - q_down
        north = even_up + left_up * lo - left * p_down + behind(right_up * ro - right * q_up)
        north = jnp.where(top, 0.0, north)
        north_east = jnp.where(last | top, 0.0, right_up * lo - left * q_up)
        north_west = jnp.where(last | top, 0.0, left_up * ro - right * p_down)
        west = behind(east)
        ne_back = behind(north_east)
        nw_back = behind(north_west)
        cols = pl.ds(pl.multiple_of(t * LANES, LANES), LANES)

        def below(x):
            return jnp.where(bottom, 0.0, down(x))

        for at, value in enumerate(
            (below(ne_back), below(north), below(north_west), west, centre, east, nw_back, north, north_east)
        ):
            held[at, :, cols] = value[:half]
        return tuple(rolled)

    def leave(c):
        cols = pl.ds(c * chunk * LANES, chunk * LANES)
        return pltpu.make_async_copy(held.at[:, :, cols], out.at[:, :, cols], sent.at[c])

    carry = (jnp.zeros((rows, LANES), jnp.float32),) * 7
    for c in range(tiles // chunk):
        carry = lax.fori_loop(c * chunk, (c + 1) * chunk, step, carry, unroll=STEPS)
        leave(c).start()
    for c in range(tiles // chunk):
        leave(c).wait()


def shards(n, m, conductivity):
    planes, local_rows, local_cols = conductivity.shape
    band = local_rows // n
    half = band // 2
    rows = -(-(half + 2) // 8) * 8
    tiles = n * local_cols // (2 * LANES)
    vmem = pl.BlockSpec(memory_space=pltpu.VMEM)
    anywhere = pl.BlockSpec(memory_space=pl.ANY)
    dma = pltpu.SemaphoreType.DMA
    shape = (tiles + 1, 20, rows, LANES)
    fields = pl.pallas_call(
        functools.partial(coarse_kernel, n, m),
        out_shape=jax.ShapeDtypeStruct(shape, jnp.float32),
        in_specs=[anywhere],
        out_specs=vmem,
        scratch_shapes=[
            pltpu.VMEM((n, planes, band, local_cols), jnp.bfloat16),
            pltpu.VMEM((n, 8, local_cols), jnp.bfloat16),
            pltpu.VMEM((n, planes, 8, local_cols), jnp.bfloat16),
            pltpu.VMEM((n, planes, 8, local_cols), jnp.bfloat16),
            pltpu.VMEM((planes, 8, local_cols), jnp.bfloat16),
            pltpu.VMEM((planes, 8, local_cols), jnp.bfloat16),
            pltpu.VMEM((n, 8, local_cols), jnp.bfloat16),
            dma((n,)),
            dma((n,)),
            dma((n,)),
            dma((n,)),
            dma((2,)),
            dma((2,)),
            pltpu.SemaphoreType.REGULAR((2, n)),
            dma((2 * n + 2,)),
        ],
        compiler_params=pltpu.CompilerParams(
            collective_id=0, has_side_effects=True, vmem_limit_bytes=VMEM_LIMIT
        ),
        name="coarse",
    )(pltpu.with_memory_space_constraint(conductivity, pltpu.HBM))
    chunk = tiles // 4
    stencil = pl.pallas_call(
        functools.partial(stencil_kernel, n, m, half, chunk),
        out_shape=jax.ShapeDtypeStruct((9, half, tiles * LANES), jnp.float32),
        in_specs=[vmem],
        out_specs=anywhere,
        scratch_shapes=[pltpu.VMEM((9, half, tiles * LANES), jnp.float32), dma((4,))],
        compiler_params=pltpu.CompilerParams(vmem_limit_bytes=VMEM_LIMIT),
        name="stencil",
    )(fields)
    return stencil[:, None]


def solution(mesh):
    n, m = mesh.shape["gx"], mesh.shape["gy"]
    return jax.shard_map(
        functools.partial(shards, n, m),
        mesh=mesh,
        in_specs=(P(None, "gy", "gx"),),
        out_specs=P(None, "gy", "gx", None),
        check_vma=False,
    )
```

```python
import functools

import jax
import jax.numpy as jnp
from jax import lax
from jax.experimental import pallas as pl
from jax.experimental.pallas import tpu as pltpu
from jax.sharding import PartitionSpec as P

MESH = pl.DeviceIdType.MESH
LANES = 128
UNROLL = 4
STEPS = 4
VMEM_LIMIT = 16 * 1024 * 1024


def arrivals(n, i):
    half = n // 2
    own_half = range(half) if i < half else range(half, n)
    if i < half:
        return [k for k in own_half if k != i] + list(range(n - 1, half - 1, -1))
    return [k for k in own_half if k < i] + list(range(half)) + [k for k in own_half if k > i]


def chosen(i, values):
    picked = values[-1]
    for at in range(len(values) - 2, -1, -1):
        picked = jnp.where(i == at, values[at], picked)
    return picked


def coarse_kernel(
    n, m, cells, fields, main, mid, tails, heads, south_in, north_in, pack,
    main_send, main_recv, mid_send, mid_recv, edge_send, edge_recv, known, own,
):
    i = lax.axis_index("gx")
    j = lax.axis_index("gy")
    band = main.shape[2]
    has_left, has_right = i > 0, i < n - 1
    has_south, has_north = j > 0, j < m - 1
    before, after = jnp.maximum(j - 1, 0), jnp.minimum(j + 1, m - 1)

    def signal(sem, x, y):
        pl.semaphore_signal(sem, inc=1, device_id=(x, y), device_id_type=MESH)

    barrier = pltpu.get_barrier_semaphore()
    for t in range(1, n):
        @pl.when(i < t)
        def _():
            signal(barrier, t, j)

    @pl.when(has_north)
    def _():
        signal(barrier, i, after)

    first_of_all = (i == 0) & (j == 0)

    @pl.when((i == 0) & (j == 1))
    def _():
        signal(barrier, 0, 0)

    def rows_of(t):
        return cells.at[:, pl.ds(pl.multiple_of(t * band, band), band), :]

    loads = []
    for t in range(n):
        loads.append(pltpu.make_async_copy(cells.at[:, pl.ds(t * band + band - 8, 8), :], tails.at[t], own.at[2 * t]))
        loads.append(pltpu.make_async_copy(cells.at[:, pl.ds(t * band, 8), :], heads.at[t], own.at[2 * t + 1]))
    for load in loads:
        load.start()
    own_main = pltpu.make_async_copy(rows_of(i), main.at[i], own.at[2 * n])
    own_main.start()

    @pl.when(jnp.logical_not(has_south))
    def _():
        south_in[...] = jnp.ones(south_in.shape, south_in.dtype)

    @pl.when(jnp.logical_not(has_north))
    def _():
        north_in[...] = jnp.ones(north_in.shape, north_in.dtype)

    def remote(src, dst, send, recv, x, y):
        return pltpu.make_async_remote_copy(
            src_ref=src, dst_ref=dst, send_sem=send, recv_sem=recv, device_id=(x, y), device_id_type=MESH
        )

    def main_copy(t):
        return remote(rows_of(t), main.at[i], main_send.at[t], main_recv.at[i], t, j)

    def mid_copy(t):
        return remote(pack.at[t], mid.at[i], mid_send.at[t], mid_recv.at[i], t, j)

    def to_north():
        return remote(cells.at[:, pl.ds(n * band - 8, 8), :], south_in, edge_send.at[0], edge_recv.at[0], i, after)

    def to_south():
        return remote(cells.at[:, pl.ds(0, 8), :], north_in, edge_send.at[1], edge_recv.at[1], i, before)

    sub = lax.broadcasted_iota(jnp.int32, (8, cells.shape[2]), 0)

    def make_pack(t, under, over):
        low = [pltpu.roll(under[p].astype(jnp.float32), 2 + 2 * p, 0) for p in range(2)]
        high = [pltpu.roll(over[p].astype(jnp.float32), 4 + p, 0) for p in range(2)]
        rows = jnp.where(sub < 2, low[0], jnp.where(sub < 4, low[1], jnp.where(sub == 4, high[0], high[1])))
        pack[t] = rows.astype(jnp.bfloat16)

    pl.semaphore_wait(barrier, i + jnp.where(has_south | first_of_all, 1, 0))

    @pl.when(has_left)
    def _():
        main_copy(0).start()

    for t in range(n - 2, -1, -1):
        @pl.when(i > t)
        def _():
            signal(known.at[i], t, j)

    @pl.when(has_south)
    def _():
        signal(known.at[0], i, before)
        to_south().start()

    for load in loads:
        load.wait()
    for t in range(1, n - 1):
        make_pack(t, tails.at[t - 1], heads.at[t + 1])

    @pl.when(has_right)
    def _():
        pl.semaphore_wait(known.at[i + 1], 1)
        main_copy(i + 1).start()

    @pl.when(i + 1 < n - 1)
    def _():
        mid_copy(i + 1).start()

    @pl.when(has_north)
    def _():
        pl.semaphore_wait(known.at[0], 1)
        to_north().start()

    @pl.when(has_south)
    def _():
        to_north().wait_recv()

    @pl.when(has_north)
    def _():
        to_south().wait_recv()

    make_pack(0, south_in, heads.at[1])
    make_pack(n - 1, tails.at[n - 2], north_in)

    @pl.when(i + 1 == n - 1)
    def _():
        mid_copy(n - 1).start()

    @pl.when(has_left)
    def _():
        mid_copy(0).start()

    for t in range(1, n - 1):
        @pl.when(i > t)
        def _():
            main_copy(t).start()
            mid_copy(t).start()

    for t in range(2, n):
        @pl.when(i + 1 < t)
        def _():
            pl.semaphore_wait(known.at[t], 1)
            main_copy(t).start()
            mid_copy(t).start()

    own_mid = pltpu.make_async_copy(pack.at[i], mid.at[i], own.at[2 * n + 1])
    own_mid.start()

    first = arrival_stage(n, m, main, mid, fields)
    own_main.wait()
    own_mid.wait()
    first(i)
    orders = [arrivals(n, at) for at in range(n)]
    for step in range(n - 1):
        k = chosen(i, [order[step] for order in orders])
        remote(pack.at[0], mid.at[k], mid_send.at[k], mid_recv.at[k], k, j).wait_recv()
        remote(rows_of(0), main.at[k], main_send.at[k], main_recv.at[k], k, j).wait_recv()
        first(k)

    for t in range(n):
        @pl.when(i != t)
        def _():
            main_copy(t).wait_send()
            mid_copy(t).wait_send()

    @pl.when(has_north)
    def _():
        to_north().wait_send()

    @pl.when(has_south)
    def _():
        to_south().wait_send()


def parts(x0, y0, x1, y1):
    s0, s1 = x0 + y0, x1 + y1
    return x0 * y0 * s1 + x1 * y1 * s0, s0 * s1


def two_faces(one, two):
    scale = 2.0 / (one[1] * two[1])
    return one[0] * two[1] * scale, two[0] * one[1] * scale


def middle(one, two):
    x, y = one[0] * two[1], two[0] * one[1]
    total = 1.0 / (x + y)
    return x * total, y * total, 2.0 * (one[0] * two[0]) * total


def verticals(pairs):
    sums = [x + y for x, y in pairs]
    low, high = sums[0] * sums[1], sums[2] * sums[3]
    scale = 4.0 / (low * high)
    low, high = high * scale, low * scale
    shares = (sums[1] * low, sums[0] * low, sums[3] * high, sums[2] * high)
    return [x * y * share for (x, y), share in zip(pairs, shares)]


def arrival_stage(n, m, main, mid, fields):
    band = main.shape[2]
    block = main.shape[3]
    half = band // 2
    rows = fields.shape[2]
    tiles = fields.shape[0] - 1
    per_block = block // (2 * LANES)
    i = lax.axis_index("gx")
    j = lax.axis_index("gy")
    last_rows = (i == n - 1) & (j == m - 1)

    taken = 2 * band + 8
    want = lax.broadcasted_iota(jnp.int32, (4 * rows, taken), 0)
    have = lax.broadcasted_iota(jnp.int32, (4 * rows, taken), 1)
    group = jnp.where(want >= 3 * rows, 3, jnp.where(want >= 2 * rows, 2, jnp.where(want >= rows, 1, 0)))
    place = want - group * rows
    plane = jnp.where(group >= 2, 1, 0)
    odd = group - 2 * plane
    inside = plane * band + 2 * jnp.where(place < half, place, 0) + odd
    above = jnp.where(odd == 0, 2 * band + 4 + plane, plane * band + 1)
    below = 2 * band + 2 * plane + odd
    source = jnp.where(place == half, above, jnp.where(place == rows - 1, below, inside))
    pick_rows = jnp.where(have == source, 1.0, 0.0).astype(jnp.bfloat16)
    fine = lax.broadcasted_iota(jnp.int32, (2 * LANES, 2 * LANES), 0)
    to = lax.broadcasted_iota(jnp.int32, (2 * LANES, 2 * LANES), 1)
    pick_cols = jnp.where(fine == jnp.where(to < LANES, 2 * to, 2 * (to - LANES) + 1), 1.0, 0.0).astype(jnp.bfloat16)

    top = (lax.broadcasted_iota(jnp.int32, (rows, LANES), 0) == half - 1) & last_rows

    def up(x):
        return pltpu.roll(x, rows - 1, 0)

    def tile_terms(k, part):
        t = k * per_block + part
        cols = pl.ds(pl.multiple_of(part * 2 * LANES, 2 * LANES), 2 * LANES)
        stored = jnp.concatenate(
            [
                main[k, 0, :, cols].astype(jnp.float32),
                main[k, 1, :, cols].astype(jnp.float32),
                mid[k, :, cols].astype(jnp.float32),
            ],
            axis=0,
        ).astype(jnp.bfloat16)
        picked = jnp.dot(pick_rows, stored, preferred_element_type=jnp.float32).astype(jnp.bfloat16)
        split = jnp.dot(picked, pick_cols, preferred_element_type=jnp.float32)
        a0, c0, a1, c1 = (split[g * rows : (g + 1) * rows, :LANES] for g in range(4))
        b0, d0, b1, d1 = (split[g * rows : (g + 1) * rows, LANES:] for g in range(4))
        def wall(x0, x1, inner):
            return jnp.where(top, 0.5 * (x0 + x1), inner[0]), jnp.where(top, 1.0, inner[1])

        s0, n0, t0 = middle(parts(a0, c0, a1, c1), wall(c0, c1, parts(c0, up(a0), c1, up(a1))))
        s1, n1, t1 = middle(parts(b0, d0, b1, d1), wall(d0, d1, parts(d0, up(b0), d1, up(b1))))
        h1, g1 = two_faces(parts(a0, b0, a1, b1), parts(c0, d0, c1, d1))
        pairs = ((a0, a1), (b0, b1), (c0, c1), (d0, d1))
        side_a, side_b, side_c, side_d = (
            (x + ((k0 + k1) + v)) - v for x, (k0, k1), v in zip((h1, h1, g1, g1), pairs, verticals(pairs))
        )
        for at, value in enumerate(
            (a0, a1, c0, c1, s0, n0, b0, b1, d0, d1, t0, s1, n1, t1, h1, g1, side_a, side_b, side_c, side_d)
        ):
            fields[t, at] = value

    def first(k):
        lax.fori_loop(0, per_block, lambda part, carry: (tile_terms(k, part), carry)[1], 0, unroll=UNROLL)

    ones = jnp.ones((rows, LANES), jnp.float32)
    for at in range(6):
        fields[tiles, at] = ones

    return first


def stencil_kernel(n, m, half, chunk, fields, out, held, sent):
    rows = fields.shape[2]
    tiles = fields.shape[0] - 1
    i = lax.axis_index("gx")
    j = lax.axis_index("gy")
    lane = lax.broadcasted_iota(jnp.int32, (rows, LANES), 1)
    sub = lax.broadcasted_iota(jnp.int32, (rows, LANES), 0)
    bottom = (sub == 0) & (i == 0) & (j == 0)
    top = (sub == half - 1) & (i == n - 1) & (j == m - 1)

    def up(x):
        return pltpu.roll(x, rows - 1, 0)

    def down(x):
        return pltpu.roll(x, 1, 0)

    def step(t, carry):
        last = (lane == LANES - 1) & (t == tiles - 1)
        first_lane = (lane == 0) & (t == 0)

        def ahead(at):
            return pltpu.roll(jnp.where(lane == 0, fields[t + 1, at], fields[t, at]), LANES - 1, 1)

        rolled = []

        def behind(x):
            turned = pltpu.roll(x, 1, 1)
            before = carry[len(rolled)]
            rolled.append(turned)
            return jnp.where(lane == 0, before, turned)

        a0, a1, c0, c1, s0, n0, b0, b1, d0, d1 = (fields[t, at] for at in range(10))
        t0, s1, n1, t1, h1, g1, side_a, side_b, side_c, side_d = (fields[t, at] for at in range(10, 20))
        wall_a, wall_b = a0 + a1, b0 + b1
        h2, g2 = two_faces(parts(b0, ahead(0), b1, ahead(1)), parts(d0, ahead(2), d1, ahead(3)))
        h2 = jnp.where(last, wall_b, h2)
        g2 = jnp.where(last, d0 + d1, g2)
        total = 1.0 / (h1 + h2)
        left, right = h1 * total, h2 * total
        left_up = up(left)
        right_up = up(right)
        s0_next = ahead(4)
        n0_next = ahead(5)
        side_a = side_a + jnp.where(first_lane, wall_a, behind(h2))
        side_c = side_c + jnp.where(first_lane, c0 + c1, behind(g2))
        side_b = side_b + h2
        side_d = side_d + g2

        nc = n0 * side_c
        sc = s0 * side_c
        nd = n1 * side_d
        sd = s1 * side_d
        even = side_a + t0 + s0 * sc + jnp.where(bottom, wall_a, down(t0 + n0 * nc))
        odd_ = side_b + t1 + s1 * sd + jnp.where(bottom, wall_b, down(t1 + n1 * nd))
        even_up = s0 * nc - t0
        odd_up = s1 * nd - t1
        sg = s0 * g1
        ng = n0 * g1
        sq = s0_next * g2
        nq = n0_next * g2
        p = h1 + s1 * sg + jnp.where(bottom, 0.0, down(n1 * ng))
        q = h2 + s1 * sq + jnp.where(bottom, 0.0, down(n1 * nq))
        p_up = n1 * sg
        p_down = s1 * ng
        q_up = s1 * nq
        q_down = n1 * sq

        mid = left * odd_ - p
        east = jnp.where(last, 0.0, right * mid - left * q)
        centre = even + left * (mid - p) + behind(right * (right * odd_ - 2.0 * q))
        lo = left * odd_up - p_up
        ro = right * odd_up - q_down
        north = even_up + left_up * lo - left * p_down + behind(right_up * ro - right * q_up)
        north = jnp.where(top, 0.0, north)
        north_east = jnp.where(last | top, 0.0, right_up * lo - left * q_up)
        north_west = jnp.where(last | top, 0.0, left_up * ro - right * p_down)
        west = behind(east)
        ne_back = behind(north_east)
        nw_back = behind(north_west)
        cols = pl.ds(pl.multiple_of(t * LANES, LANES), LANES)

        def below(x):
            return jnp.where(bottom, 0.0, down(x))

        for at, value in enumerate(
            (below(ne_back), below(north), below(north_west), west, centre, east, nw_back, north, north_east)
        ):
            held[at, :, cols] = value[:half]
        return tuple(rolled)

    def leave(c):
        cols = pl.ds(c * chunk * LANES, chunk * LANES)
        return pltpu.make_async_copy(held.at[:, :, cols], out.at[:, :, cols], sent.at[c])

    carry = (jnp.zeros((rows, LANES), jnp.float32),) * 7
    for c in range(tiles // chunk):
        carry = lax.fori_loop(c * chunk, (c + 1) * chunk, step, carry, unroll=STEPS)
        leave(c).start()
    for c in range(tiles // chunk):
        leave(c).wait()


def shards(n, m, conductivity):
    planes, local_rows, local_cols = conductivity.shape
    band = local_rows // n
    half = band // 2
    rows = -(-(half + 2) // 8) * 8
    tiles = n * local_cols // (2 * LANES)
    vmem = pl.BlockSpec(memory_space=pltpu.VMEM)
    anywhere = pl.BlockSpec(memory_space=pl.ANY)
    dma = pltpu.SemaphoreType.DMA
    shape = (tiles + 1, 20, rows, LANES)
    fields = pl.pallas_call(
        functools.partial(coarse_kernel, n, m),
        out_shape=jax.ShapeDtypeStruct(shape, jnp.float32),
        in_specs=[anywhere],
        out_specs=vmem,
        scratch_shapes=[
            pltpu.VMEM((n, planes, band, local_cols), jnp.bfloat16),
            pltpu.VMEM((n, 8, local_cols), jnp.bfloat16),
            pltpu.VMEM((n, planes, 8, local_cols), jnp.bfloat16),
            pltpu.VMEM((n, planes, 8, local_cols), jnp.bfloat16),
            pltpu.VMEM((planes, 8, local_cols), jnp.bfloat16),
            pltpu.VMEM((planes, 8, local_cols), jnp.bfloat16),
            pltpu.VMEM((n, 8, local_cols), jnp.bfloat16),
            dma((n,)),
            dma((n,)),
            dma((n,)),
            dma((n,)),
            dma((2,)),
            dma((2,)),
            pltpu.SemaphoreType.REGULAR((n,)),
            dma((2 * n + 2,)),
        ],
        compiler_params=pltpu.CompilerParams(
            collective_id=0, has_side_effects=True, vmem_limit_bytes=VMEM_LIMIT
        ),
        name="coarse",
    )(pltpu.with_memory_space_constraint(conductivity, pltpu.HBM))
    chunk = tiles // 4
    stencil = pl.pallas_call(
        functools.partial(stencil_kernel, n, m, half, chunk),
        out_shape=jax.ShapeDtypeStruct((9, half, tiles * LANES), jnp.float32),
        in_specs=[vmem],
        out_specs=anywhere,
        scratch_shapes=[pltpu.VMEM((9, half, tiles * LANES), jnp.float32), dma((4,))],
        compiler_params=pltpu.CompilerParams(vmem_limit_bytes=VMEM_LIMIT),
        name="stencil",
    )(fields)
    return stencil[:, None]


def solution(mesh):
    n, m = mesh.shape["gx"], mesh.shape["gy"]
    return jax.shard_map(
        functools.partial(shards, n, m),
        mesh=mesh,
        in_specs=(P(None, "gy", "gx"),),
        out_specs=P(None, "gy", "gx", None),
        check_vma=False,
    )
```

```python
import functools

import jax
import jax.numpy as jnp
from jax import lax
from jax.experimental import pallas as pl
from jax.experimental.pallas import tpu as pltpu
from jax.sharding import PartitionSpec as P

MESH = pl.DeviceIdType.MESH
LANES = 128
UNROLL = 4
VMEM_LIMIT = 16 * 1024 * 1024


def arrivals(n, i):
    half = n // 2
    own_half = range(half) if i < half else range(half, n)
    if i < half:
        return [k for k in own_half if k != i] + list(range(n - 1, half - 1, -1))
    return [k for k in own_half if k < i] + list(range(half)) + [k for k in own_half if k > i]


def spans(n, i, per_block):
    tiles = n * per_block
    there, found = set(), []
    for k in [i] + arrivals(n, i):
        new = set(range(k * per_block, (k + 1) * per_block))
        there |= new
        ready = [
            t for t in range(tiles)
            if {max(t - 1, 0), t, min(t + 1, tiles - 1)} <= there and {t - 1, t, t + 1} & new
        ]
        found.append((ready[0], ready[-1] + 1) if ready else (0, 0))
    return found


def last_span(n, i, per_block):
    first, end = spans(n, i, per_block)[-1]
    return min(first, n * per_block - per_block - 2)


def chosen(i, values):
    picked = values[-1]
    for at in range(len(values) - 2, -1, -1):
        picked = jnp.where(i == at, values[at], picked)
    return picked


def coarse_kernel(
    n, m, cells, fields, held, main, mid, tails, heads, south_in, north_in, pack,
    main_send, main_recv, mid_send, mid_recv, edge_send, edge_recv, known, own,
):
    i = lax.axis_index("gx")
    j = lax.axis_index("gy")
    band = main.shape[2]
    has_left, has_right = i > 0, i < n - 1
    has_south, has_north = j > 0, j < m - 1
    before, after = jnp.maximum(j - 1, 0), jnp.minimum(j + 1, m - 1)

    def signal(sem, x, y):
        pl.semaphore_signal(sem, inc=1, device_id=(x, y), device_id_type=MESH)

    barrier = pltpu.get_barrier_semaphore()
    for t in range(1, n):
        @pl.when(i < t)
        def _():
            signal(barrier, t, j)

    @pl.when(has_north)
    def _():
        signal(barrier, i, after)

    first_of_all = (i == 0) & (j == 0)

    @pl.when((i == 0) & (j == 1))
    def _():
        signal(barrier, 0, 0)

    def rows_of(t):
        return cells.at[:, pl.ds(pl.multiple_of(t * band, band), band), :]

    loads = []
    for t in range(n):
        loads.append(pltpu.make_async_copy(cells.at[:, pl.ds(t * band + band - 8, 8), :], tails.at[t], own.at[2 * t]))
        loads.append(pltpu.make_async_copy(cells.at[:, pl.ds(t * band, 8), :], heads.at[t], own.at[2 * t + 1]))
    for load in loads:
        load.start()
    own_main = pltpu.make_async_copy(rows_of(i), main.at[i], own.at[2 * n])
    own_main.start()

    @pl.when(jnp.logical_not(has_south))
    def _():
        south_in[...] = jnp.ones(south_in.shape, south_in.dtype)

    @pl.when(jnp.logical_not(has_north))
    def _():
        north_in[...] = jnp.ones(north_in.shape, north_in.dtype)

    def remote(src, dst, send, recv, x, y):
        return pltpu.make_async_remote_copy(
            src_ref=src, dst_ref=dst, send_sem=send, recv_sem=recv, device_id=(x, y), device_id_type=MESH
        )

    def main_copy(t):
        return remote(rows_of(t), main.at[i], main_send.at[t], main_recv.at[i], t, j)

    def mid_copy(t):
        return remote(pack.at[t], mid.at[i], mid_send.at[t], mid_recv.at[i], t, j)

    def to_north():
        return remote(cells.at[:, pl.ds(n * band - 8, 8), :], south_in, edge_send.at[0], edge_recv.at[0], i, after)

    def to_south():
        return remote(cells.at[:, pl.ds(0, 8), :], north_in, edge_send.at[1], edge_recv.at[1], i, before)

    sub = lax.broadcasted_iota(jnp.int32, (8, cells.shape[2]), 0)

    def make_pack(t, under, over):
        low = [pltpu.roll(under[p].astype(jnp.float32), 2 + 2 * p, 0) for p in range(2)]
        high = [pltpu.roll(over[p].astype(jnp.float32), 4 + p, 0) for p in range(2)]
        rows = jnp.where(sub < 2, low[0], jnp.where(sub < 4, low[1], jnp.where(sub == 4, high[0], high[1])))
        pack[t] = rows.astype(jnp.bfloat16)

    pl.semaphore_wait(barrier, i + jnp.where(has_south | first_of_all, 1, 0))

    @pl.when(has_left)
    def _():
        main_copy(0).start()

    for t in range(n - 2, -1, -1):
        @pl.when(i > t)
        def _():
            signal(known.at[i], t, j)

    @pl.when(has_south)
    def _():
        signal(known.at[0], i, before)
        to_south().start()

    for load in loads:
        load.wait()
    for t in range(1, n - 1):
        make_pack(t, tails.at[t - 1], heads.at[t + 1])

    @pl.when(has_right)
    def _():
        pl.semaphore_wait(known.at[i + 1], 1)
        main_copy(i + 1).start()

    @pl.when(i + 1 < n - 1)
    def _():
        mid_copy(i + 1).start()

    @pl.when(has_north)
    def _():
        pl.semaphore_wait(known.at[0], 1)
        to_north().start()

    @pl.when(has_south)
    def _():
        to_north().wait_recv()

    @pl.when(has_north)
    def _():
        to_south().wait_recv()

    make_pack(0, south_in, heads.at[1])
    make_pack(n - 1, tails.at[n - 2], north_in)

    @pl.when(i + 1 == n - 1)
    def _():
        mid_copy(n - 1).start()

    @pl.when(has_left)
    def _():
        mid_copy(0).start()

    for t in range(1, n - 1):
        @pl.when(i > t)
        def _():
            main_copy(t).start()
            mid_copy(t).start()

    for t in range(2, n):
        @pl.when(i + 1 < t)
        def _():
            pl.semaphore_wait(known.at[t], 1)
            main_copy(t).start()
            mid_copy(t).start()

    own_mid = pltpu.make_async_copy(pack.at[i], mid.at[i], own.at[2 * n + 1])
    own_mid.start()

    first = arrival_stage(n, m, main, mid, fields)
    tile_stencil, carry_into = stencil_stage(n, m, band // 2, fields)
    per_block = cells.shape[2] // (2 * LANES)
    ranges = [spans(n, at, per_block) for at in range(n)]

    def second(step):
        low, end = (chosen(i, [found[step][side] for found in ranges]) for side in range(2))

        def one(t, carry):
            values, carry = tile_stencil(t, carry)
            cols = pl.ds(pl.multiple_of(t * LANES, LANES), LANES)
            for at, value in enumerate(values):
                held[at, :, cols] = value
            return carry

        lax.fori_loop(low, end, one, carry_into(low))

    own_main.wait()
    own_mid.wait()
    first(i)
    second(0)
    orders = [arrivals(n, at) for at in range(n)]
    for step in range(n - 1):
        k = chosen(i, [order[step] for order in orders])
        remote(pack.at[0], mid.at[k], mid_send.at[k], mid_recv.at[k], k, j).wait_recv()
        remote(rows_of(0), main.at[k], main_send.at[k], main_recv.at[k], k, j).wait_recv()
        first(k)
        if step < n - 2:
            second(step + 1)

    for t in range(n):
        @pl.when(i != t)
        def _():
            main_copy(t).wait_send()
            mid_copy(t).wait_send()

    @pl.when(has_north)
    def _():
        to_north().wait_send()

    @pl.when(has_south)
    def _():
        to_south().wait_send()


def parts(x0, y0, x1, y1):
    s0, s1 = x0 + y0, x1 + y1
    return x0 * y0 * s1 + x1 * y1 * s0, s0 * s1


def two_faces(one, two):
    scale = 2.0 / (one[1] * two[1])
    return one[0] * two[1] * scale, two[0] * one[1] * scale


def middle(one, two):
    x, y = one[0] * two[1], two[0] * one[1]
    total = 1.0 / (x + y)
    return x * total, y * total, 2.0 * (one[0] * two[0]) * total


def verticals(pairs):
    sums = [x + y for x, y in pairs]
    low, high = sums[0] * sums[1], sums[2] * sums[3]
    scale = 4.0 / (low * high)
    low, high = high * scale, low * scale
    shares = (sums[1] * low, sums[0] * low, sums[3] * high, sums[2] * high)
    return [x * y * share for (x, y), share in zip(pairs, shares)]


def arrival_stage(n, m, main, mid, fields):
    band = main.shape[2]
    block = main.shape[3]
    half = band // 2
    rows = fields.shape[2]
    tiles = fields.shape[0] - 1
    per_block = block // (2 * LANES)
    i = lax.axis_index("gx")
    j = lax.axis_index("gy")
    last_rows = (i == n - 1) & (j == m - 1)

    taken = 2 * band + 8
    want = lax.broadcasted_iota(jnp.int32, (4 * rows, taken), 0)
    have = lax.broadcasted_iota(jnp.int32, (4 * rows, taken), 1)
    group = jnp.where(want >= 3 * rows, 3, jnp.where(want >= 2 * rows, 2, jnp.where(want >= rows, 1, 0)))
    place = want - group * rows
    plane = jnp.where(group >= 2, 1, 0)
    odd = group - 2 * plane
    inside = plane * band + 2 * jnp.where(place < half, place, 0) + odd
    above = jnp.where(odd == 0, 2 * band + 4 + plane, plane * band + 1)
    below = 2 * band + 2 * plane + odd
    source = jnp.where(place == half, above, jnp.where(place == rows - 1, below, inside))
    pick_rows = jnp.where(have == source, 1.0, 0.0).astype(jnp.bfloat16)
    fine = lax.broadcasted_iota(jnp.int32, (2 * LANES, 2 * LANES), 0)
    to = lax.broadcasted_iota(jnp.int32, (2 * LANES, 2 * LANES), 1)
    pick_cols = jnp.where(fine == jnp.where(to < LANES, 2 * to, 2 * (to - LANES) + 1), 1.0, 0.0).astype(jnp.bfloat16)

    top = (lax.broadcasted_iota(jnp.int32, (rows, LANES), 0) == half - 1) & last_rows

    def up(x):
        return pltpu.roll(x, rows - 1, 0)

    def tile_terms(k, part):
        t = k * per_block + part
        cols = pl.ds(pl.multiple_of(part * 2 * LANES, 2 * LANES), 2 * LANES)
        stored = jnp.concatenate(
            [
                main[k, 0, :, cols].astype(jnp.float32),
                main[k, 1, :, cols].astype(jnp.float32),
                mid[k, :, cols].astype(jnp.float32),
            ],
            axis=0,
        ).astype(jnp.bfloat16)
        picked = jnp.dot(pick_rows, stored, preferred_element_type=jnp.float32).astype(jnp.bfloat16)
        split = jnp.dot(picked, pick_cols, preferred_element_type=jnp.float32)
        a0, c0, a1, c1 = (split[g * rows : (g + 1) * rows, :LANES] for g in range(4))
        b0, d0, b1, d1 = (split[g * rows : (g + 1) * rows, LANES:] for g in range(4))
        def wall(x0, x1, inner):
            return jnp.where(top, 0.5 * (x0 + x1), inner[0]), jnp.where(top, 1.0, inner[1])

        s0, n0, t0 = middle(parts(a0, c0, a1, c1), wall(c0, c1, parts(c0, up(a0), c1, up(a1))))
        s1, n1, t1 = middle(parts(b0, d0, b1, d1), wall(d0, d1, parts(d0, up(b0), d1, up(b1))))
        h1, g1 = two_faces(parts(a0, b0, a1, b1), parts(c0, d0, c1, d1))
        pairs = ((a0, a1), (b0, b1), (c0, c1), (d0, d1))
        side_a, side_b, side_c, side_d = (
            (x + ((k0 + k1) + v)) - v for x, (k0, k1), v in zip((h1, h1, g1, g1), pairs, verticals(pairs))
        )
        for at, value in enumerate(
            (a0, a1, c0, c1, s0, n0, b0, b1, d0, d1, t0, s1, n1, t1, h1, g1, side_a, side_b, side_c, side_d)
        ):
            fields[t, at] = value

    def first(k):
        lax.fori_loop(0, per_block, lambda part, carry: (tile_terms(k, part), carry)[1], 0, unroll=UNROLL)

    ones = jnp.ones((rows, LANES), jnp.float32)
    for at in range(6):
        fields[tiles, at] = ones

    return first


def stencil_stage(n, m, half, fields):
    rows = fields.shape[2]
    tiles = fields.shape[0] - 1
    i = lax.axis_index("gx")
    j = lax.axis_index("gy")
    lane = lax.broadcasted_iota(jnp.int32, (rows, LANES), 1)
    sub = lax.broadcasted_iota(jnp.int32, (rows, LANES), 0)
    bottom = (sub == 0) & (i == 0) & (j == 0)
    top = (sub == half - 1) & (i == n - 1) & (j == m - 1)

    def up(x):
        return pltpu.roll(x, rows - 1, 0)

    def down(x):
        return pltpu.roll(x, 1, 0)

    def step(t, carry):
        last = (lane == LANES - 1) & (t == tiles - 1)
        first_lane = (lane == 0) & (t == 0)

        def ahead(at):
            return pltpu.roll(jnp.where(lane == 0, fields[t + 1, at], fields[t, at]), LANES - 1, 1)

        rolled = []

        def behind(x):
            turned = pltpu.roll(x, 1, 1)
            before = carry[len(rolled)]
            rolled.append(turned)
            return jnp.where(lane == 0, before, turned)

        a0, a1, c0, c1, s0, n0, b0, b1, d0, d1 = (fields[t, at] for at in range(10))
        t0, s1, n1, t1, h1, g1, side_a, side_b, side_c, side_d = (fields[t, at] for at in range(10, 20))
        wall_a, wall_b = a0 + a1, b0 + b1
        h2, g2 = two_faces(parts(b0, ahead(0), b1, ahead(1)), parts(d0, ahead(2), d1, ahead(3)))
        h2 = jnp.where(last, wall_b, h2)
        g2 = jnp.where(last, d0 + d1, g2)
        total = 1.0 / (h1 + h2)
        left, right = h1 * total, h2 * total
        left_up = up(left)
        right_up = up(right)
        s0_next = ahead(4)
        n0_next = ahead(5)
        side_a = side_a + jnp.where(first_lane, wall_a, behind(h2))
        side_c = side_c + jnp.where(first_lane, c0 + c1, behind(g2))
        side_b = side_b + h2
        side_d = side_d + g2

        nc = n0 * side_c
        sc = s0 * side_c
        nd = n1 * side_d
        sd = s1 * side_d
        even = side_a + t0 + s0 * sc + jnp.where(bottom, wall_a, down(t0 + n0 * nc))
        odd_ = side_b + t1 + s1 * sd + jnp.where(bottom, wall_b, down(t1 + n1 * nd))
        even_up = s0 * nc - t0
        odd_up = s1 * nd - t1
        sg = s0 * g1
        ng = n0 * g1
        sq = s0_next * g2
        nq = n0_next * g2
        p = h1 + s1 * sg + jnp.where(bottom, 0.0, down(n1 * ng))
        q = h2 + s1 * sq + jnp.where(bottom, 0.0, down(n1 * nq))
        p_up = n1 * sg
        p_down = s1 * ng
        q_up = s1 * nq
        q_down = n1 * sq

        mid = left * odd_ - p
        east = jnp.where(last, 0.0, right * mid - left * q)
        centre = even + left * (mid - p) + behind(right * (right * odd_ - 2.0 * q))
        lo = left * odd_up - p_up
        ro = right * odd_up - q_down
        north = even_up + left_up * lo - left * p_down + behind(right_up * ro - right * q_up)
        north = jnp.where(top, 0.0, north)
        north_east = jnp.where(last | top, 0.0, right_up * lo - left * q_up)
        north_west = jnp.where(last | top, 0.0, left_up * ro - right * p_down)
        west = behind(east)
        ne_back = behind(north_east)
        nw_back = behind(north_west)

        def below(x):
            return jnp.where(bottom, 0.0, down(x))

        values = (below(ne_back), below(north), below(north_west), west, centre, east, nw_back, north, north_east)
        return tuple(value[:half] for value in values), tuple(rolled)

    def carry_into(t):
        carry = step(jnp.maximum(t - 1, 0), (jnp.zeros((rows, LANES), jnp.float32),) * 7)[1]
        return tuple(jnp.where(t > 0, x, 0.0) for x in carry)

    return step, carry_into


def stencil_kernel(n, m, half, per_block, fields, held, out, late, sent):
    tiles = fields.shape[0] - 1
    count = per_block + 2
    i = lax.axis_index("gx")
    low = chosen(i, [last_span(n, at, per_block) for at in range(n)])
    tile_stencil, carry_into = stencil_stage(n, m, half, fields)

    def columns(t, width):
        return pl.ds(pl.multiple_of(t * LANES, LANES), width * LANES)

    def early(q):
        cols = columns(jnp.where(q < low, q, q + count), 1)
        return pltpu.make_async_copy(held.at[:, :, cols], out.at[:, :, cols], sent.at[q])

    for q in range(tiles - count):
        early(q).start()

    def leave(c):
        return pltpu.make_async_copy(
            late.at[:, :, pl.ds(c * 2 * LANES, 2 * LANES)], out.at[:, :, columns(low + 2 * c, 2)],
            sent.at[tiles - count + c],
        )

    carry = carry_into(low)
    for q in range(count):
        values, carry = tile_stencil(low + q, carry)
        for at, value in enumerate(values):
            late[at, :, q * LANES : (q + 1) * LANES] = value
        if q % 2:
            leave(q // 2).start()
    for q in range(tiles - count):
        early(q).wait()
    for c in range(count // 2):
        leave(c).wait()


def shards(n, m, conductivity):
    planes, local_rows, local_cols = conductivity.shape
    band = local_rows // n
    half = band // 2
    rows = -(-(half + 2) // 8) * 8
    tiles = n * local_cols // (2 * LANES)
    vmem = pl.BlockSpec(memory_space=pltpu.VMEM)
    anywhere = pl.BlockSpec(memory_space=pl.ANY)
    dma = pltpu.SemaphoreType.DMA
    shape = (tiles + 1, 20, rows, LANES)
    per_block = local_cols // (2 * LANES)
    result = jax.ShapeDtypeStruct((9, half, tiles * LANES), jnp.float32)
    fields, held = pl.pallas_call(
        functools.partial(coarse_kernel, n, m),
        out_shape=(jax.ShapeDtypeStruct(shape, jnp.float32), result),
        in_specs=[anywhere],
        out_specs=(vmem, vmem),
        scratch_shapes=[
            pltpu.VMEM((n, planes, band, local_cols), jnp.bfloat16),
            pltpu.VMEM((n, 8, local_cols), jnp.bfloat16),
            pltpu.VMEM((n, planes, 8, local_cols), jnp.bfloat16),
            pltpu.VMEM((n, planes, 8, local_cols), jnp.bfloat16),
            pltpu.VMEM((planes, 8, local_cols), jnp.bfloat16),
            pltpu.VMEM((planes, 8, local_cols), jnp.bfloat16),
            pltpu.VMEM((n, 8, local_cols), jnp.bfloat16),
            dma((n,)),
            dma((n,)),
            dma((n,)),
            dma((n,)),
            dma((2,)),
            dma((2,)),
            pltpu.SemaphoreType.REGULAR((n,)),
            dma((2 * n + 2,)),
        ],
        compiler_params=pltpu.CompilerParams(
            collective_id=0, has_side_effects=True, vmem_limit_bytes=VMEM_LIMIT
        ),
        name="coarse",
    )(pltpu.with_memory_space_constraint(conductivity, pltpu.HBM))
    count = per_block + 2
    stencil = pl.pallas_call(
        functools.partial(stencil_kernel, n, m, half, per_block),
        out_shape=result,
        in_specs=[vmem, vmem],
        out_specs=anywhere,
        scratch_shapes=[pltpu.VMEM((9, half, count * LANES), jnp.float32), dma((tiles - count + count // 2,))],
        compiler_params=pltpu.CompilerParams(vmem_limit_bytes=VMEM_LIMIT),
        name="stencil",
    )(fields, held)
    return stencil[:, None]


def solution(mesh):
    n, m = mesh.shape["gx"], mesh.shape["gy"]
    return jax.shard_map(
        functools.partial(shards, n, m),
        mesh=mesh,
        in_specs=(P(None, "gy", "gx"),),
        out_specs=P(None, "gy", "gx", None),
        check_vma=False,
    )
```

```python
import functools

import jax
import jax.numpy as jnp
from jax import lax
from jax.experimental import pallas as pl
from jax.experimental.pallas import tpu as pltpu
from jax.sharding import PartitionSpec as P

MESH = pl.DeviceIdType.MESH
LANES = 128
PIECES = 2
VMEM_LIMIT = 16 * 1024 * 1024


def arrivals(n, i):
    half = n // 2
    if i < half:
        return list(range(i)) + list(range(n - 1, half, -1)) + list(range(i + 1, half)) + [half]
    return list(range(half, i)) + list(range(half - 1)) + list(range(i + 1, n)) + [half - 1]


def spans(n, i, per_block):
    tiles, piece = n * per_block, per_block // PIECES
    order = [i] + arrivals(n, i)
    arrived = [set(range(k * per_block, (k + 1) * per_block)) for k in order[:-1]]
    last = order[-1] * per_block
    arrived += [set(range(last + p * piece, last + (p + 1) * piece)) for p in range(PIECES)]
    there, found = set(), []
    for new in arrived:
        there |= new
        ready = [
            t for t in range(tiles)
            if {max(t - 1, 0), t, min(t + 1, tiles - 1)} <= there and {t - 1, t, t + 1} & new
        ]
        found.append((ready[0], ready[-1] + 1) if ready else (0, 0))
    return found


def last_count(per_block):
    return per_block // PIECES + 2


def last_low(n, i, per_block):
    return min(spans(n, i, per_block)[-1][0], n * per_block - last_count(per_block))


def chosen(i, values):
    picked = values[-1]
    for at in range(len(values) - 2, -1, -1):
        picked = jnp.where(i == at, values[at], picked)
    return picked


def coarse_kernel(
    n, m, cells, fields, held, carried, blocks, rims, south_in, north_in, pack,
    arrived, sent, edge_sent, edge_arrived, known, own,
):
    i = lax.axis_index("gx")
    j = lax.axis_index("gy")
    block = cells.shape[2]
    band = cells.shape[1] // n
    width = block // PIECES
    has_left, has_right = i > 0, i < n - 1
    has_south, has_north = j > 0, j < m - 1
    before, after = jnp.maximum(j - 1, 0), jnp.minimum(j + 1, m - 1)

    def signal(sem, x, y):
        pl.semaphore_signal(sem, inc=1, device_id=(x, y), device_id_type=MESH)

    barrier = pltpu.get_barrier_semaphore()
    for t in range(1, n):
        @pl.when(i < t)
        def _():
            signal(barrier, t, j)

    @pl.when(has_north)
    def _():
        signal(barrier, i, after)

    first_of_all = (i == 0) & (j == 0)

    @pl.when((i == 0) & (j == 1))
    def _():
        signal(barrier, 0, 0)

    def rows_of(t):
        return pl.ds(pl.multiple_of(t * band, band), band)

    loads = []
    for t in range(n - 1):
        loads.append(pltpu.make_async_copy(cells.at[:, pl.ds((t + 1) * band - 8, 8), :], rims.at[0, t], own.at[0]))
        loads.append(pltpu.make_async_copy(cells.at[:, pl.ds((t + 1) * band, 8), :], rims.at[1, t], own.at[0]))
    for plane in range(2):
        loads.append(pltpu.make_async_copy(cells.at[plane, rows_of(i), :], blocks.at[i, pl.ds(plane * band, band), :], own.at[1]))
    for load in loads:
        load.start()

    @pl.when(jnp.logical_not(has_south))
    def _():
        south_in[...] = jnp.ones(south_in.shape, south_in.dtype)

    @pl.when(jnp.logical_not(has_north))
    def _():
        north_in[...] = jnp.ones(north_in.shape, north_in.dtype)

    def remote(src, dst, send, recv, x, y):
        return pltpu.make_async_remote_copy(
            src_ref=src, dst_ref=dst, send_sem=send, recv_sem=recv, device_id=(x, y), device_id_type=MESH
        )

    def cols_of(p):
        return pl.ds(p * width, width)

    def send_rows(t, p):
        for plane in range(2):
            remote(
                cells.at[plane, rows_of(t), cols_of(p)], blocks.at[i, pl.ds(plane * band, band), cols_of(p)],
                sent.at[0], arrived.at[i, p], t, j,
            ).start()

    def send_halo(t, p):
        remote(
            pack.at[t, :, cols_of(p)], blocks.at[i, pl.ds(2 * band, 8), cols_of(p)], sent.at[0], arrived.at[i, p], t, j
        ).start()

    def send(t, rows, halo):
        for p in range(PIECES):
            if halo:
                send_halo(t, p)
            if rows:
                send_rows(t, p)

    def to_north():
        return remote(cells.at[:, pl.ds(n * band - 8, 8), :], south_in, edge_sent.at[0], edge_arrived.at[0], i, after)

    def to_south():
        return remote(cells.at[:, pl.ds(0, 8), :], north_in, edge_sent.at[1], edge_arrived.at[1], i, before)

    sub = lax.broadcasted_iota(jnp.int32, (8, block), 0)

    def make_pack(t, under, over):
        low = [pltpu.roll(under[p].astype(jnp.float32), 2 + 2 * p, 0) for p in range(2)]
        high = [pltpu.roll(over[p].astype(jnp.float32), 4 + p, 0) for p in range(2)]
        rows = jnp.where(sub < 2, low[0], jnp.where(sub < 4, low[1], jnp.where(sub == 4, high[0], high[1])))
        pack[t] = rows.astype(jnp.bfloat16)

    pl.semaphore_wait(barrier, i + jnp.where(has_south | first_of_all, 1, 0))

    @pl.when(has_left)
    def _():
        send(0, True, False)

    for t in range(n - 2, -1, -1):
        @pl.when(i > t)
        def _():
            signal(known.at[i], t, j)

    @pl.when(has_south)
    def _():
        signal(known.at[0], i, before)
        to_south().start()

    pltpu.make_async_copy(rims, rims, own.at[0]).wait()
    for t in range(1, n - 1):
        make_pack(t, rims.at[0, t - 1], rims.at[1, t])

    @pl.when(has_right)
    def _():
        pl.semaphore_wait(known.at[i + 1], 1)
        send(i + 1, True, False)

    @pl.when(i + 1 < n - 1)
    def _():
        send(i + 1, False, True)

    @pl.when(has_north)
    def _():
        pl.semaphore_wait(known.at[0], 1)
        to_north().start()

    @pl.when(has_south)
    def _():
        to_north().wait_recv()

    @pl.when(has_north)
    def _():
        to_south().wait_recv()

    make_pack(0, south_in, rims.at[1, 0])
    make_pack(n - 1, rims.at[0, n - 2], north_in)

    @pl.when(i + 1 == n - 1)
    def _():
        send(n - 1, False, True)

    @pl.when(has_left)
    def _():
        send(0, False, True)

    for t in range(1, n - 1):
        @pl.when(i > t)
        def _():
            send(t, True, True)

    for t in range(2, n):
        @pl.when(i + 1 < t)
        def _():
            pl.semaphore_wait(known.at[t], 1)
            send(t, True, True)

    blocks[i, pl.ds(2 * band, 8), :] = pack[i]

    first = arrival_stage(n, m, band, blocks, fields)
    tile_stencil, carry_into = stencil_stage(n, m, band // 2, fields)
    per_block = block // (2 * LANES)
    per_piece = per_block // PIECES
    ranges = [spans(n, at, per_block) for at in range(n)]

    def second(step):
        low, end = (chosen(i, [found[step][side] for found in ranges]) for side in range(2))

        def one(t, carry):
            values, carry = tile_stencil(t, carry)
            cols = pl.ds(pl.multiple_of(t * LANES, LANES), LANES)
            for at, value in enumerate(values):
                held[at, :, cols] = value
            return carry

        lax.fori_loop(low, end, one, carry_into(low))

    def await_piece(k, p):
        landed = blocks.at[k, :, cols_of(p)]
        remote(landed, landed, sent.at[0], arrived.at[k, p], k, j).wait_recv()

    mine = blocks.at[i, pl.ds(0, 2 * band), :]
    pltpu.make_async_copy(mine, mine, own.at[1]).wait()
    first(i, 0, per_block)
    second(0)
    orders = [arrivals(n, at) for at in range(n)]
    for step in range(n - 2):
        k = chosen(i, [order[step] for order in orders])
        for p in range(PIECES):
            await_piece(k, p)
        first(k, 0, per_block)
        second(step + 1)
    k = chosen(i, [order[n - 2] for order in orders])
    for p in range(PIECES):
        if p == PIECES - 1:
            low = chosen(i, [last_low(n, at, per_block) for at in range(n)])
            for at, value in enumerate(carry_into(low)):
                carried[at] = value
        await_piece(k, p)
        first(k, p * per_piece, per_piece)
        if p < PIECES - 1:
            second(n - 1 + p)

    others = blocks.at[pl.ds(0, n - 1)]
    remote(others, others, sent.at[0], arrived.at[0, 0], i, j).wait_send()

    @pl.when(has_north)
    def _():
        to_north().wait_send()

    @pl.when(has_south)
    def _():
        to_south().wait_send()


def parts(x0, y0, x1, y1):
    s0, s1 = x0 + y0, x1 + y1
    return x0 * y0 * s1 + x1 * y1 * s0, s0 * s1


def two_faces(one, two):
    scale = 2.0 / (one[1] * two[1])
    return one[0] * two[1] * scale, two[0] * one[1] * scale


def middle(one, two):
    x, y = one[0] * two[1], two[0] * one[1]
    total = 1.0 / (x + y)
    return x * total, y * total, 2.0 * (one[0] * two[0]) * total


def verticals(pairs):
    sums = [x + y for x, y in pairs]
    low, high = sums[0] * sums[1], sums[2] * sums[3]
    scale = 4.0 / (low * high)
    low, high = high * scale, low * scale
    shares = (sums[1] * low, sums[0] * low, sums[3] * high, sums[2] * high)
    return [x * y * share for (x, y), share in zip(pairs, shares)]


def arrival_stage(n, m, band, blocks, fields):
    block = blocks.shape[2]
    half = band // 2
    rows = fields.shape[2]
    tiles = fields.shape[0] - 1
    per_block = block // (2 * LANES)
    i = lax.axis_index("gx")
    j = lax.axis_index("gy")
    last_rows = (i == n - 1) & (j == m - 1)

    taken = 2 * band + 8
    want = lax.broadcasted_iota(jnp.int32, (4 * rows, taken), 0)
    have = lax.broadcasted_iota(jnp.int32, (4 * rows, taken), 1)
    group = jnp.where(want >= 3 * rows, 3, jnp.where(want >= 2 * rows, 2, jnp.where(want >= rows, 1, 0)))
    place = want - group * rows
    plane = jnp.where(group >= 2, 1, 0)
    odd = group - 2 * plane
    inside = plane * band + 2 * jnp.where(place < half, place, 0) + odd
    above = jnp.where(odd == 0, 2 * band + 4 + plane, plane * band + 1)
    below = 2 * band + 2 * plane + odd
    source = jnp.where(place == half, above, jnp.where(place == rows - 1, below, inside))
    pick_rows = jnp.where(have == source, 1.0, 0.0).astype(jnp.bfloat16)
    fine = lax.broadcasted_iota(jnp.int32, (2 * LANES, 2 * LANES), 0)
    to = lax.broadcasted_iota(jnp.int32, (2 * LANES, 2 * LANES), 1)
    pick_cols = jnp.where(fine == jnp.where(to < LANES, 2 * to, 2 * (to - LANES) + 1), 1.0, 0.0).astype(jnp.bfloat16)

    top = (lax.broadcasted_iota(jnp.int32, (rows, LANES), 0) == half - 1) & last_rows

    def up(x):
        return pltpu.roll(x, rows - 1, 0)

    def tile_terms(k, part):
        t = k * per_block + part
        cols = pl.ds(part * 2 * LANES, 2 * LANES)
        stored = blocks[k, :, cols]
        picked = jnp.dot(pick_rows, stored, preferred_element_type=jnp.float32).astype(jnp.bfloat16)
        split = jnp.dot(picked, pick_cols, preferred_element_type=jnp.float32)
        a0, c0, a1, c1 = (split[g * rows : (g + 1) * rows, :LANES] for g in range(4))
        b0, d0, b1, d1 = (split[g * rows : (g + 1) * rows, LANES:] for g in range(4))
        def wall(x0, x1, inner):
            return jnp.where(top, 0.5 * (x0 + x1), inner[0]), jnp.where(top, 1.0, inner[1])

        s0, n0, t0 = middle(parts(a0, c0, a1, c1), wall(c0, c1, parts(c0, up(a0), c1, up(a1))))
        s1, n1, t1 = middle(parts(b0, d0, b1, d1), wall(d0, d1, parts(d0, up(b0), d1, up(b1))))
        h1, g1 = two_faces(parts(a0, b0, a1, b1), parts(c0, d0, c1, d1))
        pairs = ((a0, a1), (b0, b1), (c0, c1), (d0, d1))
        side_a, side_b, side_c, side_d = (
            (x + ((k0 + k1) + v)) - v for x, (k0, k1), v in zip((h1, h1, g1, g1), pairs, verticals(pairs))
        )
        for at, value in enumerate(
            (a0, a1, c0, c1, s0, n0, b0, b1, d0, d1, t0, s1, n1, t1, h1, g1, side_a, side_b, side_c, side_d)
        ):
            fields[t, at] = value

    def first(k, start, count):
        for part in range(start, start + count):
            tile_terms(k, part)

    ones = jnp.ones((rows, LANES), jnp.float32)
    for at in range(6):
        fields[tiles, at] = ones

    return first


def stencil_stage(n, m, half, fields):
    rows = fields.shape[2]
    tiles = fields.shape[0] - 1
    i = lax.axis_index("gx")
    j = lax.axis_index("gy")
    lane = lax.broadcasted_iota(jnp.int32, (rows, LANES), 1)
    sub = lax.broadcasted_iota(jnp.int32, (rows, LANES), 0)
    bottom = (sub == 0) & (i == 0) & (j == 0)
    top = (sub == half - 1) & (i == n - 1) & (j == m - 1)

    def up(x):
        return pltpu.roll(x, rows - 1, 0)

    def down(x):
        return pltpu.roll(x, 1, 0)

    def step(t, carry):
        last = (lane == LANES - 1) & (t == tiles - 1)
        first_lane = (lane == 0) & (t == 0)

        def ahead(at):
            return pltpu.roll(jnp.where(lane == 0, fields[t + 1, at], fields[t, at]), LANES - 1, 1)

        rolled = []

        def behind(x):
            turned = pltpu.roll(x, 1, 1)
            before = carry[len(rolled)]
            rolled.append(turned)
            return jnp.where(lane == 0, before, turned)

        a0, a1, c0, c1, s0, n0, b0, b1, d0, d1 = (fields[t, at] for at in range(10))
        t0, s1, n1, t1, h1, g1, side_a, side_b, side_c, side_d = (fields[t, at] for at in range(10, 20))
        wall_a, wall_b = a0 + a1, b0 + b1
        h2, g2 = two_faces(parts(b0, ahead(0), b1, ahead(1)), parts(d0, ahead(2), d1, ahead(3)))
        h2 = jnp.where(last, wall_b, h2)
        g2 = jnp.where(last, d0 + d1, g2)
        total = 1.0 / (h1 + h2)
        left, right = h1 * total, h2 * total
        left_up = up(left)
        right_up = up(right)
        s0_next = ahead(4)
        n0_next = ahead(5)
        side_a = side_a + jnp.where(first_lane, wall_a, behind(h2))
        side_c = side_c + jnp.where(first_lane, c0 + c1, behind(g2))
        side_b = side_b + h2
        side_d = side_d + g2

        nc = n0 * side_c
        sc = s0 * side_c
        nd = n1 * side_d
        sd = s1 * side_d
        even = side_a + t0 + s0 * sc + jnp.where(bottom, wall_a, down(t0 + n0 * nc))
        odd_ = side_b + t1 + s1 * sd + jnp.where(bottom, wall_b, down(t1 + n1 * nd))
        even_up = s0 * nc - t0
        odd_up = s1 * nd - t1
        sg = s0 * g1
        ng = n0 * g1
        sq = s0_next * g2
        nq = n0_next * g2
        p = h1 + s1 * sg + jnp.where(bottom, 0.0, down(n1 * ng))
        q = h2 + s1 * sq + jnp.where(bottom, 0.0, down(n1 * nq))
        p_up = n1 * sg
        p_down = s1 * ng
        q_up = s1 * nq
        q_down = n1 * sq

        mid = left * odd_ - p
        east = jnp.where(last, 0.0, right * mid - left * q)
        centre = even + left * (mid - p) + behind(right * (right * odd_ - 2.0 * q))
        lo = left * odd_up - p_up
        ro = right * odd_up - q_down
        north = even_up + left_up * lo - left * p_down + behind(right_up * ro - right * q_up)
        north = jnp.where(top, 0.0, north)
        north_east = jnp.where(last | top, 0.0, right_up * lo - left * q_up)
        north_west = jnp.where(last | top, 0.0, left_up * ro - right * p_down)
        west = behind(east)
        ne_back = behind(north_east)
        nw_back = behind(north_west)

        def below(x):
            return jnp.where(bottom, 0.0, down(x))

        values = (below(ne_back), below(north), below(north_west), west, centre, east, nw_back, north, north_east)
        return tuple(value[:half] for value in values), tuple(rolled)

    def carry_into(t):
        carry = step(jnp.maximum(t - 1, 0), (jnp.zeros((rows, LANES), jnp.float32),) * 7)[1]
        return tuple(jnp.where(t > 0, x, 0.0) for x in carry)

    return step, carry_into


def stencil_kernel(n, m, half, per_block, fields, held, carried, out, late, stored):
    tiles = fields.shape[0] - 1
    count = last_count(per_block)
    i = lax.axis_index("gx")
    low = chosen(i, [last_low(n, at, per_block) for at in range(n)])
    tile_stencil, _ = stencil_stage(n, m, half, fields)

    def columns(t, width):
        return pl.ds(pl.multiple_of(t * LANES, LANES), width * LANES)

    for q in range(tiles - count):
        cols = columns(jnp.where(q < low, q, q + count), 1)
        pltpu.make_async_copy(held.at[:, :, cols], out.at[:, :, cols], stored.at[0]).start()

    carry = tuple(carried[at] for at in range(7))
    for q in range(count):
        values, carry = tile_stencil(low + q, carry)
        for at, value in enumerate(values):
            late[at, :, q * LANES : (q + 1) * LANES] = value
    pltpu.make_async_copy(late, out.at[:, :, columns(low, count)], stored.at[0]).start()
    pltpu.make_async_copy(held, out, stored.at[0]).wait()


def shards(n, m, conductivity):
    planes, local_rows, local_cols = conductivity.shape
    band = local_rows // n
    half = band // 2
    rows = -(-(half + 2) // 8) * 8
    tiles = n * local_cols // (2 * LANES)
    vmem = pl.BlockSpec(memory_space=pltpu.VMEM)
    anywhere = pl.BlockSpec(memory_space=pl.ANY)
    dma = pltpu.SemaphoreType.DMA
    shape = (tiles + 1, 20, rows, LANES)
    per_block = local_cols // (2 * LANES)
    result = jax.ShapeDtypeStruct((9, half, tiles * LANES), jnp.float32)
    fields, held, carried = pl.pallas_call(
        functools.partial(coarse_kernel, n, m),
        out_shape=(
            jax.ShapeDtypeStruct(shape, jnp.float32),
            result,
            jax.ShapeDtypeStruct((7, rows, LANES), jnp.float32),
        ),
        in_specs=[anywhere],
        out_specs=(vmem, vmem, vmem),
        scratch_shapes=[
            pltpu.VMEM((n, 2 * band + 8, local_cols), jnp.bfloat16),
            pltpu.VMEM((2, n - 1, planes, 8, local_cols), jnp.bfloat16),
            pltpu.VMEM((planes, 8, local_cols), jnp.bfloat16),
            pltpu.VMEM((planes, 8, local_cols), jnp.bfloat16),
            pltpu.VMEM((n, 8, local_cols), jnp.bfloat16),
            dma((n, PIECES)),
            dma((1,)),
            dma((2,)),
            dma((2,)),
            pltpu.SemaphoreType.REGULAR((n,)),
            dma((2,)),
        ],
        compiler_params=pltpu.CompilerParams(
            collective_id=0, has_side_effects=True, vmem_limit_bytes=VMEM_LIMIT
        ),
        name="coarse",
    )(pltpu.with_memory_space_constraint(conductivity, pltpu.HBM))
    stencil = pl.pallas_call(
        functools.partial(stencil_kernel, n, m, half, per_block),
        out_shape=result,
        in_specs=[vmem, vmem, vmem],
        out_specs=anywhere,
        scratch_shapes=[pltpu.VMEM((9, half, last_count(per_block) * LANES), jnp.float32), dma((1,))],
        compiler_params=pltpu.CompilerParams(vmem_limit_bytes=VMEM_LIMIT),
        name="stencil",
    )(fields, held, carried)
    return stencil[:, None]


def solution(mesh):
    n, m = mesh.shape["gx"], mesh.shape["gy"]
    return jax.shard_map(
        functools.partial(shards, n, m),
        mesh=mesh,
        in_specs=(P(None, "gy", "gx"),),
        out_specs=P(None, "gy", "gx", None),
        check_vma=False,
    )
```

```python
import functools

import jax
import jax.numpy as jnp
from jax import lax
from jax.experimental import pallas as pl
from jax.experimental.pallas import tpu as pltpu
from jax.sharding import PartitionSpec as P

MESH = pl.DeviceIdType.MESH
LANES = 128
LAST = 3
VMEM_LIMIT = 16 * 1024 * 1024


def arrivals(n, i):
    half = n // 2
    if i < half:
        return list(range(i)) + list(range(n - 1, half, -1)) + list(range(i + 1, half)) + [half]
    return list(range(half, i)) + list(range(half - 1)) + list(range(i + 1, n)) + [half - 1]


def last_block(n, i):
    return arrivals(n, i)[-1]


def spans(n, i, per_block):
    tiles = n * per_block
    there, found = set(), []
    for k in [i] + arrivals(n, i)[:-1]:
        new = set(range(k * per_block, (k + 1) * per_block))
        there |= new
        ready = [
            t for t in range(tiles)
            if {max(t - 1, 0), t, min(t + 1, tiles - 1)} <= there and {t - 1, t, t + 1} & new
        ]
        found.append((ready[0], ready[-1] + 1) if ready else (0, 0))
    return found


def chosen(i, values):
    picked = values[-1]
    for at in range(len(values) - 2, -1, -1):
        picked = jnp.where(i == at, values[at], picked)
    return picked


def coarse_kernel(
    n, m, cells, fields, held, carried, blocks, rims, south_in, north_in, pack,
    arrived, around, piece, sent, edge_sent, edge_arrived, known, own,
):
    i = lax.axis_index("gx")
    j = lax.axis_index("gy")
    block = cells.shape[2]
    band = cells.shape[1] // n
    half = n // 2
    per_block = block // (2 * LANES)
    has_left, has_right = i > 0, i < n - 1
    has_south, has_north = j > 0, j < m - 1
    before, after = jnp.maximum(j - 1, 0), jnp.minimum(j + 1, m - 1)

    def signal(sem, x, y):
        pl.semaphore_signal(sem, inc=1, device_id=(x, y), device_id_type=MESH)

    barrier = pltpu.get_barrier_semaphore()
    for t in range(1, n):
        @pl.when(i < t)
        def _():
            signal(barrier, t, j)

    @pl.when(has_north)
    def _():
        signal(barrier, i, after)

    first_of_all = (i == 0) & (j == 0)

    @pl.when((i == 0) & (j == 1))
    def _():
        signal(barrier, 0, 0)

    def rows_of(t):
        return pl.ds(pl.multiple_of(t * band, band), band)

    loads = []
    for t in range(n - 1):
        loads.append(pltpu.make_async_copy(cells.at[:, pl.ds((t + 1) * band - 8, 8), :], rims.at[0, t], own.at[0]))
        loads.append(pltpu.make_async_copy(cells.at[:, pl.ds((t + 1) * band, 8), :], rims.at[1, t], own.at[0]))
    for plane in range(2):
        loads.append(pltpu.make_async_copy(cells.at[plane, rows_of(i), :], blocks.at[i, pl.ds(plane * band, band), :], own.at[1]))
    for load in loads:
        load.start()

    @pl.when(jnp.logical_not(has_south))
    def _():
        south_in[...] = jnp.ones(south_in.shape, south_in.dtype)

    @pl.when(jnp.logical_not(has_north))
    def _():
        north_in[...] = jnp.ones(north_in.shape, north_in.dtype)

    def remote(src, dst, send, recv, x, y):
        return pltpu.make_async_remote_copy(
            src_ref=src, dst_ref=dst, send_sem=send, recv_sem=recv, device_id=(x, y), device_id_type=MESH
        )

    def cols_of(p):
        return pl.ds(p * 2 * LANES, 2 * LANES)

    def send_rows(t):
        last = i == chosen(t, [last_block(n, at) for at in range(n)])
        for plane in range(2):
            rows = pl.ds(plane * band, band)

            @pl.when(jnp.logical_not(last))
            def _():
                remote(cells.at[plane, rows_of(t), :], blocks.at[i, rows, :], sent.at[0], arrived.at[i], t, j).start()

        @pl.when(last)
        def _():
            for p in range(per_block):
                for plane in range(2):
                    rows = pl.ds(plane * band, band)
                    remote(
                        cells.at[plane, rows_of(t), cols_of(p)], blocks.at[i, rows, cols_of(p)],
                        sent.at[0], piece.at[p], t, j,
                    ).start()

    def send_halo(t):
        def part(start, size, sem):
            remote(
                pack.at[t, pl.ds(start, size), :], blocks.at[i, pl.ds(2 * band + start, size), :],
                sem, around.at[i], t, j,
            ).start()

        slim = ((i < half) != (t < half)) & (lax.rem(t, half) != 0)

        @pl.when(slim)
        def _():
            part(4, 2, sent.at[2])

        @pl.when(jnp.logical_not(slim))
        def _():
            part(0, 6, sent.at[1])

    passes_on = lax.rem(i, half) != half - 1

    def pass_on(k):
        @pl.when(passes_on & ((i < half) != (k < half)))
        def _():
            for plane in range(2):
                remote(
                    blocks.at[k, pl.ds(plane * band + band - 2, 2), :], blocks.at[k, pl.ds(2 * band + 2 * plane, 2), :],
                    sent.at[3], around.at[k], jnp.minimum(i + 1, n - 1), j,
                ).start()

    def to_north():
        return remote(cells.at[:, pl.ds(n * band - 8, 8), :], south_in, edge_sent.at[0], edge_arrived.at[0], i, after)

    def to_south():
        return remote(cells.at[:, pl.ds(0, 8), :], north_in, edge_sent.at[1], edge_arrived.at[1], i, before)

    sub = lax.broadcasted_iota(jnp.int32, (8, block), 0)

    def make_pack(t, under, over):
        low = [pltpu.roll(under[p].astype(jnp.float32), 2 + 2 * p, 0) for p in range(2)]
        high = [pltpu.roll(over[p].astype(jnp.float32), 4 + p, 0) for p in range(2)]
        rows = jnp.where(sub < 2, low[0], jnp.where(sub < 4, low[1], jnp.where(sub == 4, high[0], high[1])))
        pack[t] = rows.astype(jnp.bfloat16)

    pl.semaphore_wait(barrier, i + jnp.where(has_south | first_of_all, 1, 0))

    @pl.when(has_left)
    def _():
        send_rows(0)

    for t in range(n - 2, -1, -1):
        @pl.when(i > t)
        def _():
            signal(known.at[i], t, j)

    @pl.when(has_south)
    def _():
        signal(known.at[0], i, before)
        to_south().start()

    pltpu.make_async_copy(rims, rims, own.at[0]).wait()
    for t in range(1, n - 1):
        make_pack(t, rims.at[0, t - 1], rims.at[1, t])

    @pl.when(has_right)
    def _():
        pl.semaphore_wait(known.at[i + 1], 1)

    @pl.when(i + 1 < n - 1)
    def _():
        send_halo(i + 1)

    @pl.when(has_right)
    def _():
        send_rows(i + 1)

    @pl.when(has_north)
    def _():
        pl.semaphore_wait(known.at[0], 1)
        to_north().start()

    @pl.when(has_south)
    def _():
        to_north().wait_recv()

    @pl.when(has_north)
    def _():
        to_south().wait_recv()

    make_pack(0, south_in, rims.at[1, 0])
    make_pack(n - 1, rims.at[0, n - 2], north_in)

    @pl.when(i + 1 == n - 1)
    def _():
        send_halo(n - 1)

    @pl.when(has_left)
    def _():
        send_halo(0)

    for t in range(n - 2, 0, -1):
        @pl.when(i > t)
        def _():
            send_halo(t)
            send_rows(t)

    for t in range(2, n):
        @pl.when(i + 1 < t)
        def _():
            pl.semaphore_wait(known.at[t], 1)
            send_halo(t)
            send_rows(t)

    blocks[i, pl.ds(2 * band, 8), :] = pack[i]

    first = arrival_stage(n, m, band, blocks, fields)
    tile_stencil, carry_into = stencil_stage(n, m, band // 2, fields)
    ranges = [spans(n, at, per_block) for at in range(n)]

    def second(step):
        low, end = (chosen(i, [found[step][side] for found in ranges]) for side in range(2))

        def one(t, carry):
            values, carry = tile_stencil(t, carry)
            hold(t, values)
            return carry

        lax.fori_loop(low, end, one, carry_into(low))

    def hold(t, values):
        cols = pl.ds(pl.multiple_of(t * LANES, LANES), LANES)
        for at, value in enumerate(values):
            held[at, :, cols] = value

    def landed(ref, sem, k):
        remote(ref, ref, sent.at[0], sem, k, j).wait_recv()

    mine = blocks.at[i, pl.ds(0, 2 * band), :]
    pltpu.make_async_copy(mine, mine, own.at[1]).wait()
    first(i, 0, per_block)
    second(0)
    orders = [arrivals(n, at) for at in range(n)]
    for step in range(n - 2):
        k = chosen(i, [order[step] for order in orders])
        landed(blocks.at[k, pl.ds(0, 2 * band), :], arrived.at[k], k)
        pass_on(k)
        landed(blocks.at[k, pl.ds(2 * band, 6), :], around.at[k], k)
        first(k, 0, per_block)
        second(step + 1)
    k = chosen(i, [order[n - 2] for order in orders])
    low = k * per_block - 1
    carry = carry_into(low)
    landed(blocks.at[k, pl.ds(2 * band, 6), :], around.at[k], k)
    for p in range(per_block):
        if p == per_block - 1:
            for at, value in enumerate(carry):
                carried[at] = value
        landed(blocks.at[k, pl.ds(0, 2 * band), cols_of(p)], piece.at[p], k)
        if p == per_block - 1:
            pass_on(k)
        first(k, p, 1)
        if p < per_block - 1:
            values, carry = tile_stencil(low + p, carry)
            hold(low + p, values)

    def drained(ref, sem):
        remote(ref, ref, sem, arrived.at[0], i, j).wait_send()

    drained(blocks.at[pl.ds(0, n - 1), pl.ds(0, 2 * band), :], sent.at[0])
    drained(blocks.at[pl.ds(0, half), pl.ds(2 * band, 6), :], sent.at[1])
    drained(blocks.at[pl.ds(0, half - 1), pl.ds(2 * band, 2), :], sent.at[2])

    @pl.when(passes_on)
    def _():
        drained(blocks.at[pl.ds(0, half), pl.ds(2 * band, 4), :], sent.at[3])

    @pl.when(has_north)
    def _():
        to_north().wait_send()

    @pl.when(has_south)
    def _():
        to_south().wait_send()


def parts(x0, y0, x1, y1):
    s0, s1 = x0 + y0, x1 + y1
    return x0 * y0 * s1 + x1 * y1 * s0, s0 * s1


def two_faces(one, two):
    scale = 2.0 / (one[1] * two[1])
    return one[0] * two[1] * scale, two[0] * one[1] * scale


def middle(one, two):
    x, y = one[0] * two[1], two[0] * one[1]
    total = 1.0 / (x + y)
    return x * total, y * total, 2.0 * (one[0] * two[0]) * total


def verticals(pairs):
    sums = [x + y for x, y in pairs]
    low, high = sums[0] * sums[1], sums[2] * sums[3]
    scale = 4.0 / (low * high)
    low, high = high * scale, low * scale
    shares = (sums[1] * low, sums[0] * low, sums[3] * high, sums[2] * high)
    return [x * y * share for (x, y), share in zip(pairs, shares)]


def arrival_stage(n, m, band, blocks, fields):
    block = blocks.shape[2]
    half = band // 2
    rows = fields.shape[2]
    tiles = fields.shape[0] - 1
    per_block = block // (2 * LANES)
    i = lax.axis_index("gx")
    j = lax.axis_index("gy")
    last_rows = (i == n - 1) & (j == m - 1)

    taken = 2 * band + 6
    want = lax.broadcasted_iota(jnp.int32, (4 * rows, taken), 0)
    have = lax.broadcasted_iota(jnp.int32, (4 * rows, taken), 1)
    group = jnp.where(want >= 3 * rows, 3, jnp.where(want >= 2 * rows, 2, jnp.where(want >= rows, 1, 0)))
    place = want - group * rows
    plane = jnp.where(group >= 2, 1, 0)
    odd = group - 2 * plane
    inside = plane * band + 2 * jnp.where(place < half, place, 0) + odd
    above = jnp.where(odd == 0, 2 * band + 4 + plane, plane * band + 1)
    below = 2 * band + 2 * plane + odd
    source = jnp.where(place == half, above, jnp.where(place == rows - 1, below, inside))
    pick_rows = jnp.where(have == source, 1.0, 0.0).astype(jnp.bfloat16)
    fine = lax.broadcasted_iota(jnp.int32, (2 * LANES, 2 * LANES), 0)
    to = lax.broadcasted_iota(jnp.int32, (2 * LANES, 2 * LANES), 1)
    pick_cols = jnp.where(fine == jnp.where(to < LANES, 2 * to, 2 * (to - LANES) + 1), 1.0, 0.0).astype(jnp.bfloat16)

    top = (lax.broadcasted_iota(jnp.int32, (rows, LANES), 0) == half - 1) & last_rows

    def up(x):
        return pltpu.roll(x, rows - 1, 0)

    def tile_terms(k, part):
        t = k * per_block + part
        cols = pl.ds(part * 2 * LANES, 2 * LANES)
        stored = blocks[k, pl.ds(0, taken), cols]
        picked = jnp.dot(pick_rows, stored, preferred_element_type=jnp.float32).astype(jnp.bfloat16)
        split = jnp.dot(picked, pick_cols, preferred_element_type=jnp.float32)
        a0, c0, a1, c1 = (split[g * rows : (g + 1) * rows, :LANES] for g in range(4))
        b0, d0, b1, d1 = (split[g * rows : (g + 1) * rows, LANES:] for g in range(4))
        def wall(x0, x1, inner):
            return jnp.where(top, 0.5 * (x0 + x1), inner[0]), jnp.where(top, 1.0, inner[1])

        s0, n0, t0 = middle(parts(a0, c0, a1, c1), wall(c0, c1, parts(c0, up(a0), c1, up(a1))))
        s1, n1, t1 = middle(parts(b0, d0, b1, d1), wall(d0, d1, parts(d0, up(b0), d1, up(b1))))
        h1, g1 = two_faces(parts(a0, b0, a1, b1), parts(c0, d0, c1, d1))
        pairs = ((a0, a1), (b0, b1), (c0, c1), (d0, d1))
        side_a, side_b, side_c, side_d = (
            (x + ((k0 + k1) + v)) - v for x, (k0, k1), v in zip((h1, h1, g1, g1), pairs, verticals(pairs))
        )
        for at, value in enumerate(
            (a0, a1, c0, c1, s0, n0, b0, b1, d0, d1, t0, s1, n1, t1, h1, g1, side_a, side_b, side_c, side_d)
        ):
            fields[t, at] = value

    def first(k, start, count):
        for part in range(start, start + count):
            tile_terms(k, part)

    ones = jnp.ones((rows, LANES), jnp.float32)
    for at in range(6):
        fields[tiles, at] = ones

    return first


def stencil_stage(n, m, half, fields):
    rows = fields.shape[2]
    tiles = fields.shape[0] - 1
    i = lax.axis_index("gx")
    j = lax.axis_index("gy")
    lane = lax.broadcasted_iota(jnp.int32, (rows, LANES), 1)
    sub = lax.broadcasted_iota(jnp.int32, (rows, LANES), 0)
    bottom = (sub == 0) & (i == 0) & (j == 0)
    top = (sub == half - 1) & (i == n - 1) & (j == m - 1)

    def up(x):
        return pltpu.roll(x, rows - 1, 0)

    def down(x):
        return pltpu.roll(x, 1, 0)

    def step(t, carry):
        last = (lane == LANES - 1) & (t == tiles - 1)
        first_lane = (lane == 0) & (t == 0)

        def ahead(at):
            return pltpu.roll(jnp.where(lane == 0, fields[t + 1, at], fields[t, at]), LANES - 1, 1)

        rolled = []

        def behind(x):
            turned = pltpu.roll(x, 1, 1)
            before = carry[len(rolled)]
            rolled.append(turned)
            return jnp.where(lane == 0, before, turned)

        a0, a1, c0, c1, s0, n0, b0, b1, d0, d1 = (fields[t, at] for at in range(10))
        t0, s1, n1, t1, h1, g1, side_a, side_b, side_c, side_d = (fields[t, at] for at in range(10, 20))
        wall_a, wall_b = a0 + a1, b0 + b1
        h2, g2 = two_faces(parts(b0, ahead(0), b1, ahead(1)), parts(d0, ahead(2), d1, ahead(3)))
        h2 = jnp.where(last, wall_b, h2)
        g2 = jnp.where(last, d0 + d1, g2)
        total = 1.0 / (h1 + h2)
        left, right = h1 * total, h2 * total
        left_up = up(left)
        right_up = up(right)
        s0_next = ahead(4)
        n0_next = ahead(5)
        side_a = side_a + jnp.where(first_lane, wall_a, behind(h2))
        side_c = side_c + jnp.where(first_lane, c0 + c1, behind(g2))
        side_b = side_b + h2
        side_d = side_d + g2

        nc = n0 * side_c
        sc = s0 * side_c
        nd = n1 * side_d
        sd = s1 * side_d
        even = side_a + t0 + s0 * sc + jnp.where(bottom, wall_a, down(t0 + n0 * nc))
        odd_ = side_b + t1 + s1 * sd + jnp.where(bottom, wall_b, down(t1 + n1 * nd))
        even_up = s0 * nc - t0
        odd_up = s1 * nd - t1
        sg = s0 * g1
        ng = n0 * g1
        sq = s0_next * g2
        nq = n0_next * g2
        p = h1 + s1 * sg + jnp.where(bottom, 0.0, down(n1 * ng))
        q = h2 + s1 * sq + jnp.where(bottom, 0.0, down(n1 * nq))
        p_up = n1 * sg
        p_down = s1 * ng
        q_up = s1 * nq
        q_down = n1 * sq

        mid = left * odd_ - p
        east = jnp.where(last, 0.0, right * mid - left * q)
        centre = even + left * (mid - p) + behind(right * (right * odd_ - 2.0 * q))
        lo = left * odd_up - p_up
        ro = right * odd_up - q_down
        north = even_up + left_up * lo - left * p_down + behind(right_up * ro - right * q_up)
        north = jnp.where(top, 0.0, north)
        north_east = jnp.where(last | top, 0.0, right_up * lo - left * q_up)
        north_west = jnp.where(last | top, 0.0, left_up * ro - right * p_down)
        west = behind(east)
        ne_back = behind(north_east)
        nw_back = behind(north_west)

        def below(x):
            return jnp.where(bottom, 0.0, down(x))

        values = (below(ne_back), below(north), below(north_west), west, centre, east, nw_back, north, north_east)
        return tuple(value[:half] for value in values), tuple(rolled)

    def carry_into(t):
        carry = step(jnp.maximum(t - 1, 0), (jnp.zeros((rows, LANES), jnp.float32),) * 7)[1]
        return tuple(jnp.where(t > 0, x, 0.0) for x in carry)

    return step, carry_into


def stencil_kernel(n, m, half, per_block, fields, held, carried, out, late, stored):
    tiles = fields.shape[0] - 1
    i = lax.axis_index("gx")
    low = (chosen(i, [last_block(n, at) for at in range(n)]) + 1) * per_block - 2
    count = LAST
    tile_stencil, _ = stencil_stage(n, m, half, fields)

    def columns(t, width):
        return pl.ds(pl.multiple_of(t * LANES, LANES), width * LANES)

    for q in range(tiles - count):
        cols = columns(jnp.where(q < low, q, q + count), 1)
        pltpu.make_async_copy(held.at[:, :, cols], out.at[:, :, cols], stored.at[0]).start()

    carry = tuple(carried[at] for at in range(7))
    for q in range(count):
        values, carry = tile_stencil(low + q, carry)
        for at, value in enumerate(values):
            late[at, :, q * LANES : (q + 1) * LANES] = value
    pltpu.make_async_copy(late, out.at[:, :, columns(low, count)], stored.at[0]).start()
    pltpu.make_async_copy(held, out, stored.at[0]).wait()


def shards(n, m, conductivity):
    planes, local_rows, local_cols = conductivity.shape
    band = local_rows // n
    half = band // 2
    rows = -(-(half + 2) // 8) * 8
    tiles = n * local_cols // (2 * LANES)
    vmem = pl.BlockSpec(memory_space=pltpu.VMEM)
    anywhere = pl.BlockSpec(memory_space=pl.ANY)
    dma = pltpu.SemaphoreType.DMA
    shape = (tiles + 1, 20, rows, LANES)
    per_block = local_cols // (2 * LANES)
    result = jax.ShapeDtypeStruct((9, half, tiles * LANES), jnp.float32)
    fields, held, carried = pl.pallas_call(
        functools.partial(coarse_kernel, n, m),
        out_shape=(
            jax.ShapeDtypeStruct(shape, jnp.float32),
            result,
            jax.ShapeDtypeStruct((7, rows, LANES), jnp.float32),
        ),
        in_specs=[anywhere],
        out_specs=(vmem, vmem, vmem),
        scratch_shapes=[
            pltpu.VMEM((n, 2 * band + 8, local_cols), jnp.bfloat16),
            pltpu.VMEM((2, n - 1, planes, 8, local_cols), jnp.bfloat16),
            pltpu.VMEM((planes, 8, local_cols), jnp.bfloat16),
            pltpu.VMEM((planes, 8, local_cols), jnp.bfloat16),
            pltpu.VMEM((n, 8, local_cols), jnp.bfloat16),
            dma((n,)),
            dma((n,)),
            dma((per_block,)),
            dma((4,)),
            dma((2,)),
            dma((2,)),
            pltpu.SemaphoreType.REGULAR((n,)),
            dma((2,)),
        ],
        compiler_params=pltpu.CompilerParams(
            collective_id=0, has_side_effects=True, vmem_limit_bytes=VMEM_LIMIT
        ),
        name="coarse",
    )(pltpu.with_memory_space_constraint(conductivity, pltpu.HBM))
    stencil = pl.pallas_call(
        functools.partial(stencil_kernel, n, m, half, per_block),
        out_shape=result,
        in_specs=[vmem, vmem, vmem],
        out_specs=anywhere,
        scratch_shapes=[pltpu.VMEM((9, half, LAST * LANES), jnp.float32), dma((1,))],
        compiler_params=pltpu.CompilerParams(vmem_limit_bytes=VMEM_LIMIT),
        name="stencil",
    )(fields, held, carried)
    return stencil[:, None]


def solution(mesh):
    n, m = mesh.shape["gx"], mesh.shape["gy"]
    return jax.shard_map(
        functools.partial(shards, n, m),
        mesh=mesh,
        in_specs=(P(None, "gy", "gx"),),
        out_specs=P(None, "gy", "gx", None),
        check_vma=False,
    )
```

```python
import functools

import jax
import jax.numpy as jnp
from jax import lax
from jax.experimental import pallas as pl
from jax.experimental.pallas import tpu as pltpu
from jax.sharding import PartitionSpec as P

MESH = pl.DeviceIdType.MESH
LANES = 128
LAST = 3
VMEM_LIMIT = 16 * 1024 * 1024


def arrivals(n, i):
    half = n // 2
    if i < half:
        return list(range(i)) + list(range(n - 1, i, -1))
    return list(range(half, i)) + list(range(half - 1)) + list(range(i + 1, n)) + [half - 1]


def last_block(n, i):
    return arrivals(n, i)[-1]


def spans(n, i, per_block):
    tiles = n * per_block
    there, found = set(), []
    for k in [i] + arrivals(n, i)[:-1]:
        new = set(range(k * per_block, (k + 1) * per_block))
        there |= new
        ready = [
            t for t in range(tiles)
            if {max(t - 1, 0), t, min(t + 1, tiles - 1)} <= there and {t - 1, t, t + 1} & new
        ]
        found.append((ready[0], ready[-1] + 1) if ready else (0, 0))
    return found


def chosen(i, values):
    picked = values[-1]
    for at in range(len(values) - 2, -1, -1):
        picked = jnp.where(i == at, values[at], picked)
    return picked


def coarse_kernel(
    n, m, cells, fields, held, carried, blocks, rims, south_in, north_in, pack,
    arrived, around, piece, sent, edge_sent, edge_arrived, known, own,
):
    i = lax.axis_index("gx")
    j = lax.axis_index("gy")
    block = cells.shape[2]
    band = cells.shape[1] // n
    per_block = block // (2 * LANES)
    has_left, has_right = i > 0, i < n - 1
    has_south, has_north = j > 0, j < m - 1
    before, after = jnp.maximum(j - 1, 0), jnp.minimum(j + 1, m - 1)

    def signal(sem, x, y):
        pl.semaphore_signal(sem, inc=1, device_id=(x, y), device_id_type=MESH)

    barrier = pltpu.get_barrier_semaphore()
    for t in range(1, n):
        @pl.when(i < t)
        def _():
            signal(barrier, t, j)

    @pl.when(has_north)
    def _():
        signal(barrier, i, after)

    first_of_all = (i == 0) & (j == 0)

    @pl.when((i == 0) & (j == 1))
    def _():
        signal(barrier, 0, 0)

    def rows_of(t):
        return pl.ds(pl.multiple_of(t * band, band), band)

    loads = []
    for t in range(n - 1):
        loads.append(pltpu.make_async_copy(cells.at[:, pl.ds((t + 1) * band - 8, 8), :], rims.at[0, t], own.at[0]))
        loads.append(pltpu.make_async_copy(cells.at[:, pl.ds((t + 1) * band, 8), :], rims.at[1, t], own.at[0]))
    for plane in range(2):
        loads.append(pltpu.make_async_copy(cells.at[plane, rows_of(i), :], blocks.at[i, pl.ds(plane * band, band), :], own.at[1]))
    for load in loads:
        load.start()

    @pl.when(jnp.logical_not(has_south))
    def _():
        south_in[...] = jnp.ones(south_in.shape, south_in.dtype)

    @pl.when(jnp.logical_not(has_north))
    def _():
        north_in[...] = jnp.ones(north_in.shape, north_in.dtype)

    def remote(src, dst, send, recv, x, y):
        return pltpu.make_async_remote_copy(
            src_ref=src, dst_ref=dst, send_sem=send, recv_sem=recv, device_id=(x, y), device_id_type=MESH
        )

    def cols_of(p):
        return pl.ds(p * 2 * LANES, 2 * LANES)

    def send_rows(t):
        last = i == chosen(t, [last_block(n, at) for at in range(n)])
        for plane in range(2):
            rows = pl.ds(plane * band, band)

            @pl.when(jnp.logical_not(last))
            def _():
                remote(cells.at[plane, rows_of(t), :], blocks.at[i, rows, :], sent.at[0], arrived.at[i], t, j).start()

        @pl.when(last)
        def _():
            for p in range(per_block):
                for plane in range(2):
                    rows = pl.ds(plane * band, band)
                    remote(
                        cells.at[plane, rows_of(t), cols_of(p)], blocks.at[i, rows, cols_of(p)],
                        sent.at[0], piece.at[p], t, j,
                    ).start()

    def send_halo(t):
        rows = pl.ds(2 * band, 6)
        remote(pack.at[t, pl.ds(0, 6), :], blocks.at[i, rows, :], sent.at[1], around.at[i], t, j).start()

    def to_north():
        return remote(cells.at[:, pl.ds(n * band - 8, 8), :], south_in, edge_sent.at[0], edge_arrived.at[0], i, after)

    def to_south():
        return remote(cells.at[:, pl.ds(0, 8), :], north_in, edge_sent.at[1], edge_arrived.at[1], i, before)

    sub = lax.broadcasted_iota(jnp.int32, (8, block), 0)

    def make_pack(t, under, over):
        low = [pltpu.roll(under[p].astype(jnp.float32), 2 + 2 * p, 0) for p in range(2)]
        high = [pltpu.roll(over[p].astype(jnp.float32), 4 + p, 0) for p in range(2)]
        rows = jnp.where(sub < 2, low[0], jnp.where(sub < 4, low[1], jnp.where(sub == 4, high[0], high[1])))
        pack[t] = rows.astype(jnp.bfloat16)

    pl.semaphore_wait(barrier, i + jnp.where(has_south | first_of_all, 1, 0))

    @pl.when(has_left)
    def _():
        send_rows(0)

    for t in range(n - 2, -1, -1):
        @pl.when(i > t)
        def _():
            signal(known.at[i], t, j)

    @pl.when(has_south)
    def _():
        signal(known.at[0], i, before)
        to_south().start()

    pltpu.make_async_copy(rims, rims, own.at[0]).wait()
    for t in range(1, n - 1):
        make_pack(t, rims.at[0, t - 1], rims.at[1, t])

    @pl.when(has_right)
    def _():
        pl.semaphore_wait(known.at[i + 1], 1)

    @pl.when(i + 1 < n - 1)
    def _():
        send_halo(i + 1)

    @pl.when(has_right)
    def _():
        send_rows(i + 1)

    @pl.when(has_north)
    def _():
        pl.semaphore_wait(known.at[0], 1)
        to_north().start()

    @pl.when(has_south)
    def _():
        to_north().wait_recv()

    @pl.when(has_north)
    def _():
        to_south().wait_recv()

    make_pack(0, south_in, rims.at[1, 0])
    make_pack(n - 1, rims.at[0, n - 2], north_in)

    @pl.when(i + 1 == n - 1)
    def _():
        send_halo(n - 1)

    @pl.when(has_left)
    def _():
        send_halo(0)

    for t in range(n - 2, 0, -1):
        @pl.when(i > t)
        def _():
            send_halo(t)
            send_rows(t)

    for t in range(2, n):
        @pl.when(i + 1 < t)
        def _():
            pl.semaphore_wait(known.at[t], 1)
            send_halo(t)
            send_rows(t)

    blocks[i, pl.ds(2 * band, 8), :] = pack[i]

    tile_terms, first = arrival_stage(n, m, band, blocks, fields)
    tile_stencil, carry_into = stencil_stage(n, m, band // 2, fields)
    ranges = [spans(n, at, per_block) for at in range(n)]

    def second(step):
        low, end = (chosen(i, [found[step][side] for found in ranges]) for side in range(2))

        def one(t, carry):
            values, carry = tile_stencil(t, carry)
            hold(t, values)
            return carry

        lax.fori_loop(low, end, one, carry_into(low))

    def hold(t, values):
        cols = pl.ds(pl.multiple_of(t * LANES, LANES), LANES)
        for at, value in enumerate(values):
            held[at, :, cols] = value

    def landed(ref, sem, k):
        remote(ref, ref, sent.at[0], sem, k, j).wait_recv()

    mine = blocks.at[i, pl.ds(0, 2 * band), :]
    pltpu.make_async_copy(mine, mine, own.at[1]).wait()
    first(i, 0, per_block)
    second(0)
    orders = [arrivals(n, at) for at in range(n)]
    for step in range(n - 2):
        k = chosen(i, [order[step] for order in orders])
        landed(blocks.at[k, pl.ds(0, 2 * band), :], arrived.at[k], k)
        landed(blocks.at[k, pl.ds(2 * band, 6), :], around.at[k], k)
        first(k, 0, per_block)
        second(step + 1)
    k = chosen(i, [order[n - 2] for order in orders])
    low = k * per_block - 1
    carry = carry_into(low)
    landed(blocks.at[k, pl.ds(2 * band, 6), :], around.at[k], k)
    for p in range(per_block):
        landed(blocks.at[k, pl.ds(0, 2 * band), cols_of(p)], piece.at[p], k)
        if p:
            values, carry = tile_stencil(low + p - 1, carry)
        store = tile_terms(k, p)
        if p:
            hold(low + p - 1, values)
        if p == per_block - 1:
            for at, value in enumerate(carry):
                carried[at] = value
        store()

    def drained(ref, sem):
        remote(ref, ref, sem, arrived.at[0], i, j).wait_send()

    drained(blocks.at[pl.ds(0, n - 1), pl.ds(0, 2 * band), :], sent.at[0])
    drained(blocks.at[pl.ds(0, n - 1), pl.ds(2 * band, 6), :], sent.at[1])

    @pl.when(has_north)
    def _():
        to_north().wait_send()

    @pl.when(has_south)
    def _():
        to_south().wait_send()


def parts(x0, y0, x1, y1):
    s0, s1 = x0 + y0, x1 + y1
    return x0 * y0 * s1 + x1 * y1 * s0, s0 * s1


def two_faces(one, two):
    scale = 2.0 / (one[1] * two[1])
    return one[0] * two[1] * scale, two[0] * one[1] * scale


def middle(one, two):
    x, y = one[0] * two[1], two[0] * one[1]
    total = 1.0 / (x + y)
    return x * total, y * total, 2.0 * (one[0] * two[0]) * total


def verticals(pairs):
    sums = [x + y for x, y in pairs]
    low, high = sums[0] * sums[1], sums[2] * sums[3]
    scale = 4.0 / (low * high)
    low, high = high * scale, low * scale
    shares = (sums[1] * low, sums[0] * low, sums[3] * high, sums[2] * high)
    return [x * y * share for (x, y), share in zip(pairs, shares)]


def arrival_stage(n, m, band, blocks, fields):
    block = blocks.shape[2]
    half = band // 2
    rows = fields.shape[2]
    tiles = fields.shape[0] - 1
    per_block = block // (2 * LANES)
    i = lax.axis_index("gx")
    j = lax.axis_index("gy")
    last_rows = (i == n - 1) & (j == m - 1)

    taken = 2 * band + 6
    want = lax.broadcasted_iota(jnp.int32, (4 * rows, taken), 0)
    have = lax.broadcasted_iota(jnp.int32, (4 * rows, taken), 1)
    group = jnp.where(want >= 3 * rows, 3, jnp.where(want >= 2 * rows, 2, jnp.where(want >= rows, 1, 0)))
    place = want - group * rows
    plane = jnp.where(group >= 2, 1, 0)
    odd = group - 2 * plane
    inside = plane * band + 2 * jnp.where(place < half, place, 0) + odd
    above = jnp.where(odd == 0, 2 * band + 4 + plane, plane * band + 1)
    below = 2 * band + 2 * plane + odd
    source = jnp.where(place == half, above, jnp.where(place == rows - 1, below, inside))
    pick_rows = jnp.where(have == source, 1.0, 0.0).astype(jnp.bfloat16)
    fine = lax.broadcasted_iota(jnp.int32, (2 * LANES, 2 * LANES), 0)
    to = lax.broadcasted_iota(jnp.int32, (2 * LANES, 2 * LANES), 1)
    pick_cols = jnp.where(fine == jnp.where(to < LANES, 2 * to, 2 * (to - LANES) + 1), 1.0, 0.0).astype(jnp.bfloat16)

    top = (lax.broadcasted_iota(jnp.int32, (rows, LANES), 0) == half - 1) & last_rows

    def up(x):
        return pltpu.roll(x, rows - 1, 0)

    def tile_terms(k, part):
        t = k * per_block + part
        cols = pl.ds(part * 2 * LANES, 2 * LANES)
        stored = blocks[k, pl.ds(0, taken), cols]
        picked = jnp.dot(pick_rows, stored, preferred_element_type=jnp.float32).astype(jnp.bfloat16)
        split = jnp.dot(picked, pick_cols, preferred_element_type=jnp.float32)
        a0, c0, a1, c1 = (split[g * rows : (g + 1) * rows, :LANES] for g in range(4))
        b0, d0, b1, d1 = (split[g * rows : (g + 1) * rows, LANES:] for g in range(4))
        def wall(x0, x1, inner):
            return jnp.where(top, 0.5 * (x0 + x1), inner[0]), jnp.where(top, 1.0, inner[1])

        s0, n0, t0 = middle(parts(a0, c0, a1, c1), wall(c0, c1, parts(c0, up(a0), c1, up(a1))))
        s1, n1, t1 = middle(parts(b0, d0, b1, d1), wall(d0, d1, parts(d0, up(b0), d1, up(b1))))
        h1, g1 = two_faces(parts(a0, b0, a1, b1), parts(c0, d0, c1, d1))
        pairs = ((a0, a1), (b0, b1), (c0, c1), (d0, d1))
        side_a, side_b, side_c, side_d = (
            (x + ((k0 + k1) + v)) - v for x, (k0, k1), v in zip((h1, h1, g1, g1), pairs, verticals(pairs))
        )
        values = (a0, a1, c0, c1, s0, n0, b0, b1, d0, d1, t0, s1, n1, t1, h1, g1, side_a, side_b, side_c, side_d)

        def store():
            for at, value in enumerate(values):
                fields[t, at] = value

        return store

    def first(k, start, count):
        for part in range(start, start + count):
            tile_terms(k, part)()

    ones = jnp.ones((rows, LANES), jnp.float32)
    for at in range(6):
        fields[tiles, at] = ones

    return tile_terms, first


def stencil_stage(n, m, half, fields):
    rows = fields.shape[2]
    tiles = fields.shape[0] - 1
    i = lax.axis_index("gx")
    j = lax.axis_index("gy")
    lane = lax.broadcasted_iota(jnp.int32, (rows, LANES), 1)
    sub = lax.broadcasted_iota(jnp.int32, (rows, LANES), 0)
    bottom = (sub == 0) & (i == 0) & (j == 0)
    top = (sub == half - 1) & (i == n - 1) & (j == m - 1)

    def up(x):
        return pltpu.roll(x, rows - 1, 0)

    def down(x):
        return pltpu.roll(x, 1, 0)

    def step(t, carry):
        last = (lane == LANES - 1) & (t == tiles - 1)
        first_lane = (lane == 0) & (t == 0)

        def ahead(at):
            return pltpu.roll(jnp.where(lane == 0, fields[t + 1, at], fields[t, at]), LANES - 1, 1)

        rolled = []

        def behind(x):
            turned = pltpu.roll(x, 1, 1)
            before = carry[len(rolled)]
            rolled.append(turned)
            return jnp.where(lane == 0, before, turned)

        a0, a1, c0, c1, s0, n0, b0, b1, d0, d1 = (fields[t, at] for at in range(10))
        t0, s1, n1, t1, h1, g1, side_a, side_b, side_c, side_d = (fields[t, at] for at in range(10, 20))
        wall_a, wall_b = a0 + a1, b0 + b1
        h2, g2 = two_faces(parts(b0, ahead(0), b1, ahead(1)), parts(d0, ahead(2), d1, ahead(3)))
        h2 = jnp.where(last, wall_b, h2)
        g2 = jnp.where(last, d0 + d1, g2)
        total = 1.0 / (h1 + h2)
        left, right = h1 * total, h2 * total
        left_up = up(left)
        right_up = up(right)
        s0_next = ahead(4)
        n0_next = ahead(5)
        side_a = side_a + jnp.where(first_lane, wall_a, behind(h2))
        side_c = side_c + jnp.where(first_lane, c0 + c1, behind(g2))
        side_b = side_b + h2
        side_d = side_d + g2

        nc = n0 * side_c
        sc = s0 * side_c
        nd = n1 * side_d
        sd = s1 * side_d
        even = side_a + t0 + s0 * sc + jnp.where(bottom, wall_a, down(t0 + n0 * nc))
        odd_ = side_b + t1 + s1 * sd + jnp.where(bottom, wall_b, down(t1 + n1 * nd))
        even_up = s0 * nc - t0
        odd_up = s1 * nd - t1
        sg = s0 * g1
        ng = n0 * g1
        sq = s0_next * g2
        nq = n0_next * g2
        p = h1 + s1 * sg + jnp.where(bottom, 0.0, down(n1 * ng))
        q = h2 + s1 * sq + jnp.where(bottom, 0.0, down(n1 * nq))
        p_up = n1 * sg
        p_down = s1 * ng
        q_up = s1 * nq
        q_down = n1 * sq

        mid = left * odd_ - p
        east = jnp.where(last, 0.0, right * mid - left * q)
        centre = even + left * (mid - p) + behind(right * (right * odd_ - 2.0 * q))
        lo = left * odd_up - p_up
        ro = right * odd_up - q_down
        north = even_up + left_up * lo - left * p_down + behind(right_up * ro - right * q_up)
        north = jnp.where(top, 0.0, north)
        north_east = jnp.where(last | top, 0.0, right_up * lo - left * q_up)
        north_west = jnp.where(last | top, 0.0, left_up * ro - right * p_down)
        west = behind(east)
        ne_back = behind(north_east)
        nw_back = behind(north_west)

        def below(x):
            return jnp.where(bottom, 0.0, down(x))

        values = (below(ne_back), below(north), below(north_west), west, centre, east, nw_back, north, north_east)
        return tuple(value[:half] for value in values), tuple(rolled)

    def carry_into(t):
        carry = step(jnp.maximum(t - 1, 0), (jnp.zeros((rows, LANES), jnp.float32),) * 7)[1]
        return tuple(jnp.where(t > 0, x, 0.0) for x in carry)

    return step, carry_into


def stencil_kernel(n, m, half, per_block, fields, held, carried, out, late, stored):
    tiles = fields.shape[0] - 1
    i = lax.axis_index("gx")
    low = (chosen(i, [last_block(n, at) for at in range(n)]) + 1) * per_block - 2
    count = LAST
    tile_stencil, _ = stencil_stage(n, m, half, fields)

    def columns(t, width):
        return pl.ds(pl.multiple_of(t * LANES, LANES), width * LANES)

    for q in range(tiles - count):
        cols = columns(jnp.where(q < low, q, q + count), 1)
        pltpu.make_async_copy(held.at[:, :, cols], out.at[:, :, cols], stored.at[0]).start()

    carry = tuple(carried[at] for at in range(7))
    for q in range(count):
        values, carry = tile_stencil(low + q, carry)
        for at, value in enumerate(values):
            late[at, :, q * LANES : (q + 1) * LANES] = value
    pltpu.make_async_copy(late, out.at[:, :, columns(low, count)], stored.at[0]).start()
    pltpu.make_async_copy(held, out, stored.at[0]).wait()


def shards(n, m, conductivity):
    planes, local_rows, local_cols = conductivity.shape
    band = local_rows // n
    half = band // 2
    rows = -(-(half + 2) // 8) * 8
    tiles = n * local_cols // (2 * LANES)
    vmem = pl.BlockSpec(memory_space=pltpu.VMEM)
    anywhere = pl.BlockSpec(memory_space=pl.ANY)
    dma = pltpu.SemaphoreType.DMA
    shape = (tiles + 1, 20, rows, LANES)
    per_block = local_cols // (2 * LANES)
    result = jax.ShapeDtypeStruct((9, half, tiles * LANES), jnp.float32)
    fields, held, carried = pl.pallas_call(
        functools.partial(coarse_kernel, n, m),
        out_shape=(
            jax.ShapeDtypeStruct(shape, jnp.float32),
            result,
            jax.ShapeDtypeStruct((7, rows, LANES), jnp.float32),
        ),
        in_specs=[anywhere],
        out_specs=(vmem, vmem, vmem),
        scratch_shapes=[
            pltpu.VMEM((n, 2 * band + 8, local_cols), jnp.bfloat16),
            pltpu.VMEM((2, n - 1, planes, 8, local_cols), jnp.bfloat16),
            pltpu.VMEM((planes, 8, local_cols), jnp.bfloat16),
            pltpu.VMEM((planes, 8, local_cols), jnp.bfloat16),
            pltpu.VMEM((n, 8, local_cols), jnp.bfloat16),
            dma((n,)),
            dma((n,)),
            dma((per_block,)),
            dma((2,)),
            dma((2,)),
            dma((2,)),
            pltpu.SemaphoreType.REGULAR((n,)),
            dma((2,)),
        ],
        compiler_params=pltpu.CompilerParams(
            collective_id=0, has_side_effects=True, vmem_limit_bytes=VMEM_LIMIT
        ),
        name="coarse",
    )(pltpu.with_memory_space_constraint(conductivity, pltpu.HBM))
    stencil = pl.pallas_call(
        functools.partial(stencil_kernel, n, m, half, per_block),
        out_shape=result,
        in_specs=[vmem, vmem, vmem],
        out_specs=anywhere,
        scratch_shapes=[pltpu.VMEM((9, half, LAST * LANES), jnp.float32), dma((1,))],
        compiler_params=pltpu.CompilerParams(vmem_limit_bytes=VMEM_LIMIT),
        name="stencil",
    )(fields, held, carried)
    return stencil[:, None]


def solution(mesh):
    n, m = mesh.shape["gx"], mesh.shape["gy"]
    return jax.shard_map(
        functools.partial(shards, n, m),
        mesh=mesh,
        in_specs=(P(None, "gy", "gx"),),
        out_specs=P(None, "gy", "gx", None),
        check_vma=False,
    )
```

```python
import functools

import jax
import jax.numpy as jnp
from jax import lax
from jax.experimental import pallas as pl
from jax.experimental.pallas import tpu as pltpu
from jax.sharding import PartitionSpec as P

MESH = pl.DeviceIdType.MESH
LANES = 128
LAST = 3
VMEM_LIMIT = 16 * 1024 * 1024


def arrivals(n, i):
    half = n // 2
    if i < half:
        return list(range(i)) + list(range(n - 1, i, -1))
    return list(range(half, i)) + list(range(half - 1)) + list(range(i + 1, n)) + [half - 1]


def last_block(n, i):
    return arrivals(n, i)[-1]


def spans(n, i, per_block):
    tiles = n * per_block
    there, found = set(), []
    for k in [i] + arrivals(n, i)[:-1]:
        new = set(range(k * per_block, (k + 1) * per_block))
        there |= new
        ready = [
            t for t in range(tiles)
            if {max(t - 1, 0), t, min(t + 1, tiles - 1)} <= there and {t - 1, t, t + 1} & new
        ]
        found.append((ready[0], ready[-1] + 1) if ready else (0, 0))
    return found


def chosen(i, values):
    picked = values[-1]
    for at in range(len(values) - 2, -1, -1):
        picked = jnp.where(i == at, values[at], picked)
    return picked


def coarse_kernel(
    n, m, cells, fields, held, carried, blocks, rims, south_in, north_in, pack,
    arrived, around, piece, sent, edge_sent, edge_arrived, known, own,
):
    i = lax.axis_index("gx")
    j = lax.axis_index("gy")
    block = cells.shape[2]
    band = cells.shape[1] // n
    half = n // 2
    per_block = block // (2 * LANES)
    has_left, has_right = i > 0, i < n - 1
    has_south, has_north = j > 0, j < m - 1
    before, after = jnp.maximum(j - 1, 0), jnp.minimum(j + 1, m - 1)

    def signal(sem, x, y):
        pl.semaphore_signal(sem, inc=1, device_id=(x, y), device_id_type=MESH)

    barrier = pltpu.get_barrier_semaphore()
    for t in range(1, n):
        @pl.when(i < t)
        def _():
            signal(barrier, t, j)

    @pl.when(has_north)
    def _():
        signal(barrier, i, after)

    @pl.when(has_left & (i <= half))
    def _():
        signal(barrier, i - 1, j)

    def rows_of(t):
        return pl.ds(pl.multiple_of(t * band, band), band)

    loads = []
    for t in range(n - 1):
        loads.append(pltpu.make_async_copy(cells.at[:, pl.ds((t + 1) * band - 8, 8), :], rims.at[0, t], own.at[0]))
        loads.append(pltpu.make_async_copy(cells.at[:, pl.ds((t + 1) * band, 8), :], rims.at[1, t], own.at[0]))
    for plane in range(2):
        loads.append(pltpu.make_async_copy(cells.at[plane, rows_of(i), :], blocks.at[i, pl.ds(plane * band, band), :], own.at[1]))
    for load in loads:
        load.start()

    @pl.when(jnp.logical_not(has_south))
    def _():
        south_in[...] = jnp.ones(south_in.shape, south_in.dtype)

    @pl.when(jnp.logical_not(has_north))
    def _():
        north_in[...] = jnp.ones(north_in.shape, north_in.dtype)

    def remote(src, dst, send, recv, x, y):
        return pltpu.make_async_remote_copy(
            src_ref=src, dst_ref=dst, send_sem=send, recv_sem=recv, device_id=(x, y), device_id_type=MESH
        )

    def cols_of(p):
        return pl.ds(p * 2 * LANES, 2 * LANES)

    def send_rows(t, planes=(0, 1)):
        last = i == chosen(t, [last_block(n, at) for at in range(n)])
        for plane in planes:
            rows = pl.ds(plane * band, band)

            @pl.when(jnp.logical_not(last))
            def _():
                remote(cells.at[plane, rows_of(t), :], blocks.at[i, rows, :], sent.at[0], arrived.at[i], t, j).start()

        @pl.when(last)
        def _():
            for p in range(per_block):
                for plane in planes:
                    rows = pl.ds(plane * band, band)
                    remote(
                        cells.at[plane, rows_of(t), cols_of(p)], blocks.at[i, rows, cols_of(p)],
                        sent.at[0], piece.at[p], t, j,
                    ).start()

    def send_halo(t):
        rows = pl.ds(2 * band, 6)
        remote(pack.at[t, pl.ds(0, 6), :], blocks.at[i, rows, :], sent.at[1], around.at[i], t, j).start()

    def to_north():
        return remote(cells.at[:, pl.ds(n * band - 8, 8), :], south_in, edge_sent.at[0], edge_arrived.at[0], i, after)

    def to_south():
        return remote(cells.at[:, pl.ds(0, 8), :], north_in, edge_sent.at[1], edge_arrived.at[1], i, before)

    sub = lax.broadcasted_iota(jnp.int32, (8, block), 0)

    def make_pack(t, under, over):
        low = [pltpu.roll(under[p].astype(jnp.float32), 2 + 2 * p, 0) for p in range(2)]
        high = [pltpu.roll(over[p].astype(jnp.float32), 4 + p, 0) for p in range(2)]
        rows = jnp.where(sub < 2, low[0], jnp.where(sub < 4, low[1], jnp.where(sub == 4, high[0], high[1])))
        pack[t] = rows.astype(jnp.bfloat16)

    pl.semaphore_wait(barrier, i + jnp.where(has_south, 1, 0) + jnp.where(i < half, 1, 0))

    @pl.when(has_left)
    def _():
        send_rows(0)

    @pl.when(i < half)
    def _():
        send_rows(i + 1)

    for t in range(n - 2, -1, -1):
        @pl.when((i > t) & ((i > t + 1) | (i > half)))
        def _():
            signal(known.at[i], t, j)

    @pl.when(has_south)
    def _():
        signal(known.at[0], i, before)
        to_south().start()

    pltpu.make_async_copy(rims, rims, own.at[0]).wait()
    for t in range(1, n - 1):
        make_pack(t, rims.at[0, t - 1], rims.at[1, t])

    @pl.when(i + 1 < n - 1)
    def _():
        send_halo(i + 1)

    @pl.when(has_right & (i >= half))
    def _():
        pl.semaphore_wait(known.at[i + 1], 1)
        send_rows(i + 1)

    @pl.when(has_north)
    def _():
        pl.semaphore_wait(known.at[0], 1)
        to_north().start()

    @pl.when(has_south)
    def _():
        to_north().wait_recv()

    @pl.when(has_north)
    def _():
        to_south().wait_recv()

    make_pack(0, south_in, rims.at[1, 0])
    make_pack(n - 1, rims.at[0, n - 2], north_in)

    @pl.when(i + 1 == n - 1)
    def _():
        send_halo(n - 1)

    @pl.when(has_left)
    def _():
        send_halo(0)

    splits = i > half

    @pl.when(splits)
    def _():
        send_rows(i - 1, (0,))

    for t in range(1, n - 1):
        @pl.when((i > t) & jnp.logical_not(splits & (i == t + 1)))
        def _():
            send_halo(t)
            send_rows(t)

    @pl.when(splits)
    def _():
        send_halo(i - 1)
        send_rows(i - 1, (1,))

    for t in range(2, n):
        @pl.when(i + 1 < t)
        def _():
            pl.semaphore_wait(known.at[t], 1)
            send_halo(t)
            send_rows(t)

    blocks[i, pl.ds(2 * band, 8), :] = pack[i]

    tile_terms, first = arrival_stage(n, m, band, blocks, fields)
    tile_stencil, carry_into = stencil_stage(n, m, band // 2, fields)
    ranges = [spans(n, at, per_block) for at in range(n)]

    def second(step):
        found = [of_device[step] for of_device in ranges]
        count = max(end - low for low, end in found)
        low = chosen(i, [min(low, n * per_block - count) for low, _ in found])
        carry = carry_into(low)
        for q in range(count):
            values, carry = tile_stencil(low + q, carry)
            hold(low + q, values)

    def hold(t, values):
        cols = pl.ds(pl.multiple_of(t * LANES, LANES), LANES)
        for at, value in enumerate(values):
            held[at, :, cols] = value

    def landed(ref, sem, k):
        remote(ref, ref, sent.at[0], sem, k, j).wait_recv()

    mine = blocks.at[i, pl.ds(0, 2 * band), :]
    pltpu.make_async_copy(mine, mine, own.at[1]).wait()
    first(i, 0, per_block)
    second(0)
    orders = [arrivals(n, at) for at in range(n)]
    for step in range(n - 2):
        k = chosen(i, [order[step] for order in orders])
        landed(blocks.at[k, pl.ds(0, 2 * band), :], arrived.at[k], k)
        landed(blocks.at[k, pl.ds(2 * band, 6), :], around.at[k], k)
        first(k, 0, per_block)
        second(step + 1)
    k = chosen(i, [order[n - 2] for order in orders])
    low = k * per_block - 1
    carry = carry_into(low)
    landed(blocks.at[k, pl.ds(2 * band, 6), :], around.at[k], k)
    done = 0
    for group in [range(per_block - 2)] + [(p,) for p in range(per_block - 2, per_block)]:
        for p in group:
            landed(blocks.at[k, pl.ds(0, 2 * band), cols_of(p)], piece.at[p], k)
        between = []
        for q in range(done, group[0]):
            values, carry = tile_stencil(low + q, carry)
            between.append((low + q, values))
        done = group[0]
        stores = [tile_terms(k, p) for p in group]
        for t, values in between:
            hold(t, values)
        if group[-1] == per_block - 1:
            for at, value in enumerate(carry):
                carried[at] = value
        for store in stores:
            store()

    def drained(ref, sem):
        remote(ref, ref, sem, arrived.at[0], i, j).wait_send()

    drained(blocks.at[pl.ds(0, n - 1), pl.ds(0, 2 * band), :], sent.at[0])
    drained(blocks.at[pl.ds(0, n - 1), pl.ds(2 * band, 6), :], sent.at[1])

    @pl.when(has_north)
    def _():
        to_north().wait_send()

    @pl.when(has_south)
    def _():
        to_south().wait_send()


def parts(x0, y0, x1, y1):
    s0, s1 = x0 + y0, x1 + y1
    return x0 * y0 * s1 + x1 * y1 * s0, s0 * s1


def two_faces(one, two):
    scale = 2.0 / (one[1] * two[1])
    return one[0] * two[1] * scale, two[0] * one[1] * scale


def middle(one, two):
    x, y = one[0] * two[1], two[0] * one[1]
    total = 1.0 / (x + y)
    return x * total, y * total, 2.0 * (one[0] * two[0]) * total


def verticals(pairs):
    sums = [x + y for x, y in pairs]
    low, high = sums[0] * sums[1], sums[2] * sums[3]
    scale = 4.0 / (low * high)
    low, high = high * scale, low * scale
    shares = (sums[1] * low, sums[0] * low, sums[3] * high, sums[2] * high)
    return [x * y * share for (x, y), share in zip(pairs, shares)]


def arrival_stage(n, m, band, blocks, fields):
    block = blocks.shape[2]
    half = band // 2
    rows = fields.shape[2]
    tiles = fields.shape[0] - 1
    per_block = block // (2 * LANES)
    i = lax.axis_index("gx")
    j = lax.axis_index("gy")
    last_rows = (i == n - 1) & (j == m - 1)

    taken = 2 * band + 6
    want = lax.broadcasted_iota(jnp.int32, (4 * rows, taken), 0)
    have = lax.broadcasted_iota(jnp.int32, (4 * rows, taken), 1)
    group = jnp.where(want >= 3 * rows, 3, jnp.where(want >= 2 * rows, 2, jnp.where(want >= rows, 1, 0)))
    place = want - group * rows
    plane = jnp.where(group >= 2, 1, 0)
    odd = group - 2 * plane
    inside = plane * band + 2 * jnp.where(place < half, place, 0) + odd
    above = jnp.where(odd == 0, 2 * band + 4 + plane, plane * band + 1)
    below = 2 * band + 2 * plane + odd
    source = jnp.where(place == half, above, jnp.where(place == rows - 1, below, inside))
    pick_rows = jnp.where(have == source, 1.0, 0.0).astype(jnp.bfloat16)
    fine = lax.broadcasted_iota(jnp.int32, (2 * LANES, 2 * LANES), 0)
    to = lax.broadcasted_iota(jnp.int32, (2 * LANES, 2 * LANES), 1)
    pick_cols = jnp.where(fine == jnp.where(to < LANES, 2 * to, 2 * (to - LANES) + 1), 1.0, 0.0).astype(jnp.bfloat16)

    top = (lax.broadcasted_iota(jnp.int32, (rows, LANES), 0) == half - 1) & last_rows

    def up(x):
        return pltpu.roll(x, rows - 1, 0)

    def tile_terms(k, part):
        t = k * per_block + part
        cols = pl.ds(part * 2 * LANES, 2 * LANES)
        stored = blocks[k, pl.ds(0, taken), cols]
        picked = jnp.dot(pick_rows, stored, preferred_element_type=jnp.float32).astype(jnp.bfloat16)
        split = jnp.dot(picked, pick_cols, preferred_element_type=jnp.float32)
        a0, c0, a1, c1 = (split[g * rows : (g + 1) * rows, :LANES] for g in range(4))
        b0, d0, b1, d1 = (split[g * rows : (g + 1) * rows, LANES:] for g in range(4))
        def wall(x0, x1, inner):
            return jnp.where(top, 0.5 * (x0 + x1), inner[0]), jnp.where(top, 1.0, inner[1])

        s0, n0, t0 = middle(parts(a0, c0, a1, c1), wall(c0, c1, parts(c0, up(a0), c1, up(a1))))
        s1, n1, t1 = middle(parts(b0, d0, b1, d1), wall(d0, d1, parts(d0, up(b0), d1, up(b1))))
        h1, g1 = two_faces(parts(a0, b0, a1, b1), parts(c0, d0, c1, d1))
        pairs = ((a0, a1), (b0, b1), (c0, c1), (d0, d1))
        side_a, side_b, side_c, side_d = (
            (x + ((k0 + k1) + v)) - v for x, (k0, k1), v in zip((h1, h1, g1, g1), pairs, verticals(pairs))
        )
        values = (a0, a1, c0, c1, s0, n0, b0, b1, d0, d1, t0, s1, n1, t1, h1, g1, side_a, side_b, side_c, side_d)

        def store():
            for at, value in enumerate(values):
                fields[t, at] = value

        return store

    def first(k, start, count):
        for part in range(start, start + count):
            tile_terms(k, part)()

    ones = jnp.ones((rows, LANES), jnp.float32)
    for at in range(6):
        fields[tiles, at] = ones

    return tile_terms, first


def stencil_stage(n, m, half, fields):
    rows = fields.shape[2]
    tiles = fields.shape[0] - 1
    i = lax.axis_index("gx")
    j = lax.axis_index("gy")
    lane = lax.broadcasted_iota(jnp.int32, (rows, LANES), 1)
    sub = lax.broadcasted_iota(jnp.int32, (rows, LANES), 0)
    bottom = (sub == 0) & (i == 0) & (j == 0)
    top = (sub == half - 1) & (i == n - 1) & (j == m - 1)

    def up(x):
        return pltpu.roll(x, rows - 1, 0)

    def down(x):
        return pltpu.roll(x, 1, 0)

    def step(t, carry):
        last = (lane == LANES - 1) & (t == tiles - 1)
        first_lane = (lane == 0) & (t == 0)

        def ahead(at):
            return pltpu.roll(jnp.where(lane == 0, fields[t + 1, at], fields[t, at]), LANES - 1, 1)

        rolled = []

        def behind(x):
            turned = pltpu.roll(x, 1, 1)
            before = carry[len(rolled)]
            rolled.append(turned)
            return jnp.where(lane == 0, before, turned)

        a0, a1, c0, c1, s0, n0, b0, b1, d0, d1 = (fields[t, at] for at in range(10))
        t0, s1, n1, t1, h1, g1, side_a, side_b, side_c, side_d = (fields[t, at] for at in range(10, 20))
        wall_a, wall_b = a0 + a1, b0 + b1
        h2, g2 = two_faces(parts(b0, ahead(0), b1, ahead(1)), parts(d0, ahead(2), d1, ahead(3)))
        h2 = jnp.where(last, wall_b, h2)
        g2 = jnp.where(last, d0 + d1, g2)
        total = 1.0 / (h1 + h2)
        left, right = h1 * total, h2 * total
        left_up = up(left)
        right_up = up(right)
        s0_next = ahead(4)
        n0_next = ahead(5)
        side_a = side_a + jnp.where(first_lane, wall_a, behind(h2))
        side_c = side_c + jnp.where(first_lane, c0 + c1, behind(g2))
        side_b = side_b + h2
        side_d = side_d + g2

        nc = n0 * side_c
        sc = s0 * side_c
        nd = n1 * side_d
        sd = s1 * side_d
        even = side_a + t0 + s0 * sc + jnp.where(bottom, wall_a, down(t0 + n0 * nc))
        odd_ = side_b + t1 + s1 * sd + jnp.where(bottom, wall_b, down(t1 + n1 * nd))
        even_up = s0 * nc - t0
        odd_up = s1 * nd - t1
        sg = s0 * g1
        ng = n0 * g1
        sq = s0_next * g2
        nq = n0_next * g2
        p = h1 + s1 * sg + jnp.where(bottom, 0.0, down(n1 * ng))
        q = h2 + s1 * sq + jnp.where(bottom, 0.0, down(n1 * nq))
        p_up = n1 * sg
        p_down = s1 * ng
        q_up = s1 * nq
        q_down = n1 * sq

        mid = left * odd_ - p
        east = jnp.where(last, 0.0, right * mid - left * q)
        centre = even + left * (mid - p) + behind(right * (right * odd_ - 2.0 * q))
        lo = left * odd_up - p_up
        ro = right * odd_up - q_down
        north = even_up + left_up * lo - left * p_down + behind(right_up * ro - right * q_up)
        north = jnp.where(top, 0.0, north)
        north_east = jnp.where(last | top, 0.0, right_up * lo - left * q_up)
        north_west = jnp.where(last | top, 0.0, left_up * ro - right * p_down)
        west = behind(east)
        ne_back = behind(north_east)
        nw_back = behind(north_west)

        def below(x):
            return jnp.where(bottom, 0.0, down(x))

        values = (below(ne_back), below(north), below(north_west), west, centre, east, nw_back, north, north_east)
        return tuple(value[:half] for value in values), tuple(rolled)

    def carry_into(t):
        carry = step(jnp.maximum(t - 1, 0), (jnp.zeros((rows, LANES), jnp.float32),) * 7)[1]
        return tuple(jnp.where(t > 0, x, 0.0) for x in carry)

    return step, carry_into


def stencil_kernel(n, m, half, per_block, fields, held, carried, out, late, stored):
    tiles = fields.shape[0] - 1
    i = lax.axis_index("gx")
    low = (chosen(i, [last_block(n, at) for at in range(n)]) + 1) * per_block - 2
    count = LAST
    tile_stencil, _ = stencil_stage(n, m, half, fields)

    def columns(t, width):
        return pl.ds(pl.multiple_of(t * LANES, LANES), width * LANES)

    for q in range(tiles - count):
        cols = columns(jnp.where(q < low, q, q + count), 1)
        pltpu.make_async_copy(held.at[:, :, cols], out.at[:, :, cols], stored.at[0]).start()

    carry = tuple(carried[at] for at in range(7))
    for q in range(count):
        values, carry = tile_stencil(low + q, carry)
        for at, value in enumerate(values):
            late[at, :, q * LANES : (q + 1) * LANES] = value
    pltpu.make_async_copy(late, out.at[:, :, columns(low, count)], stored.at[0]).start()
    pltpu.make_async_copy(held, out, stored.at[0]).wait()


def shards(n, m, conductivity):
    planes, local_rows, local_cols = conductivity.shape
    band = local_rows // n
    half = band // 2
    rows = -(-(half + 2) // 8) * 8
    tiles = n * local_cols // (2 * LANES)
    vmem = pl.BlockSpec(memory_space=pltpu.VMEM)
    anywhere = pl.BlockSpec(memory_space=pl.ANY)
    dma = pltpu.SemaphoreType.DMA
    shape = (tiles + 1, 20, rows, LANES)
    per_block = local_cols // (2 * LANES)
    result = jax.ShapeDtypeStruct((9, half, tiles * LANES), jnp.float32)
    fields, held, carried = pl.pallas_call(
        functools.partial(coarse_kernel, n, m),
        out_shape=(
            jax.ShapeDtypeStruct(shape, jnp.float32),
            result,
            jax.ShapeDtypeStruct((7, rows, LANES), jnp.float32),
        ),
        in_specs=[anywhere],
        out_specs=(vmem, vmem, vmem),
        scratch_shapes=[
            pltpu.VMEM((n, 2 * band + 8, local_cols), jnp.bfloat16),
            pltpu.VMEM((2, n - 1, planes, 8, local_cols), jnp.bfloat16),
            pltpu.VMEM((planes, 8, local_cols), jnp.bfloat16),
            pltpu.VMEM((planes, 8, local_cols), jnp.bfloat16),
            pltpu.VMEM((n, 8, local_cols), jnp.bfloat16),
            dma((n,)),
            dma((n,)),
            dma((per_block,)),
            dma((2,)),
            dma((2,)),
            dma((2,)),
            pltpu.SemaphoreType.REGULAR((n,)),
            dma((2,)),
        ],
        compiler_params=pltpu.CompilerParams(
            collective_id=0, has_side_effects=True, vmem_limit_bytes=VMEM_LIMIT
        ),
        name="coarse",
    )(pltpu.with_memory_space_constraint(conductivity, pltpu.HBM))
    stencil = pl.pallas_call(
        functools.partial(stencil_kernel, n, m, half, per_block),
        out_shape=result,
        in_specs=[vmem, vmem, vmem],
        out_specs=anywhere,
        scratch_shapes=[pltpu.VMEM((9, half, LAST * LANES), jnp.float32), dma((1,))],
        compiler_params=pltpu.CompilerParams(vmem_limit_bytes=VMEM_LIMIT),
        name="stencil",
    )(fields, held, carried)
    return stencil[:, None]


def solution(mesh):
    n, m = mesh.shape["gx"], mesh.shape["gy"]
    return jax.shard_map(
        functools.partial(shards, n, m),
        mesh=mesh,
        in_specs=(P(None, "gy", "gx"),),
        out_specs=P(None, "gy", "gx", None),
        check_vma=False,
    )
```

```python
import functools

import jax
import jax.numpy as jnp
from jax import lax
from jax.experimental import pallas as pl
from jax.experimental.pallas import tpu as pltpu
from jax.sharding import PartitionSpec as P

MESH = pl.DeviceIdType.MESH
LANES = 128
LAST = 3
VMEM_LIMIT = 16 * 1024 * 1024


def arrivals(n, i):
    half = n // 2
    if i < half:
        return list(range(i)) + list(range(n - 1, half, -1)) + list(range(i + 1, half)) + [half]
    return list(range(half, i)) + list(range(half - 1)) + list(range(i + 1, n)) + [half - 1]


def last_block(n, i):
    return arrivals(n, i)[-1]


def spans(n, i, per_block):
    tiles = n * per_block
    there, found = set(), []
    for k in [i] + arrivals(n, i)[:-1]:
        new = set(range(k * per_block, (k + 1) * per_block))
        there |= new
        ready = [
            t for t in range(tiles)
            if {max(t - 1, 0), t, min(t + 1, tiles - 1)} <= there and {t - 1, t, t + 1} & new
        ]
        found.append((ready[0], ready[-1] + 1) if ready else (0, 0))
    return found


def chosen(i, values):
    picked = values[-1]
    for at in range(len(values) - 2, -1, -1):
        picked = jnp.where(i == at, values[at], picked)
    return picked


def coarse_kernel(
    n, m, cells, fields, held, carried, blocks, rims, south_in, north_in, pack,
    arrived, around, piece, sent, edge_sent, edge_arrived, known, own,
):
    i = lax.axis_index("gx")
    j = lax.axis_index("gy")
    block = cells.shape[2]
    band = cells.shape[1] // n
    half = n // 2
    per_block = block // (2 * LANES)
    has_left, has_right = i > 0, i < n - 1
    has_south, has_north = j > 0, j < m - 1
    before, after = jnp.maximum(j - 1, 0), jnp.minimum(j + 1, m - 1)

    def signal(sem, x, y):
        pl.semaphore_signal(sem, inc=1, device_id=(x, y), device_id_type=MESH)

    barrier = pltpu.get_barrier_semaphore()

    @pl.when(has_left & (i <= half))
    def _():
        signal(barrier, i - 1, j)

    for t in range(1, n):
        @pl.when(i < t)
        def _():
            signal(barrier, t, j)

    @pl.when(has_north)
    def _():
        signal(barrier, i, after)

    def rows_of(t):
        return pl.ds(pl.multiple_of(t * band, band), band)

    loads = []
    for t in range(n - 1):
        loads.append(pltpu.make_async_copy(cells.at[:, pl.ds((t + 1) * band - 8, 8), :], rims.at[0, t], own.at[0]))
        loads.append(pltpu.make_async_copy(cells.at[:, pl.ds((t + 1) * band, 8), :], rims.at[1, t], own.at[0]))
    for plane in range(2):
        loads.append(pltpu.make_async_copy(cells.at[plane, rows_of(i), :], blocks.at[i, pl.ds(plane * band, band), :], own.at[1]))
    for load in loads:
        load.start()

    @pl.when(jnp.logical_not(has_south))
    def _():
        south_in[...] = jnp.ones(south_in.shape, south_in.dtype)

    @pl.when(jnp.logical_not(has_north))
    def _():
        north_in[...] = jnp.ones(north_in.shape, north_in.dtype)

    def remote(src, dst, send, recv, x, y):
        return pltpu.make_async_remote_copy(
            src_ref=src, dst_ref=dst, send_sem=send, recv_sem=recv, device_id=(x, y), device_id_type=MESH
        )

    def cols_of(p):
        return pl.ds(p * 2 * LANES, 2 * LANES)

    def send_rows(t, planes=(0, 1), pieces=range(per_block)):
        last = i == chosen(t, [last_block(n, at) for at in range(n)])
        for plane in planes if pieces[0] == 0 else ():
            rows = pl.ds(plane * band, band)

            @pl.when(jnp.logical_not(last))
            def _():
                remote(cells.at[plane, rows_of(t), :], blocks.at[i, rows, :], sent.at[0], arrived.at[i], t, j).start()

        @pl.when(last)
        def _():
            for p in pieces:
                for plane in planes:
                    rows = pl.ds(plane * band, band)
                    remote(
                        cells.at[plane, rows_of(t), cols_of(p)], blocks.at[i, rows, cols_of(p)],
                        sent.at[0], piece.at[p], t, j,
                    ).start()

    def send_halo(t):
        rows = pl.ds(2 * band, 6)
        remote(pack.at[t, pl.ds(0, 6), :], blocks.at[i, rows, :], sent.at[1], around.at[i], t, j).start()

    def to_north():
        return remote(cells.at[:, pl.ds(n * band - 8, 8), :], south_in, edge_sent.at[0], edge_arrived.at[0], i, after)

    def to_south():
        return remote(cells.at[:, pl.ds(0, 8), :], north_in, edge_sent.at[1], edge_arrived.at[1], i, before)

    sub = lax.broadcasted_iota(jnp.int32, (8, block), 0)

    def make_pack(t, under, over):
        low = [pltpu.roll(under[p].astype(jnp.float32), 2 + 2 * p, 0) for p in range(2)]
        high = [pltpu.roll(over[p].astype(jnp.float32), 4 + p, 0) for p in range(2)]
        rows = jnp.where(sub < 2, low[0], jnp.where(sub < 4, low[1], jnp.where(sub == 4, high[0], high[1])))
        pack[t] = rows.astype(jnp.bfloat16)

    pl.semaphore_wait(barrier, i + jnp.where(has_south, 1, 0) + jnp.where(i < half, 1, 0))

    @pl.when(has_left)
    def _():
        send_rows(0, pieces=range(per_block // 2))

    @pl.when(i < half)
    def _():
        send_rows(i + 1)

    for t in range(n - 2, -1, -1):
        @pl.when((i > t) & ((i > t + 1) | (i > half)))
        def _():
            signal(known.at[i], t, j)

    @pl.when(has_south)
    def _():
        signal(known.at[0], i, before)
        to_south().start()

    pltpu.make_async_copy(rims, rims, own.at[0]).wait()
    for t in range(1, n - 1):
        make_pack(t, rims.at[0, t - 1], rims.at[1, t])

    @pl.when(i + 1 < n - 1)
    def _():
        send_halo(i + 1)

    @pl.when(has_right & (i >= half))
    def _():
        pl.semaphore_wait(known.at[i + 1], 1)
        send_rows(i + 1)

    @pl.when(has_north)
    def _():
        pl.semaphore_wait(known.at[0], 1)
        to_north().start()

    @pl.when(has_south)
    def _():
        to_north().wait_recv()

    @pl.when(has_north)
    def _():
        to_south().wait_recv()

    make_pack(0, south_in, rims.at[1, 0])
    make_pack(n - 1, rims.at[0, n - 2], north_in)

    @pl.when(i + 1 == n - 1)
    def _():
        send_halo(n - 1)

    @pl.when(has_left)
    def _():
        send_halo(0)
        send_rows(0, pieces=range(per_block // 2, per_block))

    splits = i > half

    @pl.when(splits)
    def _():
        send_rows(i - 1, (0,))

    for t in range(1, n - 1):
        @pl.when((i > t) & jnp.logical_not(splits & (i == t + 1)))
        def _():
            send_halo(t)
            send_rows(t)

    @pl.when(splits)
    def _():
        send_halo(i - 1)
        send_rows(i - 1, (1,))

    for t in range(2, n):
        @pl.when(i + 1 < t)
        def _():
            pl.semaphore_wait(known.at[t], 1)
            send_halo(t)
            send_rows(t)

    blocks[i, pl.ds(2 * band, 8), :] = pack[i]

    tile_terms, first = arrival_stage(n, m, band, blocks, fields)
    tile_stencil, carry_into = stencil_stage(n, m, band // 2, fields)
    ranges = [spans(n, at, per_block) for at in range(n)]

    def second(step):
        found = [of_device[step] for of_device in ranges]
        count = max(end - low for low, end in found)
        low = chosen(i, [min(low, n * per_block - count) for low, _ in found])
        carry = carry_into(low)
        for q in range(count):
            values, carry = tile_stencil(low + q, carry)
            hold(low + q, values)

    def hold(t, values):
        cols = pl.ds(pl.multiple_of(t * LANES, LANES), LANES)
        for at, value in enumerate(values):
            held[at, :, cols] = value

    def landed(ref, sem, k):
        remote(ref, ref, sent.at[0], sem, k, j).wait_recv()

    mine = blocks.at[i, pl.ds(0, 2 * band), :]
    pltpu.make_async_copy(mine, mine, own.at[1]).wait()
    first(i, 0, per_block)
    second(0)
    orders = [arrivals(n, at) for at in range(n)]
    for step in range(n - 2):
        k = chosen(i, [order[step] for order in orders])
        landed(blocks.at[k, pl.ds(0, 2 * band), :], arrived.at[k], k)
        landed(blocks.at[k, pl.ds(2 * band, 6), :], around.at[k], k)
        first(k, 0, per_block)
        second(step + 1)
    k = chosen(i, [order[n - 2] for order in orders])
    low = k * per_block - 1
    carry = carry_into(low)
    landed(blocks.at[k, pl.ds(2 * band, 6), :], around.at[k], k)
    done = 0
    for group in [range(per_block - 2)] + [(p,) for p in range(per_block - 2, per_block)]:
        for p in group:
            landed(blocks.at[k, pl.ds(0, 2 * band), cols_of(p)], piece.at[p], k)
        between = []
        for q in range(done, group[0]):
            values, carry = tile_stencil(low + q, carry)
            between.append((low + q, values))
        done = group[0]
        stores = [tile_terms(k, p) for p in group]
        for t, values in between:
            hold(t, values)
        if group[-1] == per_block - 1:
            for at, value in enumerate(carry):
                carried[at] = value
        for store in stores:
            store()

    def drained(ref, sem):
        remote(ref, ref, sem, arrived.at[0], i, j).wait_send()

    drained(blocks.at[pl.ds(0, n - 1), pl.ds(0, 2 * band), :], sent.at[0])
    drained(blocks.at[pl.ds(0, n - 1), pl.ds(2 * band, 6), :], sent.at[1])

    @pl.when(has_north)
    def _():
        to_north().wait_send()

    @pl.when(has_south)
    def _():
        to_south().wait_send()


def parts(x0, y0, x1, y1):
    s0, s1 = x0 + y0, x1 + y1
    return x0 * y0 * s1 + x1 * y1 * s0, s0 * s1


def two_faces(one, two):
    scale = 2.0 / (one[1] * two[1])
    return one[0] * two[1] * scale, two[0] * one[1] * scale


def middle(one, two):
    x, y = one[0] * two[1], two[0] * one[1]
    total = 1.0 / (x + y)
    return x * total, y * total, 2.0 * (one[0] * two[0]) * total


def verticals(pairs):
    sums = [x + y for x, y in pairs]
    low, high = sums[0] * sums[1], sums[2] * sums[3]
    scale = 4.0 / (low * high)
    low, high = high * scale, low * scale
    shares = (sums[1] * low, sums[0] * low, sums[3] * high, sums[2] * high)
    return [x * y * share for (x, y), share in zip(pairs, shares)]


def arrival_stage(n, m, band, blocks, fields):
    block = blocks.shape[2]
    half = band // 2
    rows = fields.shape[2]
    tiles = fields.shape[0] - 1
    per_block = block // (2 * LANES)
    i = lax.axis_index("gx")
    j = lax.axis_index("gy")
    last_rows = (i == n - 1) & (j == m - 1)

    taken = 2 * band + 6
    want = lax.broadcasted_iota(jnp.int32, (4 * rows, taken), 0)
    have = lax.broadcasted_iota(jnp.int32, (4 * rows, taken), 1)
    group = jnp.where(want >= 3 * rows, 3, jnp.where(want >= 2 * rows, 2, jnp.where(want >= rows, 1, 0)))
    place = want - group * rows
    plane = jnp.where(group >= 2, 1, 0)
    odd = group - 2 * plane
    inside = plane * band + 2 * jnp.where(place < half, place, 0) + odd
    above = jnp.where(odd == 0, 2 * band + 4 + plane, plane * band + 1)
    below = 2 * band + 2 * plane + odd
    source = jnp.where(place == half, above, jnp.where(place == rows - 1, below, inside))
    pick_rows = jnp.where(have == source, 1.0, 0.0).astype(jnp.bfloat16)
    fine = lax.broadcasted_iota(jnp.int32, (2 * LANES, 2 * LANES), 0)
    to = lax.broadcasted_iota(jnp.int32, (2 * LANES, 2 * LANES), 1)
    pick_cols = jnp.where(fine == jnp.where(to < LANES, 2 * to, 2 * (to - LANES) + 1), 1.0, 0.0).astype(jnp.bfloat16)

    top = (lax.broadcasted_iota(jnp.int32, (rows, LANES), 0) == half - 1) & last_rows

    def up(x):
        return pltpu.roll(x, rows - 1, 0)

    def tile_terms(k, part):
        t = k * per_block + part
        cols = pl.ds(part * 2 * LANES, 2 * LANES)
        stored = blocks[k, pl.ds(0, taken), cols]
        picked = jnp.dot(pick_rows, stored, preferred_element_type=jnp.float32).astype(jnp.bfloat16)
        split = jnp.dot(picked, pick_cols, preferred_element_type=jnp.float32)
        a0, c0, a1, c1 = (split[g * rows : (g + 1) * rows, :LANES] for g in range(4))
        b0, d0, b1, d1 = (split[g * rows : (g + 1) * rows, LANES:] for g in range(4))
        def wall(x0, x1, inner):
            return jnp.where(top, 0.5 * (x0 + x1), inner[0]), jnp.where(top, 1.0, inner[1])

        s0, n0, t0 = middle(parts(a0, c0, a1, c1), wall(c0, c1, parts(c0, up(a0), c1, up(a1))))
        s1, n1, t1 = middle(parts(b0, d0, b1, d1), wall(d0, d1, parts(d0, up(b0), d1, up(b1))))
        h1, g1 = two_faces(parts(a0, b0, a1, b1), parts(c0, d0, c1, d1))
        pairs = ((a0, a1), (b0, b1), (c0, c1), (d0, d1))
        side_a, side_b, side_c, side_d = (
            (x + ((k0 + k1) + v)) - v for x, (k0, k1), v in zip((h1, h1, g1, g1), pairs, verticals(pairs))
        )
        values = (a0, a1, c0, c1, s0, n0, b0, b1, d0, d1, t0, s1, n1, t1, h1, g1, side_a, side_b, side_c, side_d)

        def store():
            for at, value in enumerate(values):
                fields[t, at] = value

        return store

    def first(k, start, count):
        for part in range(start, start + count):
            tile_terms(k, part)()

    ones = jnp.ones((rows, LANES), jnp.float32)
    for at in range(6):
        fields[tiles, at] = ones

    return tile_terms, first


def stencil_stage(n, m, half, fields):
    rows = fields.shape[2]
    tiles = fields.shape[0] - 1
    i = lax.axis_index("gx")
    j = lax.axis_index("gy")
    lane = lax.broadcasted_iota(jnp.int32, (rows, LANES), 1)
    sub = lax.broadcasted_iota(jnp.int32, (rows, LANES), 0)
    bottom = (sub == 0) & (i == 0) & (j == 0)
    top = (sub == half - 1) & (i == n - 1) & (j == m - 1)

    def up(x):
        return pltpu.roll(x, rows - 1, 0)

    def down(x):
        return pltpu.roll(x, 1, 0)

    def step(t, carry):
        last = (lane == LANES - 1) & (t == tiles - 1)
        first_lane = (lane == 0) & (t == 0)

        def ahead(at):
            return pltpu.roll(jnp.where(lane == 0, fields[t + 1, at], fields[t, at]), LANES - 1, 1)

        rolled = []

        def behind(x):
            turned = pltpu.roll(x, 1, 1)
            before = carry[len(rolled)]
            rolled.append(turned)
            return jnp.where(lane == 0, before, turned)

        a0, a1, c0, c1, s0, n0, b0, b1, d0, d1 = (fields[t, at] for at in range(10))
        t0, s1, n1, t1, h1, g1, side_a, side_b, side_c, side_d = (fields[t, at] for at in range(10, 20))
        wall_a, wall_b = a0 + a1, b0 + b1
        h2, g2 = two_faces(parts(b0, ahead(0), b1, ahead(1)), parts(d0, ahead(2), d1, ahead(3)))
        h2 = jnp.where(last, wall_b, h2)
        g2 = jnp.where(last, d0 + d1, g2)
        total = 1.0 / (h1 + h2)
        left, right = h1 * total, h2 * total
        left_up = up(left)
        right_up = up(right)
        s0_next = ahead(4)
        n0_next = ahead(5)
        side_a = side_a + jnp.where(first_lane, wall_a, behind(h2))
        side_c = side_c + jnp.where(first_lane, c0 + c1, behind(g2))
        side_b = side_b + h2
        side_d = side_d + g2

        nc = n0 * side_c
        sc = s0 * side_c
        nd = n1 * side_d
        sd = s1 * side_d
        even = side_a + t0 + s0 * sc + jnp.where(bottom, wall_a, down(t0 + n0 * nc))
        odd_ = side_b + t1 + s1 * sd + jnp.where(bottom, wall_b, down(t1 + n1 * nd))
        even_up = s0 * nc - t0
        odd_up = s1 * nd - t1
        sg = s0 * g1
        ng = n0 * g1
        sq = s0_next * g2
        nq = n0_next * g2
        p = h1 + s1 * sg + jnp.where(bottom, 0.0, down(n1 * ng))
        q = h2 + s1 * sq + jnp.where(bottom, 0.0, down(n1 * nq))
        p_up = n1 * sg
        p_down = s1 * ng
        q_up = s1 * nq
        q_down = n1 * sq

        mid = left * odd_ - p
        east = jnp.where(last, 0.0, right * mid - left * q)
        centre = even + left * (mid - p) + behind(right * (right * odd_ - 2.0 * q))
        lo = left * odd_up - p_up
        ro = right * odd_up - q_down
        north = even_up + left_up * lo - left * p_down + behind(right_up * ro - right * q_up)
        north = jnp.where(top, 0.0, north)
        north_east = jnp.where(last | top, 0.0, right_up * lo - left * q_up)
        north_west = jnp.where(last | top, 0.0, left_up * ro - right * p_down)
        west = behind(east)
        ne_back = behind(north_east)
        nw_back = behind(north_west)

        def below(x):
            return jnp.where(bottom, 0.0, down(x))

        values = (below(ne_back), below(north), below(north_west), west, centre, east, nw_back, north, north_east)
        return tuple(value[:half] for value in values), tuple(rolled)

    def carry_into(t):
        carry = step(jnp.maximum(t - 1, 0), (jnp.zeros((rows, LANES), jnp.float32),) * 7)[1]
        return tuple(jnp.where(t > 0, x, 0.0) for x in carry)

    return step, carry_into


def stencil_kernel(n, m, half, per_block, fields, held, carried, out, late, stored):
    tiles = fields.shape[0] - 1
    i = lax.axis_index("gx")
    low = (chosen(i, [last_block(n, at) for at in range(n)]) + 1) * per_block - 2
    count = LAST
    tile_stencil, _ = stencil_stage(n, m, half, fields)

    def columns(t, width):
        return pl.ds(pl.multiple_of(t * LANES, LANES), width * LANES)

    for q in range(tiles - count):
        cols = columns(jnp.where(q < low, q, q + count), 1)
        pltpu.make_async_copy(held.at[:, :, cols], out.at[:, :, cols], stored.at[0]).start()

    carry = tuple(carried[at] for at in range(7))
    for q in range(count):
        values, carry = tile_stencil(low + q, carry)
        for at, value in enumerate(values):
            late[at, :, q * LANES : (q + 1) * LANES] = value
    pltpu.make_async_copy(late, out.at[:, :, columns(low, count)], stored.at[0]).start()
    pltpu.make_async_copy(held, out, stored.at[0]).wait()


def shards(n, m, conductivity):
    planes, local_rows, local_cols = conductivity.shape
    band = local_rows // n
    half = band // 2
    rows = -(-(half + 2) // 8) * 8
    tiles = n * local_cols // (2 * LANES)
    vmem = pl.BlockSpec(memory_space=pltpu.VMEM)
    anywhere = pl.BlockSpec(memory_space=pl.ANY)
    dma = pltpu.SemaphoreType.DMA
    shape = (tiles + 1, 20, rows, LANES)
    per_block = local_cols // (2 * LANES)
    result = jax.ShapeDtypeStruct((9, half, tiles * LANES), jnp.float32)
    fields, held, carried = pl.pallas_call(
        functools.partial(coarse_kernel, n, m),
        out_shape=(
            jax.ShapeDtypeStruct(shape, jnp.float32),
            result,
            jax.ShapeDtypeStruct((7, rows, LANES), jnp.float32),
        ),
        in_specs=[anywhere],
        out_specs=(vmem, vmem, vmem),
        scratch_shapes=[
            pltpu.VMEM((n, 2 * band + 8, local_cols), jnp.bfloat16),
            pltpu.VMEM((2, n - 1, planes, 8, local_cols), jnp.bfloat16),
            pltpu.VMEM((planes, 8, local_cols), jnp.bfloat16),
            pltpu.VMEM((planes, 8, local_cols), jnp.bfloat16),
            pltpu.VMEM((n, 8, local_cols), jnp.bfloat16),
            dma((n,)),
            dma((n,)),
            dma((per_block,)),
            dma((2,)),
            dma((2,)),
            dma((2,)),
            pltpu.SemaphoreType.REGULAR((n,)),
            dma((2,)),
        ],
        compiler_params=pltpu.CompilerParams(
            collective_id=0, has_side_effects=True, vmem_limit_bytes=VMEM_LIMIT
        ),
        name="coarse",
    )(pltpu.with_memory_space_constraint(conductivity, pltpu.HBM))
    stencil = pl.pallas_call(
        functools.partial(stencil_kernel, n, m, half, per_block),
        out_shape=result,
        in_specs=[vmem, vmem, vmem],
        out_specs=anywhere,
        scratch_shapes=[pltpu.VMEM((9, half, LAST * LANES), jnp.float32), dma((1,))],
        compiler_params=pltpu.CompilerParams(vmem_limit_bytes=VMEM_LIMIT),
        name="stencil",
    )(fields, held, carried)
    return stencil[:, None]


def solution(mesh):
    n, m = mesh.shape["gx"], mesh.shape["gy"]
    return jax.shard_map(
        functools.partial(shards, n, m),
        mesh=mesh,
        in_specs=(P(None, "gy", "gx"),),
        out_specs=P(None, "gy", "gx", None),
        check_vma=False,
    )
```

```python
import functools

import jax
import jax.numpy as jnp
from jax import lax
from jax.experimental import pallas as pl
from jax.experimental.pallas import tpu as pltpu
from jax.sharding import PartitionSpec as P

MESH = pl.DeviceIdType.MESH
LANES = 128
LAST = 3
VMEM_LIMIT = 16 * 1024 * 1024


def arrivals(n, i):
    half = n // 2
    if i < half:
        return list(range(i)) + list(range(n - 1, half, -1)) + list(range(i + 1, half)) + [half]
    return list(range(half, i)) + list(range(half - 1)) + list(range(i + 1, n)) + [half - 1]


def last_block(n, i):
    return arrivals(n, i)[-1]


def spans(n, i, per_block):
    tiles = n * per_block
    there, found = set(), []
    for k in [i] + arrivals(n, i)[:-1]:
        new = set(range(k * per_block, (k + 1) * per_block))
        there |= new
        ready = [
            t for t in range(tiles)
            if {max(t - 1, 0), t, min(t + 1, tiles - 1)} <= there and {t - 1, t, t + 1} & new
        ]
        found.append((ready[0], ready[-1] + 1) if ready else (0, 0))
    return found


def chosen(i, values):
    picked = values[-1]
    for at in range(len(values) - 2, -1, -1):
        picked = jnp.where(i == at, values[at], picked)
    return picked


def coarse_kernel(
    n, m, cells, fields, held, carried, blocks, rims, south_in, north_in, pack,
    arrived, around, piece, sent, edge_sent, edge_arrived, known, own,
):
    i = lax.axis_index("gx")
    j = lax.axis_index("gy")
    block = cells.shape[2]
    band = cells.shape[1] // n
    half = n // 2
    per_block = block // (2 * LANES)
    has_left, has_right = i > 0, i < n - 1
    has_south, has_north = j > 0, j < m - 1
    before, after = jnp.maximum(j - 1, 0), jnp.minimum(j + 1, m - 1)

    def signal(sem, x, y):
        pl.semaphore_signal(sem, inc=1, device_id=(x, y), device_id_type=MESH)

    barrier = pltpu.get_barrier_semaphore()

    @pl.when(i == 1)
    def _():
        signal(barrier, 0, j)

    for t in range(1, n):
        @pl.when(i < t)
        def _():
            signal(barrier, t, j)

    @pl.when(has_north)
    def _():
        signal(barrier, i, after)

    def rows_of(t):
        return pl.ds(pl.multiple_of(t * band, band), band)

    loads = []
    for t in range(n - 1):
        loads.append(pltpu.make_async_copy(cells.at[:, pl.ds((t + 1) * band - 8, 8), :], rims.at[0, t], own.at[0]))
        loads.append(pltpu.make_async_copy(cells.at[:, pl.ds((t + 1) * band, 8), :], rims.at[1, t], own.at[0]))
    for plane in range(2):
        loads.append(pltpu.make_async_copy(cells.at[plane, rows_of(i), :], blocks.at[i, pl.ds(plane * band, band), :], own.at[1]))
    for load in loads:
        load.start()

    @pl.when(jnp.logical_not(has_south))
    def _():
        south_in[...] = jnp.ones(south_in.shape, south_in.dtype)

    @pl.when(jnp.logical_not(has_north))
    def _():
        north_in[...] = jnp.ones(north_in.shape, north_in.dtype)

    def remote(src, dst, send, recv, x, y):
        return pltpu.make_async_remote_copy(
            src_ref=src, dst_ref=dst, send_sem=send, recv_sem=recv, device_id=(x, y), device_id_type=MESH
        )

    def cols_of(p):
        return pl.ds(p * 2 * LANES, 2 * LANES)

    def send_rows(t, planes=(0, 1), pieces=range(per_block)):
        last = i == chosen(t, [last_block(n, at) for at in range(n)])
        for plane in planes if pieces[0] == 0 else ():
            rows = pl.ds(plane * band, band)

            @pl.when(jnp.logical_not(last))
            def _():
                remote(cells.at[plane, rows_of(t), :], blocks.at[i, rows, :], sent.at[0], arrived.at[i], t, j).start()

        @pl.when(last)
        def _():
            for p in pieces:
                for plane in planes:
                    rows = pl.ds(plane * band, band)
                    remote(
                        cells.at[plane, rows_of(t), cols_of(p)], blocks.at[i, rows, cols_of(p)],
                        sent.at[0], piece.at[p], t, j,
                    ).start()

    def send_halo(t):
        rows = pl.ds(2 * band, 6)
        remote(pack.at[t, pl.ds(0, 6), :], blocks.at[i, rows, :], sent.at[1], around.at[i], t, j).start()

    def to_north():
        return remote(cells.at[:, pl.ds(n * band - 8, 8), :], south_in, edge_sent.at[0], edge_arrived.at[0], i, after)

    def to_south():
        return remote(cells.at[:, pl.ds(0, 8), :], north_in, edge_sent.at[1], edge_arrived.at[1], i, before)

    sub = lax.broadcasted_iota(jnp.int32, (8, block), 0)

    def make_pack(t, under, over):
        low = [pltpu.roll(under[p].astype(jnp.float32), 2 + 2 * p, 0) for p in range(2)]
        high = [pltpu.roll(over[p].astype(jnp.float32), 4 + p, 0) for p in range(2)]
        rows = jnp.where(sub < 2, low[0], jnp.where(sub < 4, low[1], jnp.where(sub == 4, high[0], high[1])))
        pack[t] = rows.astype(jnp.bfloat16)

    pl.semaphore_wait(barrier, i + jnp.where(has_south, 1, 0) + jnp.where(i == 0, 1, 0))

    @pl.when(has_left)
    def _():
        send_rows(0, pieces=range(per_block - 1))

    @pl.when(i == 0)
    def _():
        send_rows(1)

    for t in range(n - 2, -1, -1):
        @pl.when((i > t) & ((t > 0) | (i > 1)))
        def _():
            signal(known.at[i], t, j)

    @pl.when(has_south)
    def _():
        signal(known.at[0], i, before)
        to_south().start()

    pltpu.make_async_copy(rims, rims, own.at[0]).wait()
    for t in range(1, n - 1):
        make_pack(t, rims.at[0, t - 1], rims.at[1, t])

    @pl.when(has_right & (i > 0))
    def _():
        pl.semaphore_wait(known.at[i + 1], 1)

    @pl.when(i + 1 < n - 1)
    def _():
        send_halo(i + 1)

    @pl.when(has_right & (i > 0))
    def _():
        send_rows(i + 1)

    splits = i > half

    @pl.when(splits)
    def _():
        send_rows(i - 1, (0,))

    @pl.when(has_north)
    def _():
        pl.semaphore_wait(known.at[0], 1)
        to_north().start()

    for t in range(2, n):
        @pl.when(i + 1 < t)
        def _():
            pl.semaphore_wait(known.at[t], 1)
            if t < n - 1:
                send_halo(t)
                send_rows(t)
            else:
                send_rows(t, pieces=range(per_block // 2))

    @pl.when(has_south)
    def _():
        to_north().wait_recv()

    @pl.when(has_north)
    def _():
        to_south().wait_recv()

    make_pack(0, south_in, rims.at[1, 0])
    make_pack(n - 1, rims.at[0, n - 2], north_in)

    @pl.when(has_left)
    def _():
        send_halo(0)
        send_rows(0, pieces=range(per_block - 1, per_block))

    @pl.when(has_right)
    def _():
        send_halo(n - 1)

    @pl.when(i + 1 < n - 1)
    def _():
        send_rows(n - 1, pieces=range(per_block // 2, per_block))

    for t in range(1, n - 1):
        @pl.when((i > t) & jnp.logical_not(splits & (i == t + 1)))
        def _():
            send_halo(t)
            send_rows(t)

    @pl.when(splits)
    def _():
        send_halo(i - 1)
        send_rows(i - 1, (1,))

    blocks[i, pl.ds(2 * band, 8), :] = pack[i]

    tile_terms, first = arrival_stage(n, m, band, blocks, fields)
    tile_stencil, carry_into = stencil_stage(n, m, band // 2, fields)
    ranges = [spans(n, at, per_block) for at in range(n)]

    def second(step):
        found = [of_device[step] for of_device in ranges]
        count = max(end - low for low, end in found)
        low = chosen(i, [min(low, n * per_block - count) for low, _ in found])
        carry = carry_into(low)
        for q in range(count):
            values, carry = tile_stencil(low + q, carry)
            hold(low + q, values)

    def hold(t, values):
        cols = pl.ds(pl.multiple_of(t * LANES, LANES), LANES)
        for at, value in enumerate(values):
            held[at, :, cols] = value

    def landed(ref, sem, k):
        remote(ref, ref, sent.at[0], sem, k, j).wait_recv()

    mine = blocks.at[i, pl.ds(0, 2 * band), :]
    pltpu.make_async_copy(mine, mine, own.at[1]).wait()
    first(i, 0, per_block)
    second(0)
    orders = [arrivals(n, at) for at in range(n)]
    for step in range(n - 2):
        k = chosen(i, [order[step] for order in orders])
        landed(blocks.at[k, pl.ds(0, 2 * band), :], arrived.at[k], k)
        landed(blocks.at[k, pl.ds(2 * band, 6), :], around.at[k], k)
        first(k, 0, per_block)
        second(step + 1)
    k = chosen(i, [order[n - 2] for order in orders])
    low = k * per_block - 1
    carry = carry_into(low)
    landed(blocks.at[k, pl.ds(2 * band, 6), :], around.at[k], k)
    done = 0
    for group in [range(per_block - 2)] + [(p,) for p in range(per_block - 2, per_block)]:
        for p in group:
            landed(blocks.at[k, pl.ds(0, 2 * band), cols_of(p)], piece.at[p], k)
        between = []
        for q in range(done, group[0]):
            values, carry = tile_stencil(low + q, carry)
            between.append((low + q, values))
        done = group[0]
        stores = [tile_terms(k, p) for p in group]
        for t, values in between:
            hold(t, values)
        if group[-1] == per_block - 1:
            for at, value in enumerate(carry):
                carried[at] = value
        for store in stores:
            store()

    def drained(ref, sem):
        remote(ref, ref, sem, arrived.at[0], i, j).wait_send()

    drained(blocks.at[pl.ds(0, n - 1), pl.ds(0, 2 * band), :], sent.at[0])
    drained(blocks.at[pl.ds(0, n - 1), pl.ds(2 * band, 6), :], sent.at[1])

    @pl.when(has_north)
    def _():
        to_north().wait_send()

    @pl.when(has_south)
    def _():
        to_south().wait_send()


def parts(x0, y0, x1, y1):
    s0, s1 = x0 + y0, x1 + y1
    return x0 * y0 * s1 + x1 * y1 * s0, s0 * s1


def two_faces(one, two):
    scale = 2.0 / (one[1] * two[1])
    return one[0] * two[1] * scale, two[0] * one[1] * scale


def middle(one, two):
    x, y = one[0] * two[1], two[0] * one[1]
    total = 1.0 / (x + y)
    return x * total, y * total, 2.0 * (one[0] * two[0]) * total


def verticals(pairs):
    sums = [x + y for x, y in pairs]
    low, high = sums[0] * sums[1], sums[2] * sums[3]
    scale = 4.0 / (low * high)
    low, high = high * scale, low * scale
    shares = (sums[1] * low, sums[0] * low, sums[3] * high, sums[2] * high)
    return [x * y * share for (x, y), share in zip(pairs, shares)]


def arrival_stage(n, m, band, blocks, fields):
    block = blocks.shape[2]
    half = band // 2
    rows = fields.shape[2]
    tiles = fields.shape[0] - 1
    per_block = block // (2 * LANES)
    i = lax.axis_index("gx")
    j = lax.axis_index("gy")
    last_rows = (i == n - 1) & (j == m - 1)

    taken = 2 * band + 6
    want = lax.broadcasted_iota(jnp.int32, (4 * rows, taken), 0)
    have = lax.broadcasted_iota(jnp.int32, (4 * rows, taken), 1)
    group = jnp.where(want >= 3 * rows, 3, jnp.where(want >= 2 * rows, 2, jnp.where(want >= rows, 1, 0)))
    place = want - group * rows
    plane = jnp.where(group >= 2, 1, 0)
    odd = group - 2 * plane
    inside = plane * band + 2 * jnp.where(place < half, place, 0) + odd
    above = jnp.where(odd == 0, 2 * band + 4 + plane, plane * band + 1)
    below = 2 * band + 2 * plane + odd
    source = jnp.where(place == half, above, jnp.where(place == rows - 1, below, inside))
    pick_rows = jnp.where(have == source, 1.0, 0.0).astype(jnp.bfloat16)
    fine = lax.broadcasted_iota(jnp.int32, (2 * LANES, 2 * LANES), 0)
    to = lax.broadcasted_iota(jnp.int32, (2 * LANES, 2 * LANES), 1)
    pick_cols = jnp.where(fine == jnp.where(to < LANES, 2 * to, 2 * (to - LANES) + 1), 1.0, 0.0).astype(jnp.bfloat16)

    top = (lax.broadcasted_iota(jnp.int32, (rows, LANES), 0) == half - 1) & last_rows

    def up(x):
        return pltpu.roll(x, rows - 1, 0)

    def tile_terms(k, part):
        t = k * per_block + part
        cols = pl.ds(part * 2 * LANES, 2 * LANES)
        stored = blocks[k, pl.ds(0, taken), cols]
        picked = jnp.dot(pick_rows, stored, preferred_element_type=jnp.float32).astype(jnp.bfloat16)
        split = jnp.dot(picked, pick_cols, preferred_element_type=jnp.float32)
        a0, c0, a1, c1 = (split[g * rows : (g + 1) * rows, :LANES] for g in range(4))
        b0, d0, b1, d1 = (split[g * rows : (g + 1) * rows, LANES:] for g in range(4))
        def wall(x0, x1, inner):
            return jnp.where(top, 0.5 * (x0 + x1), inner[0]), jnp.where(top, 1.0, inner[1])

        s0, n0, t0 = middle(parts(a0, c0, a1, c1), wall(c0, c1, parts(c0, up(a0), c1, up(a1))))
        s1, n1, t1 = middle(parts(b0, d0, b1, d1), wall(d0, d1, parts(d0, up(b0), d1, up(b1))))
        h1, g1 = two_faces(parts(a0, b0, a1, b1), parts(c0, d0, c1, d1))
        pairs = ((a0, a1), (b0, b1), (c0, c1), (d0, d1))
        side_a, side_b, side_c, side_d = (
            (x + ((k0 + k1) + v)) - v for x, (k0, k1), v in zip((h1, h1, g1, g1), pairs, verticals(pairs))
        )
        values = (a0, a1, c0, c1, s0, n0, b0, b1, d0, d1, t0, s1, n1, t1, h1, g1, side_a, side_b, side_c, side_d)

        def store():
            for at, value in enumerate(values):
                fields[t, at] = value

        return store

    def first(k, start, count):
        for part in range(start, start + count):
            tile_terms(k, part)()

    ones = jnp.ones((rows, LANES), jnp.float32)
    for at in range(6):
        fields[tiles, at] = ones

    return tile_terms, first


def stencil_stage(n, m, half, fields):
    rows = fields.shape[2]
    tiles = fields.shape[0] - 1
    i = lax.axis_index("gx")
    j = lax.axis_index("gy")
    lane = lax.broadcasted_iota(jnp.int32, (rows, LANES), 1)
    sub = lax.broadcasted_iota(jnp.int32, (rows, LANES), 0)
    bottom = (sub == 0) & (i == 0) & (j == 0)
    top = (sub == half - 1) & (i == n - 1) & (j == m - 1)

    def up(x):
        return pltpu.roll(x, rows - 1, 0)

    def down(x):
        return pltpu.roll(x, 1, 0)

    def step(t, carry):
        last = (lane == LANES - 1) & (t == tiles - 1)
        first_lane = (lane == 0) & (t == 0)

        def ahead(at):
            return pltpu.roll(jnp.where(lane == 0, fields[t + 1, at], fields[t, at]), LANES - 1, 1)

        rolled = []

        def behind(x):
            turned = pltpu.roll(x, 1, 1)
            before = carry[len(rolled)]
            rolled.append(turned)
            return jnp.where(lane == 0, before, turned)

        a0, a1, c0, c1, s0, n0, b0, b1, d0, d1 = (fields[t, at] for at in range(10))
        t0, s1, n1, t1, h1, g1, side_a, side_b, side_c, side_d = (fields[t, at] for at in range(10, 20))
        wall_a, wall_b = a0 + a1, b0 + b1
        h2, g2 = two_faces(parts(b0, ahead(0), b1, ahead(1)), parts(d0, ahead(2), d1, ahead(3)))
        h2 = jnp.where(last, wall_b, h2)
        g2 = jnp.where(last, d0 + d1, g2)
        total = 1.0 / (h1 + h2)
        left, right = h1 * total, h2 * total
        left_up = up(left)
        right_up = up(right)
        s0_next = ahead(4)
        n0_next = ahead(5)
        side_a = side_a + jnp.where(first_lane, wall_a, behind(h2))
        side_c = side_c + jnp.where(first_lane, c0 + c1, behind(g2))
        side_b = side_b + h2
        side_d = side_d + g2

        nc = n0 * side_c
        sc = s0 * side_c
        nd = n1 * side_d
        sd = s1 * side_d
        even = side_a + t0 + s0 * sc + jnp.where(bottom, wall_a, down(t0 + n0 * nc))
        odd_ = side_b + t1 + s1 * sd + jnp.where(bottom, wall_b, down(t1 + n1 * nd))
        even_up = s0 * nc - t0
        odd_up = s1 * nd - t1
        sg = s0 * g1
        ng = n0 * g1
        sq = s0_next * g2
        nq = n0_next * g2
        p = h1 + s1 * sg + jnp.where(bottom, 0.0, down(n1 * ng))
        q = h2 + s1 * sq + jnp.where(bottom, 0.0, down(n1 * nq))
        p_up = n1 * sg
        p_down = s1 * ng
        q_up = s1 * nq
        q_down = n1 * sq

        mid = left * odd_ - p
        east = jnp.where(last, 0.0, right * mid - left * q)
        centre = even + left * (mid - p) + behind(right * (right * odd_ - 2.0 * q))
        lo = left * odd_up - p_up
        ro = right * odd_up - q_down
        north = even_up + left_up * lo - left * p_down + behind(right_up * ro - right * q_up)
        north = jnp.where(top, 0.0, north)
        north_east = jnp.where(last | top, 0.0, right_up * lo - left * q_up)
        north_west = jnp.where(last | top, 0.0, left_up * ro - right * p_down)
        west = behind(east)
        ne_back = behind(north_east)
        nw_back = behind(north_west)

        def below(x):
            return jnp.where(bottom, 0.0, down(x))

        values = (below(ne_back), below(north), below(north_west), west, centre, east, nw_back, north, north_east)
        return tuple(value[:half] for value in values), tuple(rolled)

    def carry_into(t):
        carry = step(jnp.maximum(t - 1, 0), (jnp.zeros((rows, LANES), jnp.float32),) * 7)[1]
        return tuple(jnp.where(t > 0, x, 0.0) for x in carry)

    return step, carry_into


def stencil_kernel(n, m, half, per_block, fields, held, carried, out, late, stored):
    tiles = fields.shape[0] - 1
    i = lax.axis_index("gx")
    low = (chosen(i, [last_block(n, at) for at in range(n)]) + 1) * per_block - 2
    count = LAST
    tile_stencil, _ = stencil_stage(n, m, half, fields)

    def columns(t, width):
        start = t * LANES
        return pl.ds(start if isinstance(t, int) else pl.multiple_of(start, LANES), width * LANES)

    for block in sorted({last_block(n, at) for at in range(n)}):
        at = (block + 1) * per_block - 2

        @pl.when(low == at)
        def _():
            for start in [*range(0, at, 5), *range(at + count, tiles, 5)]:
                cols = columns(start, min(5, (at if start < at else tiles) - start))
                pltpu.make_async_copy(held.at[:, :, cols], out.at[:, :, cols], stored.at[0]).start()

    carry = tuple(carried[at] for at in range(7))
    for q in range(count):
        values, carry = tile_stencil(low + q, carry)
        for at, value in enumerate(values):
            late[at, :, q * LANES : (q + 1) * LANES] = value
    pltpu.make_async_copy(late, out.at[:, :, columns(low, count)], stored.at[0]).start()
    pltpu.make_async_copy(held, out, stored.at[0]).wait()


def shards(n, m, conductivity):
    planes, local_rows, local_cols = conductivity.shape
    band = local_rows // n
    half = band // 2
    rows = -(-(half + 2) // 8) * 8
    tiles = n * local_cols // (2 * LANES)
    vmem = pl.BlockSpec(memory_space=pltpu.VMEM)
    anywhere = pl.BlockSpec(memory_space=pl.ANY)
    dma = pltpu.SemaphoreType.DMA
    shape = (tiles + 1, 20, rows, LANES)
    per_block = local_cols // (2 * LANES)
    result = jax.ShapeDtypeStruct((9, half, tiles * LANES), jnp.float32)
    fields, held, carried = pl.pallas_call(
        functools.partial(coarse_kernel, n, m),
        out_shape=(
            jax.ShapeDtypeStruct(shape, jnp.float32),
            result,
            jax.ShapeDtypeStruct((7, rows, LANES), jnp.float32),
        ),
        in_specs=[anywhere],
        out_specs=(vmem, vmem, vmem),
        scratch_shapes=[
            pltpu.VMEM((n, 2 * band + 8, local_cols), jnp.bfloat16),
            pltpu.VMEM((2, n - 1, planes, 8, local_cols), jnp.bfloat16),
            pltpu.VMEM((planes, 8, local_cols), jnp.bfloat16),
            pltpu.VMEM((planes, 8, local_cols), jnp.bfloat16),
            pltpu.VMEM((n, 8, local_cols), jnp.bfloat16),
            dma((n,)),
            dma((n,)),
            dma((per_block,)),
            dma((2,)),
            dma((2,)),
            dma((2,)),
            pltpu.SemaphoreType.REGULAR((n,)),
            dma((2,)),
        ],
        compiler_params=pltpu.CompilerParams(
            collective_id=0, has_side_effects=True, vmem_limit_bytes=VMEM_LIMIT
        ),
        name="coarse",
    )(pltpu.with_memory_space_constraint(conductivity, pltpu.HBM))
    stencil = pl.pallas_call(
        functools.partial(stencil_kernel, n, m, half, per_block),
        out_shape=result,
        in_specs=[vmem, vmem, vmem],
        out_specs=anywhere,
        scratch_shapes=[pltpu.VMEM((9, half, LAST * LANES), jnp.float32), dma((1,))],
        compiler_params=pltpu.CompilerParams(vmem_limit_bytes=VMEM_LIMIT),
        name="stencil",
    )(fields, held, carried)
    return stencil[:, None]


def solution(mesh):
    n, m = mesh.shape["gx"], mesh.shape["gy"]
    return jax.shard_map(
        functools.partial(shards, n, m),
        mesh=mesh,
        in_specs=(P(None, "gy", "gx"),),
        out_specs=P(None, "gy", "gx", None),
        check_vma=False,
    )
```

```python
import functools

import jax
import jax.numpy as jnp
from jax import lax
from jax.experimental import pallas as pl
from jax.experimental.pallas import tpu as pltpu
from jax.sharding import PartitionSpec as P

MESH = pl.DeviceIdType.MESH
LANES = 128
LAST = 3
VMEM_LIMIT = 16 * 1024 * 1024


def arrivals(n, i):
    half = n // 2
    if i < half:
        return list(range(i)) + list(range(n - 1, half, -1)) + list(range(i + 1, half)) + [half]
    return list(range(half, i)) + list(range(half - 1)) + list(range(i + 1, n)) + [half - 1]


def last_block(n, i):
    return arrivals(n, i)[-1]


def spans(n, i, per_block):
    tiles = n * per_block
    there, found = set(), []
    for k in [i] + arrivals(n, i)[:-1]:
        new = set(range(k * per_block, (k + 1) * per_block))
        there |= new
        ready = [
            t for t in range(tiles)
            if {max(t - 1, 0), t, min(t + 1, tiles - 1)} <= there and {t - 1, t, t + 1} & new
        ]
        found.append((ready[0], ready[-1] + 1) if ready else (0, 0))
    return found


def chosen(i, values):
    picked = values[-1]
    for at in range(len(values) - 2, -1, -1):
        picked = jnp.where(i == at, values[at], picked)
    return picked


def coarse_kernel(
    n, m, cells, fields, held, carried, blocks, rims, south_in, north_in, pack,
    arrived, around, piece, sent, edge_sent, edge_arrived, known, own,
):
    i = lax.axis_index("gx")
    j = lax.axis_index("gy")
    block = cells.shape[2]
    band = cells.shape[1] // n
    half = n // 2
    per_block = block // (2 * LANES)
    has_left, has_right = i > 0, i < n - 1
    has_south, has_north = j > 0, j < m - 1
    before, after = jnp.maximum(j - 1, 0), jnp.minimum(j + 1, m - 1)

    def signal(sem, x, y):
        pl.semaphore_signal(sem, inc=1, device_id=(x, y), device_id_type=MESH)

    barrier = pltpu.get_barrier_semaphore()

    @pl.when(i == 1)
    def _():
        signal(barrier, 0, j)

    for t in range(1, n):
        @pl.when(i < t)
        def _():
            signal(barrier, t, j)

    @pl.when(has_north)
    def _():
        signal(barrier, i, after)

    def rows_of(t):
        return pl.ds(pl.multiple_of(t * band, band), band)

    loads = []
    for t in range(n - 1):
        loads.append(pltpu.make_async_copy(cells.at[:, pl.ds((t + 1) * band - 8, 8), :], rims.at[0, t], own.at[0]))
        loads.append(pltpu.make_async_copy(cells.at[:, pl.ds((t + 1) * band, 8), :], rims.at[1, t], own.at[0]))
    for plane in range(2):
        loads.append(pltpu.make_async_copy(cells.at[plane, rows_of(i), :], blocks.at[i, pl.ds(plane * band, band), :], own.at[1]))
    for load in loads:
        load.start()

    @pl.when(jnp.logical_not(has_south))
    def _():
        south_in[...] = jnp.ones(south_in.shape, south_in.dtype)

    @pl.when(jnp.logical_not(has_north))
    def _():
        north_in[...] = jnp.ones(north_in.shape, north_in.dtype)

    def remote(src, dst, send, recv, x, y):
        return pltpu.make_async_remote_copy(
            src_ref=src, dst_ref=dst, send_sem=send, recv_sem=recv, device_id=(x, y), device_id_type=MESH
        )

    groups = tuple(enumerate([range(per_block - 2), *((p,) for p in range(per_block - 2, per_block))]))

    def cols_of(group):
        return pl.ds(group[0] * 2 * LANES, len(group) * 2 * LANES)

    def send_rows(t, planes=(0, 1), pieces=groups):
        last = i == chosen(t, [last_block(n, at) for at in range(n)])
        for plane in planes if pieces[0] == groups[0] else ():
            rows = pl.ds(plane * band, band)

            @pl.when(jnp.logical_not(last))
            def _():
                remote(cells.at[plane, rows_of(t), :], blocks.at[i, rows, :], sent.at[0], arrived.at[i], t, j).start()

        @pl.when(last)
        def _():
            for p, group in pieces:
                for plane in planes:
                    rows = pl.ds(plane * band, band)
                    remote(
                        cells.at[plane, rows_of(t), cols_of(group)], blocks.at[i, rows, cols_of(group)],
                        sent.at[0], piece.at[p], t, j,
                    ).start()

    def send_halo(t):
        rows = pl.ds(2 * band, 6)
        remote(pack.at[t, pl.ds(0, 6), :], blocks.at[i, rows, :], sent.at[1], around.at[i], t, j).start()

    def to_north():
        return remote(cells.at[:, pl.ds(n * band - 8, 8), :], south_in, edge_sent.at[0], edge_arrived.at[0], i, after)

    def to_south():
        return remote(cells.at[:, pl.ds(0, 8), :], north_in, edge_sent.at[1], edge_arrived.at[1], i, before)

    sub = lax.broadcasted_iota(jnp.int32, (8, block), 0)

    def make_pack(t, under, over):
        low = [pltpu.roll(under[p].astype(jnp.float32), 2 + 2 * p, 0) for p in range(2)]
        high = [pltpu.roll(over[p].astype(jnp.float32), 4 + p, 0) for p in range(2)]
        rows = jnp.where(sub < 2, low[0], jnp.where(sub < 4, low[1], jnp.where(sub == 4, high[0], high[1])))
        pack[t] = rows.astype(jnp.bfloat16)

    pl.semaphore_wait(barrier, i + jnp.where(has_south, 1, 0) + jnp.where(i == 0, 1, 0))

    for t in range(n - 2, -1, -1):
        @pl.when((i > t) & ((t > 0) | (i > 1)))
        def _():
            signal(known.at[i - 1], t, j)

    @pl.when(has_left)
    def _():
        send_rows(0, pieces=groups[:2])

    @pl.when(i == 0)
    def _():
        send_rows(1)

    @pl.when(has_south)
    def _():
        signal(known.at[0], i, before)
        to_south().start()

    pltpu.make_async_copy(rims, rims, own.at[0]).wait()
    for t in range(1, n - 1):
        make_pack(t, rims.at[0, t - 1], rims.at[1, t])

    @pl.when(has_right & (i > 0))
    def _():
        pl.semaphore_wait(known.at[i], 1)

    @pl.when(i + 1 < n - 1)
    def _():
        send_halo(i + 1)

    @pl.when(has_right & (i > 0))
    def _():
        send_rows(i + 1)

    splits = i > half

    @pl.when(splits)
    def _():
        send_rows(i - 1, (0,))

    @pl.when(has_north)
    def _():
        pl.semaphore_wait(known.at[0], 1)
        to_north().start()

    for t in range(2, n):
        @pl.when(i + 1 < t)
        def _():
            pl.semaphore_wait(known.at[t - 1], 1)
            if t < n - 1:
                send_halo(t)
                send_rows(t)
            else:
                send_rows(t, pieces=groups[:1])

    @pl.when(has_south)
    def _():
        to_north().wait_recv()

    @pl.when(has_north)
    def _():
        to_south().wait_recv()

    make_pack(0, south_in, rims.at[1, 0])
    make_pack(n - 1, rims.at[0, n - 2], north_in)

    @pl.when(has_left)
    def _():
        send_halo(0)
        send_rows(0, pieces=groups[2:])

    @pl.when(has_right)
    def _():
        send_halo(n - 1)

    @pl.when(i + 1 < n - 1)
    def _():
        send_rows(n - 1, pieces=groups[1:])

    for t in range(1, n - 1):
        @pl.when((i > t) & jnp.logical_not(splits & (i == t + 1)))
        def _():
            send_halo(t)
            send_rows(t)

    @pl.when(splits)
    def _():
        send_halo(i - 1)
        send_rows(i - 1, (1,))

    blocks[i, pl.ds(2 * band, 8), :] = pack[i]

    tile_terms, first = arrival_stage(n, m, band, blocks, fields)
    tile_stencil, carry_into = stencil_stage(n, m, band // 2, fields)
    ranges = [spans(n, at, per_block) for at in range(n)]

    def second(step):
        found = [of_device[step] for of_device in ranges]
        count = max(end - low for low, end in found)
        low = chosen(i, [min(low, n * per_block - count) for low, _ in found])
        carry = carry_into(low)
        for q in range(count):
            values, carry = tile_stencil(low + q, carry)
            hold(low + q, values)

    def hold(t, values):
        cols = pl.ds(pl.multiple_of(t * LANES, LANES), LANES)
        for at, value in enumerate(values):
            held[at, :, cols] = value

    def landed(ref, sem, k):
        remote(ref, ref, sent.at[0], sem, k, j).wait_recv()

    mine = blocks.at[i, pl.ds(0, 2 * band), :]
    pltpu.make_async_copy(mine, mine, own.at[1]).wait()
    first(i, 0, per_block)
    second(0)
    orders = [arrivals(n, at) for at in range(n)]
    for step in range(n - 2):
        k = chosen(i, [order[step] for order in orders])
        landed(blocks.at[k, pl.ds(0, 2 * band), :], arrived.at[k], k)
        landed(blocks.at[k, pl.ds(2 * band, 6), :], around.at[k], k)
        first(k, 0, per_block)
        second(step + 1)
    k = chosen(i, [order[n - 2] for order in orders])
    low = k * per_block - 1
    carry = carry_into(low)
    landed(blocks.at[k, pl.ds(2 * band, 6), :], around.at[k], k)
    done = 0
    for p, group in groups:
        landed(blocks.at[k, pl.ds(0, 2 * band), cols_of(group)], piece.at[p], k)
        between = []
        for q in range(done, group[0]):
            values, carry = tile_stencil(low + q, carry)
            between.append((low + q, values))
        done = group[0]
        stores = [tile_terms(k, p) for p in group]
        for t, values in between:
            hold(t, values)
        if group[-1] == per_block - 1:
            for at, value in enumerate(carry):
                carried[at] = value
        for store in stores:
            store()

    def drained(ref, sem):
        remote(ref, ref, sem, arrived.at[0], i, j).wait_send()

    drained(blocks.at[pl.ds(0, n - 1), pl.ds(0, 2 * band), :], sent.at[0])

    drained(blocks.at[pl.ds(0, n - 1), pl.ds(2 * band, 6), :], sent.at[1])

    @pl.when(has_north)
    def _():
        to_north().wait_send()

    @pl.when(has_south)
    def _():
        to_south().wait_send()


def parts(x0, y0, x1, y1):
    s0, s1 = x0 + y0, x1 + y1
    return x0 * y0 * s1 + x1 * y1 * s0, s0 * s1


def two_faces(one, two):
    scale = 2.0 / (one[1] * two[1])
    return one[0] * two[1] * scale, two[0] * one[1] * scale


def middle(one, two):
    x, y = one[0] * two[1], two[0] * one[1]
    total = 1.0 / (x + y)
    return x * total, y * total, 2.0 * (one[0] * two[0]) * total


def verticals(pairs):
    sums = [x + y for x, y in pairs]
    low, high = sums[0] * sums[1], sums[2] * sums[3]
    scale = 4.0 / (low * high)
    low, high = high * scale, low * scale
    shares = (sums[1] * low, sums[0] * low, sums[3] * high, sums[2] * high)
    return [x * y * share for (x, y), share in zip(pairs, shares)]


def arrival_stage(n, m, band, blocks, fields):
    block = blocks.shape[2]
    half = band // 2
    rows = fields.shape[2]
    tiles = fields.shape[0] - 1
    per_block = block // (2 * LANES)
    i = lax.axis_index("gx")
    j = lax.axis_index("gy")
    last_rows = (i == n - 1) & (j == m - 1)

    taken = 2 * band + 6
    want = lax.broadcasted_iota(jnp.int32, (4 * rows, taken), 0)
    have = lax.broadcasted_iota(jnp.int32, (4 * rows, taken), 1)
    group = jnp.where(want >= 3 * rows, 3, jnp.where(want >= 2 * rows, 2, jnp.where(want >= rows, 1, 0)))
    place = want - group * rows
    plane = jnp.where(group >= 2, 1, 0)
    odd = group - 2 * plane
    inside = plane * band + 2 * jnp.where(place < half, place, 0) + odd
    above = jnp.where(odd == 0, 2 * band + 4 + plane, plane * band + 1)
    below = 2 * band + 2 * plane + odd
    source = jnp.where(place == half, above, jnp.where(place == rows - 1, below, inside))
    pick_rows = jnp.where(have == source, 1.0, 0.0).astype(jnp.bfloat16)
    fine = lax.broadcasted_iota(jnp.int32, (2 * LANES, 2 * LANES), 0)
    to = lax.broadcasted_iota(jnp.int32, (2 * LANES, 2 * LANES), 1)
    pick_cols = jnp.where(fine == jnp.where(to < LANES, 2 * to, 2 * (to - LANES) + 1), 1.0, 0.0).astype(jnp.bfloat16)

    top = (lax.broadcasted_iota(jnp.int32, (rows, LANES), 0) == half - 1) & last_rows

    def up(x):
        return pltpu.roll(x, rows - 1, 0)

    def tile_terms(k, part):
        t = k * per_block + part
        cols = pl.ds(part * 2 * LANES, 2 * LANES)
        stored = blocks[k, pl.ds(0, taken), cols]
        picked = jnp.dot(pick_rows, stored, preferred_element_type=jnp.float32).astype(jnp.bfloat16)
        split = jnp.dot(picked, pick_cols, preferred_element_type=jnp.float32)
        a0, c0, a1, c1 = (split[g * rows : (g + 1) * rows, :LANES] for g in range(4))
        b0, d0, b1, d1 = (split[g * rows : (g + 1) * rows, LANES:] for g in range(4))
        def wall(x0, x1, inner):
            return jnp.where(top, 0.5 * (x0 + x1), inner[0]), jnp.where(top, 1.0, inner[1])

        s0, n0, t0 = middle(parts(a0, c0, a1, c1), wall(c0, c1, parts(c0, up(a0), c1, up(a1))))
        s1, n1, t1 = middle(parts(b0, d0, b1, d1), wall(d0, d1, parts(d0, up(b0), d1, up(b1))))
        h1, g1 = two_faces(parts(a0, b0, a1, b1), parts(c0, d0, c1, d1))
        pairs = ((a0, a1), (b0, b1), (c0, c1), (d0, d1))
        side_a, side_b, side_c, side_d = (
            (x + ((k0 + k1) + v)) - v for x, (k0, k1), v in zip((h1, h1, g1, g1), pairs, verticals(pairs))
        )
        values = (a0, a1, c0, c1, s0, n0, b0, b1, d0, d1, t0, s1, n1, t1, h1, g1, side_a, side_b, side_c, side_d)

        def store():
            for at, value in enumerate(values):
                fields[t, at] = value

        return store

    def first(k, start, count):
        for part in range(start, start + count):
            tile_terms(k, part)()

    ones = jnp.ones((rows, LANES), jnp.float32)
    for at in range(6):
        fields[tiles, at] = ones

    return tile_terms, first


def stencil_stage(n, m, half, fields):
    rows = fields.shape[2]
    tiles = fields.shape[0] - 1
    i = lax.axis_index("gx")
    j = lax.axis_index("gy")
    lane = lax.broadcasted_iota(jnp.int32, (rows, LANES), 1)
    sub = lax.broadcasted_iota(jnp.int32, (rows, LANES), 0)
    bottom = (sub == 0) & (i == 0) & (j == 0)
    top = (sub == half - 1) & (i == n - 1) & (j == m - 1)

    def up(x):
        return pltpu.roll(x, rows - 1, 0)

    def down(x):
        return pltpu.roll(x, 1, 0)

    def step(t, carry):
        last = (lane == LANES - 1) & (t == tiles - 1)
        first_lane = (lane == 0) & (t == 0)

        def ahead(at):
            return pltpu.roll(jnp.where(lane == 0, fields[t + 1, at], fields[t, at]), LANES - 1, 1)

        rolled = []

        def behind(x):
            turned = pltpu.roll(x, 1, 1)
            before = carry[len(rolled)]
            rolled.append(turned)
            return jnp.where(lane == 0, before, turned)

        a0, a1, c0, c1, s0, n0, b0, b1, d0, d1 = (fields[t, at] for at in range(10))
        t0, s1, n1, t1, h1, g1, side_a, side_b, side_c, side_d = (fields[t, at] for at in range(10, 20))
        wall_a, wall_b = a0 + a1, b0 + b1
        h2, g2 = two_faces(parts(b0, ahead(0), b1, ahead(1)), parts(d0, ahead(2), d1, ahead(3)))
        h2 = jnp.where(last, wall_b, h2)
        g2 = jnp.where(last, d0 + d1, g2)
        total = 1.0 / (h1 + h2)
        left, right = h1 * total, h2 * total
        left_up = up(left)
        right_up = up(right)
        s0_next = ahead(4)
        n0_next = ahead(5)
        side_a = side_a + jnp.where(first_lane, wall_a, behind(h2))
        side_c = side_c + jnp.where(first_lane, c0 + c1, behind(g2))
        side_b = side_b + h2
        side_d = side_d + g2

        nc = n0 * side_c
        sc = s0 * side_c
        nd = n1 * side_d
        sd = s1 * side_d
        even = side_a + t0 + s0 * sc + jnp.where(bottom, wall_a, down(t0 + n0 * nc))
        odd_ = side_b + t1 + s1 * sd + jnp.where(bottom, wall_b, down(t1 + n1 * nd))
        even_up = s0 * nc - t0
        odd_up = s1 * nd - t1
        sg = s0 * g1
        ng = n0 * g1
        sq = s0_next * g2
        nq = n0_next * g2
        p = h1 + s1 * sg + jnp.where(bottom, 0.0, down(n1 * ng))
        q = h2 + s1 * sq + jnp.where(bottom, 0.0, down(n1 * nq))
        p_up = n1 * sg
        p_down = s1 * ng
        q_up = s1 * nq
        q_down = n1 * sq

        mid = left * odd_ - p
        east = jnp.where(last, 0.0, right * mid - left * q)
        centre = even + left * (mid - p) + behind(right * (right * odd_ - 2.0 * q))
        lo = left * odd_up - p_up
        ro = right * odd_up - q_down
        north = even_up + left_up * lo - left * p_down + behind(right_up * ro - right * q_up)
        north = jnp.where(top, 0.0, north)
        north_east = jnp.where(last | top, 0.0, right_up * lo - left * q_up)
        north_west = jnp.where(last | top, 0.0, left_up * ro - right * p_down)
        west = behind(east)
        ne_back = behind(north_east)
        nw_back = behind(north_west)

        def below(x):
            return jnp.where(bottom, 0.0, down(x))

        values = (below(ne_back), below(north), below(north_west), west, centre, east, nw_back, north, north_east)
        return tuple(value[:half] for value in values), tuple(rolled)

    def carry_into(t):
        carry = step(jnp.maximum(t - 1, 0), (jnp.zeros((rows, LANES), jnp.float32),) * 7)[1]
        return tuple(jnp.where(t > 0, x, 0.0) for x in carry)

    return step, carry_into


def stencil_kernel(n, m, half, per_block, fields, held, carried, out, late, stored):
    tiles = fields.shape[0] - 1
    i = lax.axis_index("gx")
    low = (chosen(i, [last_block(n, at) for at in range(n)]) + 1) * per_block - 2
    count = LAST
    tile_stencil, _ = stencil_stage(n, m, half, fields)

    def columns(t, width):
        return pl.ds(pl.multiple_of(t * LANES, LANES), width * LANES)

    for q in range(0, tiles - count, 2):
        cols = columns(jnp.where(q < low, q, q + count), min(2, tiles - count - q))
        pltpu.make_async_copy(held.at[:, :, cols], out.at[:, :, cols], stored.at[0]).start()

    carry = tuple(carried[at] for at in range(7))
    for q in range(count):
        values, carry = tile_stencil(low + q, carry)
        for at, value in enumerate(values):
            late[at, :, q * LANES : (q + 1) * LANES] = value
    pltpu.make_async_copy(late, out.at[:, :, columns(low, count)], stored.at[0]).start()
    pltpu.make_async_copy(held, out, stored.at[0]).wait()


def shards(n, m, conductivity):
    planes, local_rows, local_cols = conductivity.shape
    band = local_rows // n
    half = band // 2
    rows = -(-(half + 2) // 8) * 8
    tiles = n * local_cols // (2 * LANES)
    vmem = pl.BlockSpec(memory_space=pltpu.VMEM)
    anywhere = pl.BlockSpec(memory_space=pl.ANY)
    dma = pltpu.SemaphoreType.DMA
    shape = (tiles + 1, 20, rows, LANES)
    per_block = local_cols // (2 * LANES)
    result = jax.ShapeDtypeStruct((9, half, tiles * LANES), jnp.float32)
    fields, held, carried = pl.pallas_call(
        functools.partial(coarse_kernel, n, m),
        out_shape=(
            jax.ShapeDtypeStruct(shape, jnp.float32),
            result,
            jax.ShapeDtypeStruct((7, rows, LANES), jnp.float32),
        ),
        in_specs=[anywhere],
        out_specs=(vmem, vmem, vmem),
        scratch_shapes=[
            pltpu.VMEM((n, 2 * band + 8, local_cols), jnp.bfloat16),
            pltpu.VMEM((2, n - 1, planes, 8, local_cols), jnp.bfloat16),
            pltpu.VMEM((planes, 8, local_cols), jnp.bfloat16),
            pltpu.VMEM((planes, 8, local_cols), jnp.bfloat16),
            pltpu.VMEM((n, 8, local_cols), jnp.bfloat16),
            dma((n,)),
            dma((n,)),
            dma((3,)),
            dma((2,)),
            dma((2,)),
            dma((2,)),
            pltpu.SemaphoreType.REGULAR((n - 1,)),
            dma((2,)),
        ],
        compiler_params=pltpu.CompilerParams(
            collective_id=0, has_side_effects=True, vmem_limit_bytes=VMEM_LIMIT
        ),
        name="coarse",
    )(pltpu.with_memory_space_constraint(conductivity, pltpu.HBM))
    stencil = pl.pallas_call(
        functools.partial(stencil_kernel, n, m, half, per_block),
        out_shape=result,
        in_specs=[vmem, vmem, vmem],
        out_specs=anywhere,
        scratch_shapes=[pltpu.VMEM((9, half, LAST * LANES), jnp.float32), dma((1,))],
        compiler_params=pltpu.CompilerParams(vmem_limit_bytes=VMEM_LIMIT),
        name="stencil",
    )(fields, held, carried)
    return stencil[:, None]


def solution(mesh):
    n, m = mesh.shape["gx"], mesh.shape["gy"]
    return jax.shard_map(
        functools.partial(shards, n, m),
        mesh=mesh,
        in_specs=(P(None, "gy", "gx"),),
        out_specs=P(None, "gy", "gx", None),
        check_vma=False,
    )
```

```python
import functools

import jax
import jax.numpy as jnp
from jax import lax
from jax.experimental import pallas as pl
from jax.experimental.pallas import tpu as pltpu
from jax.sharding import PartitionSpec as P

MESH = pl.DeviceIdType.MESH
LANES = 128
LAST = 3
VMEM_LIMIT = 16 * 1024 * 1024


def arrivals(n, i):
    half = n // 2
    if i < half:
        return list(range(i)) + list(range(n - 1, half, -1)) + list(range(i + 1, half)) + [half]
    return list(range(half, i)) + list(range(half - 1)) + list(range(i + 1, n)) + [half - 1]


def last_block(n, i):
    return arrivals(n, i)[-1]


def spans(n, i, per_block):
    tiles = n * per_block
    there, found = set(), []
    for k in [i] + arrivals(n, i)[:-1]:
        new = set(range(k * per_block, (k + 1) * per_block))
        there |= new
        ready = [
            t for t in range(tiles)
            if {max(t - 1, 0), t, min(t + 1, tiles - 1)} <= there and {t - 1, t, t + 1} & new
        ]
        found.append((ready[0], ready[-1] + 1) if ready else (0, 0))
    return found


def chosen(i, values):
    picked = values[-1]
    for at in range(len(values) - 2, -1, -1):
        picked = jnp.where(i == at, values[at], picked)
    return picked


def coarse_kernel(
    n, m, cells, fields, held, carried, blocks, rims, south_in, north_in, pack,
    arrived, around, piece, sent, edge_sent, edge_arrived, known, own,
):
    i = lax.axis_index("gx")
    j = lax.axis_index("gy")
    block = cells.shape[2]
    band = cells.shape[1] // n
    half = n // 2
    per_block = block // (2 * LANES)
    has_left, has_right = i > 0, i < n - 1
    has_south, has_north = j > 0, j < m - 1
    before, after = jnp.maximum(j - 1, 0), jnp.minimum(j + 1, m - 1)

    def signal(sem, x, y):
        pl.semaphore_signal(sem, inc=1, device_id=(x, y), device_id_type=MESH)

    barrier = pltpu.get_barrier_semaphore()

    @pl.when(i == 1)
    def _():
        signal(barrier, 0, j)

    for t in range(1, n):
        @pl.when(i < t)
        def _():
            signal(barrier, t, j)

    @pl.when(has_north)
    def _():
        signal(barrier, i, after)

    def rows_of(t):
        return pl.ds(pl.multiple_of(t * band, band), band)

    loads = []
    for t in range(n - 1):
        loads.append(pltpu.make_async_copy(cells.at[:, pl.ds((t + 1) * band - 8, 8), :], rims.at[0, t], own.at[0]))
        loads.append(pltpu.make_async_copy(cells.at[:, pl.ds((t + 1) * band, 8), :], rims.at[1, t], own.at[0]))
    for plane in range(2):
        loads.append(pltpu.make_async_copy(cells.at[plane, rows_of(i), :], blocks.at[i, pl.ds(plane * band, band), :], own.at[1]))
    for load in loads:
        load.start()

    @pl.when(jnp.logical_not(has_south))
    def _():
        south_in[...] = jnp.ones(south_in.shape, south_in.dtype)

    @pl.when(jnp.logical_not(has_north))
    def _():
        north_in[...] = jnp.ones(north_in.shape, north_in.dtype)

    def remote(src, dst, send, recv, x, y):
        return pltpu.make_async_remote_copy(
            src_ref=src, dst_ref=dst, send_sem=send, recv_sem=recv, device_id=(x, y), device_id_type=MESH
        )

    groups = tuple(enumerate([range(per_block - 2), *((p,) for p in range(per_block - 2, per_block))]))

    def cols_of(group):
        return pl.ds(group[0] * 2 * LANES, len(group) * 2 * LANES)

    def send_rows(t, planes=(0, 1), pieces=groups):
        last = i == chosen(t, [last_block(n, at) for at in range(n)])
        low, count = planes[0], len(planes)
        rows = blocks.at[i, pl.ds(low * band, count * band), :].reshape(count, band, block)
        taken = cells.at[pl.ds(low, count), rows_of(t), :]

        if pieces[0] == groups[0]:
            @pl.when(jnp.logical_not(last))
            def _():
                remote(taken, rows, sent.at[0], arrived.at[i], t, j).start()

        @pl.when(last)
        def _():
            for p, group in pieces:
                cols = cols_of(group)
                remote(taken.at[:, :, cols], rows.at[:, :, cols], sent.at[0], piece.at[p], t, j).start()

    def send_halo(t):
        rows = pl.ds(2 * band, 6)
        remote(pack.at[t, pl.ds(0, 6), :], blocks.at[i, rows, :], sent.at[1], around.at[i], t, j).start()

    def to_north():
        return remote(cells.at[:, pl.ds(n * band - 8, 8), :], south_in, edge_sent.at[0], edge_arrived.at[0], i, after)

    def to_south():
        return remote(cells.at[:, pl.ds(0, 8), :], north_in, edge_sent.at[1], edge_arrived.at[1], i, before)

    sub = lax.broadcasted_iota(jnp.int32, (8, block), 0)

    def make_pack(t, under, over):
        low = [pltpu.roll(under[p].astype(jnp.float32), 2 + 2 * p, 0) for p in range(2)]
        high = [pltpu.roll(over[p].astype(jnp.float32), 4 + p, 0) for p in range(2)]
        rows = jnp.where(sub < 2, low[0], jnp.where(sub < 4, low[1], jnp.where(sub == 4, high[0], high[1])))
        pack[t] = rows.astype(jnp.bfloat16)

    pl.semaphore_wait(barrier, i + jnp.where(has_south, 1, 0) + jnp.where(i == 0, 1, 0))

    for t in range(n - 2, -1, -1):
        @pl.when((i > t) & ((t > 0) | (i > 1)))
        def _():
            signal(known.at[i - 1], t, j)

    @pl.when(has_left)
    def _():
        send_rows(0, pieces=groups[:2])

    @pl.when(i == 0)
    def _():
        send_rows(1)

    @pl.when(has_south)
    def _():
        signal(known.at[0], i, before)
        to_south().start()

    pltpu.make_async_copy(rims, rims, own.at[0]).wait()
    for t in range(1, n - 1):
        make_pack(t, rims.at[0, t - 1], rims.at[1, t])

    @pl.when(has_right & (i > 0))
    def _():
        pl.semaphore_wait(known.at[i], 1)

    @pl.when(i + 1 < n - 1)
    def _():
        send_halo(i + 1)

    @pl.when(has_right & (i > 0))
    def _():
        send_rows(i + 1)

    splits = i > half

    @pl.when(splits)
    def _():
        send_rows(i - 1, (0,))

    @pl.when(has_north)
    def _():
        pl.semaphore_wait(known.at[0], 1)
        to_north().start()

    for t in range(2, n):
        @pl.when(i + 1 < t)
        def _():
            pl.semaphore_wait(known.at[t - 1], 1)
            if t < n - 1:
                send_halo(t)
                send_rows(t)
            else:
                send_rows(t, pieces=groups[:1])

    @pl.when(has_south)
    def _():
        to_north().wait_recv()

    @pl.when(has_north)
    def _():
        to_south().wait_recv()

    make_pack(0, south_in, rims.at[1, 0])
    make_pack(n - 1, rims.at[0, n - 2], north_in)

    @pl.when(has_left)
    def _():
        send_halo(0)
        send_rows(0, pieces=groups[2:])

    @pl.when(has_right)
    def _():
        send_halo(n - 1)

    @pl.when(i + 1 < n - 1)
    def _():
        send_rows(n - 1, pieces=groups[1:])

    for t in range(1, n - 1):
        @pl.when((i > t) & jnp.logical_not(splits & (i == t + 1)))
        def _():
            send_halo(t)
            send_rows(t)

    @pl.when(splits)
    def _():
        send_halo(i - 1)
        send_rows(i - 1, (1,))

    blocks[i, pl.ds(2 * band, 8), :] = pack[i]

    tile_terms, first = arrival_stage(n, m, band, blocks, fields)
    tile_stencil, carry_into = stencil_stage(n, m, band // 2, fields)
    ranges = [spans(n, at, per_block) for at in range(n)]

    def second(step):
        found = [of_device[step] for of_device in ranges]
        count = max(end - low for low, end in found)
        low = chosen(i, [min(low, n * per_block - count) for low, _ in found])
        carry = carry_into(low)
        for q in range(count):
            values, carry = tile_stencil(low + q, carry)
            hold(low + q, values)

    def hold(t, values):
        cols = pl.ds(pl.multiple_of(t * LANES, LANES), LANES)
        for at, value in enumerate(values):
            held[at, :, cols] = value

    def landed(ref, sem, k):
        remote(ref, ref, sent.at[0], sem, k, j).wait_recv()

    mine = blocks.at[i, pl.ds(0, 2 * band), :]
    pltpu.make_async_copy(mine, mine, own.at[1]).wait()
    first(i, 0, per_block)
    second(0)
    orders = [arrivals(n, at) for at in range(n)]
    for step in range(n - 2):
        k = chosen(i, [order[step] for order in orders])
        landed(blocks.at[k, pl.ds(0, 2 * band), :], arrived.at[k], k)
        landed(blocks.at[k, pl.ds(2 * band, 6), :], around.at[k], k)
        first(k, 0, per_block)
        second(step + 1)
    k = chosen(i, [order[n - 2] for order in orders])
    low = k * per_block - 1
    carry = carry_into(low)
    landed(blocks.at[k, pl.ds(2 * band, 6), :], around.at[k], k)
    done = 0
    for p, group in groups:
        landed(blocks.at[k, pl.ds(0, 2 * band), cols_of(group)], piece.at[p], k)
        between = []
        for q in range(done, group[0]):
            values, carry = tile_stencil(low + q, carry)
            between.append((low + q, values))
        done = group[0]
        stores = [tile_terms(k, p) for p in group]
        for t, values in between:
            hold(t, values)
        if group[-1] == per_block - 1:
            for at, value in enumerate(carry):
                carried[at] = value
        for store in stores:
            store()

    def drained(ref, sem):
        remote(ref, ref, sem, arrived.at[0], i, j).wait_send()

    drained(blocks.at[pl.ds(0, n - 1), pl.ds(0, 2 * band), :], sent.at[0])

    drained(blocks.at[pl.ds(0, n - 1), pl.ds(2 * band, 6), :], sent.at[1])

    @pl.when(has_north)
    def _():
        to_north().wait_send()

    @pl.when(has_south)
    def _():
        to_south().wait_send()


def parts(x0, y0, x1, y1):
    s0, s1 = x0 + y0, x1 + y1
    return x0 * y0 * s1 + x1 * y1 * s0, s0 * s1


def two_faces(one, two):
    scale = 2.0 / (one[1] * two[1])
    return one[0] * two[1] * scale, two[0] * one[1] * scale


def middle(one, two):
    x, y = one[0] * two[1], two[0] * one[1]
    total = 1.0 / (x + y)
    return x * total, y * total, 2.0 * (one[0] * two[0]) * total


def verticals(pairs):
    sums = [x + y for x, y in pairs]
    low, high = sums[0] * sums[1], sums[2] * sums[3]
    scale = 4.0 / (low * high)
    low, high = high * scale, low * scale
    shares = (sums[1] * low, sums[0] * low, sums[3] * high, sums[2] * high)
    return [x * y * share for (x, y), share in zip(pairs, shares)]


def arrival_stage(n, m, band, blocks, fields):
    block = blocks.shape[2]
    half = band // 2
    rows = fields.shape[2]
    tiles = fields.shape[0] - 1
    per_block = block // (2 * LANES)
    i = lax.axis_index("gx")
    j = lax.axis_index("gy")
    last_rows = (i == n - 1) & (j == m - 1)

    taken = 2 * band + 6
    want = lax.broadcasted_iota(jnp.int32, (4 * rows, taken), 0)
    have = lax.broadcasted_iota(jnp.int32, (4 * rows, taken), 1)
    group = jnp.where(want >= 3 * rows, 3, jnp.where(want >= 2 * rows, 2, jnp.where(want >= rows, 1, 0)))
    place = want - group * rows
    plane = jnp.where(group >= 2, 1, 0)
    odd = group - 2 * plane
    inside = plane * band + 2 * jnp.where(place < half, place, 0) + odd
    above = jnp.where(odd == 0, 2 * band + 4 + plane, plane * band + 1)
    below = 2 * band + 2 * plane + odd
    source = jnp.where(place == half, above, jnp.where(place == rows - 1, below, inside))
    pick_rows = jnp.where(have == source, 1.0, 0.0).astype(jnp.bfloat16)
    fine = lax.broadcasted_iota(jnp.int32, (2 * LANES, 2 * LANES), 0)
    to = lax.broadcasted_iota(jnp.int32, (2 * LANES, 2 * LANES), 1)
    pick_cols = jnp.where(fine == jnp.where(to < LANES, 2 * to, 2 * (to - LANES) + 1), 1.0, 0.0).astype(jnp.bfloat16)

    top = (lax.broadcasted_iota(jnp.int32, (rows, LANES), 0) == half - 1) & last_rows

    def up(x):
        return pltpu.roll(x, rows - 1, 0)

    def tile_terms(k, part):
        t = k * per_block + part
        cols = pl.ds(part * 2 * LANES, 2 * LANES)
        stored = blocks[k, pl.ds(0, taken), cols]
        picked = jnp.dot(pick_rows, stored, preferred_element_type=jnp.float32).astype(jnp.bfloat16)
        split = jnp.dot(picked, pick_cols, preferred_element_type=jnp.float32)
        a0, c0, a1, c1 = (split[g * rows : (g + 1) * rows, :LANES] for g in range(4))
        b0, d0, b1, d1 = (split[g * rows : (g + 1) * rows, LANES:] for g in range(4))
        def wall(x0, x1, inner):
            return jnp.where(top, 0.5 * (x0 + x1), inner[0]), jnp.where(top, 1.0, inner[1])

        s0, n0, t0 = middle(parts(a0, c0, a1, c1), wall(c0, c1, parts(c0, up(a0), c1, up(a1))))
        s1, n1, t1 = middle(parts(b0, d0, b1, d1), wall(d0, d1, parts(d0, up(b0), d1, up(b1))))
        h1, g1 = two_faces(parts(a0, b0, a1, b1), parts(c0, d0, c1, d1))
        pairs = ((a0, a1), (b0, b1), (c0, c1), (d0, d1))
        side_a, side_b, side_c, side_d = (
            (x + ((k0 + k1) + v)) - v for x, (k0, k1), v in zip((h1, h1, g1, g1), pairs, verticals(pairs))
        )
        values = (a0, a1, c0, c1, s0, n0, b0, b1, d0, d1, t0, s1, n1, t1, h1, g1, side_a, side_b, side_c, side_d)

        def store():
            for at, value in enumerate(values):
                fields[t, at] = value

        return store

    def first(k, start, count):
        for part in range(start, start + count):
            tile_terms(k, part)()

    ones = jnp.ones((rows, LANES), jnp.float32)
    for at in range(6):
        fields[tiles, at] = ones

    return tile_terms, first


def stencil_stage(n, m, half, fields):
    rows = fields.shape[2]
    tiles = fields.shape[0] - 1
    i = lax.axis_index("gx")
    j = lax.axis_index("gy")
    lane = lax.broadcasted_iota(jnp.int32, (rows, LANES), 1)
    sub = lax.broadcasted_iota(jnp.int32, (rows, LANES), 0)
    bottom = (sub == 0) & (i == 0) & (j == 0)
    top = (sub == half - 1) & (i == n - 1) & (j == m - 1)

    def up(x):
        return pltpu.roll(x, rows - 1, 0)

    def down(x):
        return pltpu.roll(x, 1, 0)

    def step(t, carry):
        last = (lane == LANES - 1) & (t == tiles - 1)
        first_lane = (lane == 0) & (t == 0)

        def ahead(at):
            return pltpu.roll(jnp.where(lane == 0, fields[t + 1, at], fields[t, at]), LANES - 1, 1)

        rolled = []

        def behind(x):
            turned = pltpu.roll(x, 1, 1)
            before = carry[len(rolled)]
            rolled.append(turned)
            return jnp.where(lane == 0, before, turned)

        a0, a1, c0, c1, s0, n0, b0, b1, d0, d1 = (fields[t, at] for at in range(10))
        t0, s1, n1, t1, h1, g1, side_a, side_b, side_c, side_d = (fields[t, at] for at in range(10, 20))
        wall_a, wall_b = a0 + a1, b0 + b1
        h2, g2 = two_faces(parts(b0, ahead(0), b1, ahead(1)), parts(d0, ahead(2), d1, ahead(3)))
        h2 = jnp.where(last, wall_b, h2)
        g2 = jnp.where(last, d0 + d1, g2)
        total = 1.0 / (h1 + h2)
        left, right = h1 * total, h2 * total
        left_up = up(left)
        right_up = up(right)
        s0_next = ahead(4)
        n0_next = ahead(5)
        side_a = side_a + jnp.where(first_lane, wall_a, behind(h2))
        side_c = side_c + jnp.where(first_lane, c0 + c1, behind(g2))
        side_b = side_b + h2
        side_d = side_d + g2

        nc = n0 * side_c
        sc = s0 * side_c
        nd = n1 * side_d
        sd = s1 * side_d
        even = side_a + t0 + s0 * sc + jnp.where(bottom, wall_a, down(t0 + n0 * nc))
        odd_ = side_b + t1 + s1 * sd + jnp.where(bottom, wall_b, down(t1 + n1 * nd))
        even_up = s0 * nc - t0
        odd_up = s1 * nd - t1
        sg = s0 * g1
        ng = n0 * g1
        sq = s0_next * g2
        nq = n0_next * g2
        p = h1 + s1 * sg + jnp.where(bottom, 0.0, down(n1 * ng))
        q = h2 + s1 * sq + jnp.where(bottom, 0.0, down(n1 * nq))
        p_up = n1 * sg
        p_down = s1 * ng
        q_up = s1 * nq
        q_down = n1 * sq

        mid = left * odd_ - p
        east = jnp.where(last, 0.0, right * mid - left * q)
        centre = even + left * (mid - p) + behind(right * (right * odd_ - 2.0 * q))
        lo = left * odd_up - p_up
        ro = right * odd_up - q_down
        north = even_up + left_up * lo - left * p_down + behind(right_up * ro - right * q_up)
        north = jnp.where(top, 0.0, north)
        north_east = jnp.where(last | top, 0.0, right_up * lo - left * q_up)
        north_west = jnp.where(last | top, 0.0, left_up * ro - right * p_down)
        west = behind(east)
        ne_back = behind(north_east)
        nw_back = behind(north_west)

        def below(x):
            return jnp.where(bottom, 0.0, down(x))

        values = (below(ne_back), below(north), below(north_west), west, centre, east, nw_back, north, north_east)
        return tuple(value[:half] for value in values), tuple(rolled)

    def carry_into(t):
        carry = step(jnp.maximum(t - 1, 0), (jnp.zeros((rows, LANES), jnp.float32),) * 7)[1]
        return tuple(jnp.where(t > 0, x, 0.0) for x in carry)

    return step, carry_into


def stencil_kernel(n, m, half, per_block, fields, held, carried, out, late, stored):
    tiles = fields.shape[0] - 1
    i = lax.axis_index("gx")
    low = (chosen(i, [last_block(n, at) for at in range(n)]) + 1) * per_block - 2
    count = LAST
    tile_stencil, _ = stencil_stage(n, m, half, fields)

    def columns(t, width):
        return pl.ds(pl.multiple_of(t * LANES, LANES), width * LANES)

    for q in range(0, tiles - count, 2):
        cols = columns(jnp.where(q < low, q, q + count), min(2, tiles - count - q))
        pltpu.make_async_copy(held.at[:, :, cols], out.at[:, :, cols], stored.at[0]).start()

    carry = tuple(carried[at] for at in range(7))
    for q in range(count):
        values, carry = tile_stencil(low + q, carry)
        for at, value in enumerate(values):
            late[at, :, q * LANES : (q + 1) * LANES] = value
    pltpu.make_async_copy(late, out.at[:, :, columns(low, count)], stored.at[0]).start()
    pltpu.make_async_copy(held, out, stored.at[0]).wait()


def shards(n, m, conductivity):
    planes, local_rows, local_cols = conductivity.shape
    band = local_rows // n
    half = band // 2
    rows = -(-(half + 2) // 8) * 8
    tiles = n * local_cols // (2 * LANES)
    vmem = pl.BlockSpec(memory_space=pltpu.VMEM)
    anywhere = pl.BlockSpec(memory_space=pl.ANY)
    dma = pltpu.SemaphoreType.DMA
    shape = (tiles + 1, 20, rows, LANES)
    per_block = local_cols // (2 * LANES)
    result = jax.ShapeDtypeStruct((9, half, tiles * LANES), jnp.float32)
    fields, held, carried = pl.pallas_call(
        functools.partial(coarse_kernel, n, m),
        out_shape=(
            jax.ShapeDtypeStruct(shape, jnp.float32),
            result,
            jax.ShapeDtypeStruct((7, rows, LANES), jnp.float32),
        ),
        in_specs=[anywhere],
        out_specs=(vmem, vmem, vmem),
        scratch_shapes=[
            pltpu.VMEM((n, 2 * band + 8, local_cols), jnp.bfloat16),
            pltpu.VMEM((2, n - 1, planes, 8, local_cols), jnp.bfloat16),
            pltpu.VMEM((planes, 8, local_cols), jnp.bfloat16),
            pltpu.VMEM((planes, 8, local_cols), jnp.bfloat16),
            pltpu.VMEM((n, 8, local_cols), jnp.bfloat16),
            dma((n,)),
            dma((n,)),
            dma((3,)),
            dma((2,)),
            dma((2,)),
            dma((2,)),
            pltpu.SemaphoreType.REGULAR((n - 1,)),
            dma((2,)),
        ],
        compiler_params=pltpu.CompilerParams(
            collective_id=0, has_side_effects=True, vmem_limit_bytes=VMEM_LIMIT
        ),
        name="coarse",
    )(pltpu.with_memory_space_constraint(conductivity, pltpu.HBM))
    stencil = pl.pallas_call(
        functools.partial(stencil_kernel, n, m, half, per_block),
        out_shape=result,
        in_specs=[vmem, vmem, vmem],
        out_specs=anywhere,
        scratch_shapes=[pltpu.VMEM((9, half, LAST * LANES), jnp.float32), dma((1,))],
        compiler_params=pltpu.CompilerParams(vmem_limit_bytes=VMEM_LIMIT),
        name="stencil",
    )(fields, held, carried)
    return stencil[:, None]


def solution(mesh):
    n, m = mesh.shape["gx"], mesh.shape["gy"]
    return jax.shard_map(
        functools.partial(shards, n, m),
        mesh=mesh,
        in_specs=(P(None, "gy", "gx"),),
        out_specs=P(None, "gy", "gx", None),
        check_vma=False,
    )
```
